32 devices in a mesh: dp: 8 (over z, y), chan: 4 (over x, core).
Axes of the slice: x: 2, y: 2, z: 4, core: 2. Of those that a mesh axis runs over, the one named last changes fastest.
Arguments:
- inputs: bfloat16 [16, 16, 16, 512], P('dp', None, None, 'chan'), may hold values from -6 to 6
- affine: float32 [3, 2, 512], P(None, None, 'chan'), may hold values from 0.3 to 1.3
- image_sizes: int32 [16, 2], P('dp'), may hold values from 8 to 16
- labels: int32 [16, 16, 16, 7], P('dp'), may hold values from 0 to 20
- label_mask: int32 [16, 16, 16, 7], P('dp'), may hold values 0 or 1
- unit_slots: int32 [54], replicated, may hold values from 0 to 55, as said below
- conv_master: float32 [56, 256, 512], P('dp', None, 'chan'), may hold values from -0.09375 to 0.09375
- conv_first: float32 [56, 256, 512], P('dp', None, 'chan'), may hold values from -0.00390625 to 0.00390625
- conv_second: float32 [56, 256, 512], P('dp', None, 'chan'), may hold values from 2.746582e-09 to 4.3945313e-08
- head_master: float32 [7, 256, 512], P(None, 'chan'), may hold values from -0.25 to 0.25
- head_first: float32 [7, 256, 512], P(None, 'chan'), may hold values from -0.0048828125 to 0.0048828125
- head_second: float32 [7, 256, 512], P(None, 'chan'), may hold values from 4.8828124e-09 to 7.8125e-08
- join_master: float32 [7, 256, 21], P(None, 'chan'), may hold values from -4 to 4
- join_first: float32 [7, 256, 21], P(None, 'chan'), may hold values from -0.0012207031 to 0.0012207031
- join_second: float32 [7, 256, 21], P(None, 'chan'), may hold values from 3.0517577e-10 to 4.8828124e-09
- scale_master: float32 [7, 256], P(None, 'chan'), may hold values from 1 to 4
- scale_first: float32 [7, 256], P(None, 'chan'), may hold values from -0.0024414062 to 0.0024414062
- scale_second: float32 [7, 256], P(None, 'chan'), may hold values from 1.2207031e-09 to 1.953125e-08
- step_count: int32 [1], replicated, may hold values from 2 to 20
Outputs:
- loss: float32 [1], replicated
- conv_new: float32 [56, 256, 512], P('dp', None, 'chan')
- conv_first_new: float32 [56, 256, 512], P('dp', None, 'chan')
- conv_second_new: float32 [56, 256, 512], P('dp', None, 'chan')
- head_new: float32 [7, 256, 512], P(None, 'chan')
- head_first_new: float32 [7, 256, 512], P(None, 'chan')
- head_second_new: float32 [7, 256, 512], P(None, 'chan')
- join_new: float32 [7, 256, 21], P(None, 'chan')
- join_first_new: float32 [7, 256, 21], P(None, 'chan')
- join_second_new: float32 [7, 256, 21], P(None, 'chan')
- scale_new: float32 [7, 256], P(None, 'chan')
- scale_first_new: float32 [7, 256], P(None, 'chan')
- scale_second_new: float32 [7, 256], P(None, 'chan')
The draws below stay inside these ranges and needn't reach their ends.
Inputs may be any that keep to these rules, and one draw needn't show every extreme that they name: `unit_slots`: distinct slots; slot s belongs to index s // 7 of dp, so an index holds at most 7 blocks; slot 55 is always used.
All inputs are finite; a program needn't handle non-finite values. No bound on the sum of `label_mask` on one device may be relied on, other than what follows from the above.
Results may differ from the reference program's by a relative error of at most 0.0035.
The reference program's roundings to bfloat16 on the way count: a program that leaves them out, or rounds other values in their place, can miss the bound.
Values may be sent and summed in bfloat16 or wider, within the bound.
A program may use at most 128 MiB of HBM per device.

```python
import math
import jax
import jax.numpy as jnp
from jax import lax

C = 512
CH = 256
K = 21
TASKS = 7
LAYERS = 3
H = 16
W = 16
B = 16
PIXELS = 4096
UNIT_ROWS = 256
NUNITS = 54
TOTAL_SLOTS = 56


def draw_unit_slots(key, part):
    shuffled = jax.random.permutation(key, TOTAL_SLOTS - 1)[:NUNITS - 1]
    chosen = jnp.concatenate([shuffled, jnp.full((1,), TOTAL_SLOTS - 1)]).astype(jnp.int32)
    return jax.random.permutation(jax.random.fold_in(key, 7), chosen).astype(jnp.int32)


def plant(entries, own_key, low, largest):
    extent = entries.shape
    place = [jax.random.randint(jax.random.fold_in(own_key, axis), (), 0, extent[axis]) for axis in range(len(extent))]
    entries = entries.at[tuple(place)].set(low)
    longest = extent.index(max(extent))
    place[longest] = (place[longest] + 1) % extent[longest]
    return entries.at[tuple(place)].set(largest)


def steps_of(rng, dims, shards, smallest, largest):
    gain = 1.0
    for dim, blocks in shards:
        steps = jax.random.uniform(jax.random.fold_in(jax.random.fold_in(rng, 6), dim), (blocks,), jnp.float32, smallest / len(shards), largest / len(shards))
        gain = gain * jnp.repeat(jnp.exp(steps), dims[dim] // blocks).reshape((-1,) + (1,) * (len(dims) - 1 - dim))
    return gain


def noise(rng, extent, scale, limit, cuts=(), held_as=jnp.bfloat16):
    drawn = jax.random.normal(rng, extent, jnp.float32) * scale
    if len(cuts) > 0:
        drawn = steps_of(rng, extent, cuts, -0.22, 0.18) * drawn
    return jnp.clip(drawn, min=-limit, max=limit).astype(held_as)


def setup_inputs(seed: int = 0) -> dict:
    arg_keys = jax.random.split(jax.random.key(seed), 20)
    inputs = noise(arg_keys[0], (B, H, W, C), 1.0, 6.0, ((0, 8), (3, 4)))
    affine = jnp.clip(0.3 + 0.99999994 * jax.random.uniform(arg_keys[1], (LAYERS, 2, C), jnp.float32) ** steps_of(arg_keys[1], (LAYERS, 2, C), ((2, 4),), -0.2, 0.2), 0.3, 1.3)
    image_sizes = plant(jax.random.randint(arg_keys[2], (B, 2), H // 2, H + 1), jax.random.fold_in(arg_keys[2], 1), H // 2, H).astype(jnp.int32)
    labels = plant(jax.random.randint(arg_keys[3], (B, H, W, TASKS), 0, K), jax.random.fold_in(arg_keys[3], 1), 0, K - 1).astype(jnp.int32)
    label_mask = plant((jax.random.randint(arg_keys[4], (B, H, W, TASKS), 0, 4) < 3).astype(jnp.int32), jax.random.fold_in(arg_keys[4], 1), 0, 1)
    unit_slots = draw_unit_slots(jax.random.fold_in(arg_keys[19], 71), 0)
    conv_master = noise(arg_keys[6], (TOTAL_SLOTS, UNIT_ROWS, C), (9 * C) ** -0.5, 0.09375, ((0, 8), (2, 4)), jnp.float32)
    conv_first = noise(arg_keys[7], (TOTAL_SLOTS, UNIT_ROWS, C), (0.0165 / PIXELS ** 0.5), 0.00390625, ((0, 8), (2, 4)), jnp.float32)
    conv_second = jnp.clip(jnp.exp(math.log(4.394531316620487e-08) - 2.7725887 * jax.random.uniform(arg_keys[8], (TOTAL_SLOTS, UNIT_ROWS, C), jnp.float32) ** steps_of(arg_keys[8], (TOTAL_SLOTS, UNIT_ROWS, C), ((0, 8), (2, 4)), -0.2, 0.2)), 2.7465820728878043e-09, 4.394531316620487e-08)
    head_master = noise(arg_keys[9], (TASKS, CH, C), C ** -0.5, 0.25, ((1, 4),), jnp.float32)
    head_first = noise(arg_keys[10], (TASKS, CH, C), (0.022 / PIXELS ** 0.5), 0.0048828125, ((1, 4),), jnp.float32)
    head_second = jnp.clip(jnp.exp(math.log(7.81249980263965e-08) - 2.7725887 * jax.random.uniform(arg_keys[11], (TASKS, CH, C), jnp.float32) ** steps_of(arg_keys[11], (TASKS, CH, C), ((1, 4),), -0.2, 0.2)), 4.882812376649781e-09, 7.81249980263965e-08)
    join_master = noise(arg_keys[12], (TASKS, CH, K), 1.0, 4.0, ((1, 4),), jnp.float32)
    join_first = noise(arg_keys[13], (TASKS, CH, K), (0.0055 / PIXELS ** 0.5), 0.0012207031, ((1, 4),), jnp.float32)
    join_second = jnp.clip(jnp.exp(math.log(4.882812376649781e-09) - 2.7725887 * jax.random.uniform(arg_keys[14], (TASKS, CH, K), jnp.float32) ** steps_of(arg_keys[14], (TASKS, CH, K), ((1, 4),), -0.2, 0.2)), 3.051757735406113e-10, 4.882812376649781e-09)
    scale_master = jnp.clip(jnp.exp(math.log(4.0) - 1.3862944 * jax.random.uniform(arg_keys[15], (TASKS, CH), jnp.float32) ** steps_of(arg_keys[15], (TASKS, CH), ((1, 4),), -0.2, 0.2)), 1.0, 4.0)
    scale_first = noise(arg_keys[16], (TASKS, CH), (0.011 / PIXELS ** 0.5), 0.0024414062, ((1, 4),), jnp.float32)
    scale_second = jnp.clip(jnp.exp(math.log(1.9531249506599124e-08) - 2.7725887 * jax.random.uniform(arg_keys[17], (TASKS, CH), jnp.float32) ** steps_of(arg_keys[17], (TASKS, CH), ((1, 4),), -0.2, 0.2)), 1.2207030941624453e-09, 1.9531249506599124e-08)
    step_count = jax.random.randint(arg_keys[18], (1,), 2, 21).astype(jnp.int32)
    return {"inputs": inputs, "affine": affine, "image_sizes": image_sizes, "labels": labels, "label_mask": label_mask, "unit_slots": unit_slots, "conv_master": conv_master, "conv_first": conv_first, "conv_second": conv_second, "head_master": head_master, "head_first": head_first, "head_second": head_second, "join_master": join_master, "join_first": join_first, "join_second": join_second, "scale_master": scale_master, "scale_first": scale_first, "scale_second": scale_second, "step_count": step_count}


@jax.custom_vjp
def low(v):
    return lax.optimization_barrier(v.astype(jnp.bfloat16)).astype(jnp.float32)

@jax.custom_vjp
def low_back(v):
    return v

def low_keep(v):
    return (low(v), None)

def low_pass(kept, grad):
    return (grad,)

def back_keep(v):
    return (v, None)

def back_low(kept, grad):
    return (low(grad),)
low.defvjp(low_keep, low_pass)
low_back.defvjp(back_keep, back_low)
beta_one = 0.9
beta_two = 0.999
eps_adam = 1e-08
decay_rate = 0.01
eps_norm = 1e-06

def valid_pixels(image_sizes):
    row_ids = jnp.arange(H)[None, :, None] < image_sizes[:, 0][:, None, None]
    col_ids = jnp.arange(W)[None, None, :] < image_sizes[:, 1][:, None, None]
    return (row_ids & col_ids).astype(jnp.float32)[..., None]

def adamw(weight, gradient, moment_one, moment_two, step_rate, step_count):
    step_float = step_count[0].astype(jnp.float32)
    moment_one = beta_one * moment_one + (1.0 - beta_one) * gradient
    moment_two = beta_two * moment_two + (1.0 - beta_two) * gradient * gradient
    first_hat = moment_one / (1.0 - beta_one ** step_float)
    second_hat = moment_two / (1.0 - beta_two ** step_float)
    weight = weight - step_rate * (first_hat / (jnp.sqrt(second_hat) + eps_adam) + decay_rate * weight)
    return (weight, moment_one, moment_two)

def forward(conv_w, head_w, join_w, scale_w, inputs, affine, inside, labels, label_keep, counts, unit_slots):
    blocks = low(conv_w)[unit_slots]
    kernels = blocks.reshape(LAYERS, 3, 3, C, C)
    current = inputs * inside
    for layer_index in range(LAYERS):
        linear = low_back(lax.conv_general_dilated(current, kernels[layer_index], (1, 1), 'SAME', dimension_numbers=('NHWC', 'HWIO', 'NHWC'), precision=lax.Precision.HIGHEST))
        output = (jax.nn.relu(linear) * affine[layer_index, 0] + affine[layer_index, 1]) * inside
        current = low(output)
    head_low = low(head_w)
    join_low = low(join_w)

    def image_loss(pieces):
        features, label_rows, keep_rows = pieces
        hidden = low_back(jnp.einsum('pc,tdc->ptd', features, head_low, precision=lax.Precision.HIGHEST))
        normed = hidden * lax.rsqrt(lax.optimization_barrier(jnp.sum(hidden * hidden, axis=2, keepdims=True)) + eps_norm)
        scaled = low(scale_w[None] * normed)
        logits = low_back(jnp.einsum('ptd,tdk->ptk', scaled, join_low, precision=lax.Precision.HIGHEST))
        log_norm = jax.nn.logsumexp(logits, axis=2)
        onehot = (label_rows[:, :, None] == jnp.arange(K)[None, None, :]).astype(jnp.float32)
        picked = lax.optimization_barrier(jnp.sum(onehot * logits, axis=2))
        return jnp.sum(keep_rows / counts[None, :] * (log_norm - picked))
    per_image = lax.map(jax.checkpoint(image_loss), (current.reshape(B, H * W, C), labels.reshape(B, H * W, TASKS), label_keep.reshape(B, H * W, TASKS)))
    return jnp.sum(per_image)

def reference(inputs, affine, image_sizes, labels, label_mask, unit_slots, conv_master, conv_first, conv_second, head_master, head_first, head_second, join_master, join_first, join_second, scale_master, scale_first, scale_second, step_count):
    inside = valid_pixels(image_sizes)
    label_keep = label_mask.astype(jnp.float32) * inside
    counts = jnp.maximum(lax.optimization_barrier(jnp.sum(label_keep, axis=(0, 1, 2))), 1.0)
    source = inputs.astype(jnp.float32)

    def loss_of(conv_w, head_w, join_w, scale_w):
        return forward(conv_w, head_w, join_w, scale_w, source, affine, inside, labels, label_keep, counts, unit_slots)
    loss_value, pullback = jax.vjp(loss_of, conv_master, head_master, join_master, scale_master)
    conv_grad, head_grad, join_grad, scale_grad = pullback(jnp.ones((), jnp.float32))
    conv_out = adamw(conv_master, conv_grad, conv_first, conv_second, 0.01, step_count)
    head_out = adamw(head_master, head_grad, head_first, head_second, 0.03, step_count)
    join_out = adamw(join_master, join_grad, join_first, join_second, 0.4, step_count)
    scale_out = adamw(scale_master, scale_grad, scale_first, scale_second, 0.8, step_count)
    return (loss_value.reshape(1), conv_out[0], conv_out[1], conv_out[2], head_out[0], head_out[1], head_out[2], join_out[0], join_out[1], join_out[2], scale_out[0], scale_out[1], scale_out[2])
```

```python
import functools

import jax
import jax.numpy as jnp
from jax import lax
from jax.experimental import pallas as pl
from jax.experimental.pallas import tpu as pltpu
from jax.sharding import PartitionSpec as P

C = 512
K = 21
TASKS = 7
LAYERS = 3
H = 16
W = 16
PX = 512
IMG = 256
HC = 64
CHUNK = 272
SMALL = 16

beta_one = 0.9
beta_two = 0.999
eps_adam = 1e-08
decay_rate = 0.01
eps_norm = 1e-06

F32 = jnp.float32
BF16 = jnp.bfloat16
MESH = pl.DeviceIdType.MESH
NN = (((1,), (0,)), ((), ()))
NT = (((1,), (1,)), ((), ()))
TN = (((0,), (0,)), ((), ()))


def dot(a, b, dims, precision=None):
    return lax.dot_general(a, b, dims, precision=precision, preferred_element_type=F32)


def encode(values):
    top = jnp.max(jnp.abs(values), axis=0, keepdims=True)
    power = jnp.ceil(jnp.log2(jnp.maximum(top, 1e-30))) - 14.0
    codes = jnp.round(values * jnp.exp2(-power)).astype(jnp.int32).astype(jnp.int16)
    powers = jnp.broadcast_to(power, (16, 128)).astype(jnp.int32).astype(jnp.int16)
    return codes, powers


def decode(codes, powers):
    return codes.astype(F32) * jnp.exp2(powers.astype(F32)[0:1])


def kernel(
    n,
    slots_per,
    slots_ref,
    sizes_ref,
    inputs_ref,
    affine_ref,
    code_ref,
    conv_ref,
    head_ref,
    join_ref,
    grad_out,
    head_out,
    small_out,
    loss_out,
    wall,
    xs,
    xt,
    hall,
    jall,
    aall,
    cnt,
    losses,
    inv_ref,
    mask,
    coef,
    zacc,
    fbuf,
    gh,
    ghall,
    gfeat,
    gsend,
    grecv,
    jt,
    jsend,
    jrecv,
    gs,
    bpart,
    bcore,
    bx,
    bxs,
    dw,
    hg,
    small,
    ysend,
    yrecv,
    lsend,
    lright,
    lleft,
    bsend2,
    brecv2,
    hag,
    zsum,
    w_recv,
    w_zr,
    w_zl,
    w_y,
    x_send,
    x_recv,
    h_send,
    h_recv,
    j_send,
    j_recv,
    a_send,
    a_recv,
    c_send,
    c_recv,
    l_send,
    l_recv,
    f_send,
    f_recv,
    g_send,
    g_recv,
    q_send,
    q_recv,
    s_send,
    s_recv,
    bc_send,
    bc_recv,
    bx_send,
    bx_recv,
    y_send,
    y_recv,
    z_send,
    zr_recv,
    zl_recv,
    b_send,
    b_recv,
    t_recv,
    t_zr,
    t_zl,
    t_y,
):
    nz = n // 2
    last_b = slots_per // 7
    first_a = slots_per - last_b
    cargo = slots_per + last_b + 1
    piece = hg.shape[0] // n

    me = lax.axis_index("dp")
    ch = lax.axis_index("chan")
    z, y = me // 2, me % 2
    core = ch % 2
    partner = ch + 1 - 2 * core
    across = (ch + 2) % 4
    far = (partner + 2) % 4

    def at(dp=None, chan=None):
        return {"dp": me if dp is None else dp, "chan": ch if chan is None else chan}

    right, left, other = at(dp=me + 2), at(dp=me - 2), at(dp=z * 2 + 1 - y)
    has_right, has_left = z < nz - 1, z > 0

    def put(src, dst, send, recv, dev):
        return pltpu.make_async_remote_copy(
            src_ref=src, dst_ref=dst, send_sem=send, recv_sem=recv, device_id=dev, device_id_type=MESH
        )

    def came(ref, recv):
        put(ref, ref, recv, recv, other).wait_recv()

    def left_it(ref, send):
        put(ref, ref, send, send, other).wait_send()

    def loop(count, body):
        lax.fori_loop(0, count, lambda i, c: (body(i), c)[1], 0)

    barrier = pltpu.get_barrier_semaphore()

    def greet(i):
        pl.semaphore_signal(barrier, inc=1, device_id=at(dp=(me + i + 1) % n), device_id_type=MESH)

    loop(n - 1, greet)
    for peer in (partner, across, far):
        pl.semaphore_signal(barrier, inc=1, device_id=at(chan=peer), device_id_type=MESH)

    def cast_block(k):
        wall[me * slots_per + k] = conv_ref[k].astype(BF16)

    loop(slots_per, cast_block)
    pixel = lax.broadcasted_iota(jnp.int32, (IMG, 128), 0)
    row_id, col_id = pixel // W, pixel % W

    def mask_image(i):
        inside = (row_id < sizes_ref[i, 0]) & (col_id < sizes_ref[i, 1])
        rows = pl.ds(pl.multiple_of(i * IMG, IMG), IMG)
        mask[rows, :] = jnp.where(inside, 1.0, 0.0)
        xs[0, ch, rows, :] = (inputs_ref[rows, :].astype(F32) * mask[rows, :]).astype(BF16)

    loop(2, mask_image)

    def cast_head(t):
        hall[t, ch] = head_ref[t].astype(BF16)
        jall[t, ch] = join_ref[t]

    loop(TASKS, cast_head)
    aall[ch] = affine_ref[...]

    lane = lax.broadcasted_iota(jnp.int32, (8, 128), 1)

    def kept(q):
        spot = (q % 2) * 128 + lane
        hit = (spot // W < sizes_ref[q // 2, 0]) & (spot % W < sizes_ref[q // 2, 1])
        return jnp.where(hit & (code_ref[q] >= 0), 1.0, 0.0)

    total_kept = kept(0) + kept(1) + kept(2) + kept(3)
    cnt[me] = jnp.broadcast_to(jnp.sum(total_kept, axis=1, keepdims=True), (8, 128))

    pl.semaphore_wait(barrier, n - 1 + 3)

    def to_right(s):
        return put(wall.at[s], wall.at[s], w_zr.at[s], w_recv.at[s], right)

    def to_left(s):
        return put(wall.at[s], wall.at[s], w_zl.at[s], w_recv.at[s], left)

    def to_other(s):
        return put(wall.at[s], wall.at[s], w_y.at[s], w_recv.at[s], other)

    def both_ways(s):
        @pl.when(has_right)
        def _():
            to_right(s).start()

        @pl.when(has_left)
        def _():
            to_left(s).start()

    def x_copy(l, i, owner, peer, k):
        rows = pl.ds(pl.multiple_of(i * IMG, IMG), IMG)
        ref = xs.at[l, owner, rows, :]
        return put(ref, ref, x_send.at[l, i, k], x_recv.at[l, i, k], at(chan=peer))

    def x_start(l, i):
        x_copy(l, i, ch, across, 0).start()
        x_copy(l, i, ch, partner, 1).start()

    def x_relay(l, i):
        x_copy(l, i, across, across, 0).wait_recv()
        x_copy(l, i, across, partner, 2).start()

    def x_arrive(l, i):
        x_copy(l, i, partner, partner, 1).wait_recv()
        x_copy(l, i, far, partner, 2).wait_recv()

    def x_drain(l, i):
        for k in range(3):
            x_copy(l, i, ch, partner, k).wait_send()

    def h_copy(t, owner, peer, k):
        ref = hall.at[t, owner]
        return put(ref, ref, h_send.at[t, k], h_recv.at[t, k], at(chan=peer))

    def j_copy(owner, peer, k):
        ref = jall.at[:, owner]
        return put(ref, ref, j_send.at[k], j_recv.at[k], at(chan=peer))

    def a_copy(owner, peer, k):
        ref = aall.at[owner]
        return put(ref, ref, a_send.at[k], a_recv.at[k], at(chan=peer))

    def c_copy(i):
        dev = (me + i + 1) % n
        return put(cnt.at[me], cnt.at[me], c_send.at[i], c_recv.at[me], at(dp=dev))

    base = me * slots_per

    def own_b(k):
        to_other(base + first_a + k).start()

    loop(last_b, own_b)

    def own_a(k):
        both_ways(base + k)
        to_other(base + k).start()

    loop(first_a, own_a)
    for i in range(2):
        x_start(0, i)

    def own_head(t):
        h_copy(t, ch, across, 0).start()
        h_copy(t, ch, partner, 1).start()

    loop(TASKS, own_head)
    loop(last_b, lambda k: both_ways(base + first_a + k))
    for copy in (j_copy, a_copy):
        copy(ch, across, 0).start()
        copy(ch, partner, 1).start()
    loop(n - 1, lambda i: c_copy(i).start())

    neighbour = (z * 2 + 1 - y) * slots_per

    def pass_b(k):
        s = neighbour + first_a + k
        came(wall.at[s], w_recv.at[s])
        both_ways(s)

    loop(last_b, pass_b)
    for i in range(2):
        x_relay(0, i)

    def relay_head(t):
        h_copy(t, across, across, 0).wait_recv()
        h_copy(t, across, partner, 2).start()

    def line_in(d, c):
        def source(zz):
            row = jnp.where(c < slots_per, y, 1 - y)
            return (zz * 2 + row) * slots_per + jnp.where(c < slots_per, c, c - last_b)

        @pl.when(z - d >= 0)
        def _():
            s = source(z - d)
            came(wall.at[s], w_recv.at[s])

            @pl.when(has_right)
            def _():
                to_right(s).start()

            @pl.when(c < first_a)
            def _():
                to_other(s).start()

        @pl.when(z + d < nz)
        def _():
            s = source(z + d)
            came(wall.at[s], w_recv.at[s])

            @pl.when(has_left)
            def _():
                to_left(s).start()

            @pl.when(c < first_a)
            def _():
                to_other(s).start()

    def first_step(c):
        pl.when(c < slots_per + last_b)(lambda: line_in(1, c))
        pl.when(c < TASKS)(lambda: relay_head(c))

    loop(max(slots_per + last_b, TASKS), first_step)
    for copy in (j_copy, a_copy):
        copy(across, across, 0).wait_recv()
        copy(across, partner, 2).start()

    def invert(s):
        def look(u, found):
            return jnp.where(slots_ref[u] == s, u, found)

        inv_ref[s] = lax.fori_loop(0, slots_ref.shape[0], look, -1)

    loop(n * slots_per, invert)

    def transpose_layer(l):
        for c in range(4):
            xt[l, c // 2, (c % 2) * 128 : (c % 2) * 128 + 128, :] = xs[l, c].T

    for i in range(2):
        x_arrive(0, i)
    transpose_layer(0)

    loop(nz - 2, lambda d: loop(slots_per + last_b, lambda c: line_in(d + 2, c)))

    def last_in(zz):
        def block(k):
            s = (zz * 2 + 1 - y) * slots_per + k
            came(wall.at[s], w_recv.at[s])

        loop(first_a, block)

    loop(nz, last_in)

    def conv_forward(l, i):
        rows = pl.ds(pl.multiple_of(i * IMG, IMG), IMG)
        left_side = jnp.concatenate([xs[l, c, rows, :] for c in range(4)], axis=1)
        zacc[...] = jnp.zeros_like(zacc)
        for first in range(0, 9, 2):
            taps = [t for t in (first, first + 1) if t < 9]
            sides = [
                jnp.concatenate([wall[slots_ref[(l * 9 + t) * 2 + h]] for h in range(2)], axis=0)
                for t in taps
            ]
            side = jnp.concatenate(sides, axis=1) if len(sides) > 1 else sides[0]
            out = dot(left_side, side, NN)
            for k, t in enumerate(taps):
                a, e = divmod(t, 3)
                part = out[:, k * 128 : (k + 1) * 128]
                if a == 0:
                    zacc[e, W:IMG, :] += part[: IMG - W]
                elif a == 1:
                    zacc[e] += part
                else:
                    zacc[e, : IMG - W, :] += part[W:]
        linear = zacc[1]
        linear += jnp.where(col_id >= 1, pltpu.roll(zacc[0], 1, 0), 0.0)
        linear += jnp.where(col_id < W - 1, pltpu.roll(zacc[2], IMG - 1, 0), 0.0)
        inside = mask[rows, :]
        gain, shift = affine_ref[2 * l : 2 * l + 1, :], affine_ref[2 * l + 1 : 2 * l + 2, :]
        passed = jnp.where(linear > 0, inside, 0.0)
        coef[l, rows, :] = passed * gain if l < LAYERS - 1 else passed
        out = (jnp.maximum(linear, 0.0) * gain + shift) * inside
        xs[l + 1, ch, rows, :] = out.astype(BF16)

    def quarter(q):
        return pl.ds(pl.multiple_of(q * 128, 128), 128)

    for l in range(LAYERS):

        def forward_image(i, l=l):
            if l > 0:
                x_relay(l, i)
                x_arrive(l, i)
            conv_forward(l, i)
            if l < LAYERS - 1:
                x_start(l + 1, i)

        loop(2, forward_image)
        if 0 < l:
            transpose_layer(l)

    def f_copy(peer, k):
        return put(xs.at[LAYERS, ch, quarter(peer), :], fbuf.at[ch], f_send.at[k], f_recv.at[ch], at(chan=peer))

    peers = (across, far, partner)
    for k, peer in enumerate(peers):
        f_copy(peer, k).start()
    for i in range(2):
        x_start(LAYERS, i)
    fbuf[ch] = xs[LAYERS, ch, quarter(ch), :]

    loop(n - 1, lambda i: came(cnt.at[(me + i + 1) % n], c_recv.at[(me + i + 1) % n]))
    counts = lax.fori_loop(0, n, lambda i, acc: acc + cnt[i], jnp.zeros((8, 128), F32))
    counts = jnp.maximum(counts, 1.0)

    def head_in(t):
        h_copy(t, partner, partner, 1).wait_recv()
        h_copy(t, far, partner, 2).wait_recv()

    loop(TASKS, head_in)
    for copy in (j_copy, a_copy):
        copy(partner, partner, 1).wait_recv()
        copy(far, partner, 2).wait_recv()
    for peer in peers:
        came(fbuf.at[peer], f_recv.at[peer])

    weight = kept(ch) / counts
    losses[0] = weight
    losses[1] = jnp.zeros((8, 128), F32)
    features = jnp.concatenate([fbuf[c] for c in range(4)], axis=1)
    gfeat[...] = jnp.zeros_like(gfeat)
    klass = lax.broadcasted_iota(jnp.int32, (32, 128), 0)

    def head_task(t):
        low = hall[t].reshape(4 * HC, C)
        both = jall[t].reshape(4 * HC, 128)
        join = both.astype(BF16)
        scale = both[:, 32:33]
        hidden = dot(low, features, NT)
        inverse = lax.rsqrt(jnp.sum(hidden * hidden, axis=0, keepdims=True) + eps_norm)
        normed = hidden * inverse
        scaled = (scale * normed).astype(BF16)
        logits = dot(join, scaled, TN)[0:32]
        real = klass < K
        largest = jnp.max(jnp.where(real, logits, -jnp.inf), axis=0, keepdims=True)
        shifted = jnp.where(real, jnp.exp(jnp.where(real, logits - largest, 0.0)), 0.0)
        totals = jnp.sum(shifted, axis=0, keepdims=True)
        onehot = klass == code_ref[ch, pl.ds(t, 1), :]
        picked = jnp.sum(jnp.where(onehot, logits, 0.0), axis=0, keepdims=True)
        share = losses[0, pl.ds(t, 1), :]
        losses[1, pl.ds(t, 1), :] = share * (largest + jnp.log(totals) - picked)
        slope = (share * (shifted / totals - jnp.where(onehot, 1.0, 0.0))).astype(BF16)
        grad_scaled = dot(join, jnp.concatenate([slope, jnp.zeros((96, 128), BF16)], axis=0), NN)
        jt[t, 0:24, :] = dot(slope, scaled, NT)[0:24]
        jt[t, 24:32, :] = dot(jnp.ones((8, 128), F32), grad_scaled * normed, NT, lax.Precision.HIGHEST)
        grad_normed = grad_scaled * scale
        along = jnp.sum(normed * grad_normed, axis=0, keepdims=True)
        grad_hidden = ((grad_normed - normed * along) * inverse).astype(BF16)
        gh[t] = grad_hidden
        gfeat[...] += dot(grad_hidden, low, TN)

    loop(TASKS, head_task)
    loss_tile = jnp.broadcast_to(jnp.sum(losses[1], axis=1, keepdims=True), (8, 128))
    jt[TASKS, 0:8, 0:128] = loss_tile
    jt[TASKS, 0:8, 128:256] = loss_tile

    my_mask = mask[quarter(ch), :]
    for c in range(4):
        gsend[c] = (gfeat[:, c * 128 : (c + 1) * 128] * my_mask * aall[c, 4:5, :]).astype(BF16)

    def g_copy(peer, k):
        return put(gsend.at[peer], grecv.at[ch], g_send.at[k], g_recv.at[ch], at(chan=peer))

    def q_copy(peer, k):
        rows = pl.ds(pl.multiple_of(peer * HC, HC), HC)
        return put(gh.at[:, rows, :], ghall.at[ch], q_send.at[k], q_recv.at[ch], at(chan=peer))

    def s_copy(peer, k):
        return put(jsend.at[peer], jrecv.at[ch], s_send.at[k], s_recv.at[ch], at(chan=peer))

    for k, peer in enumerate(peers):
        g_copy(peer, k).start()
    for i in range(2):
        x_relay(LAYERS, i)
    grecv[ch] = gsend[ch]
    low_lane = lax.broadcasted_iota(jnp.int32, (32, 128), 1) < HC
    for c in range(4):
        side = slice((c // 2) * 128, (c // 2) * 128 + 128)
        for m in range(4):
            one, two = jt[2 * m, :, side], jt[2 * m + 1, :, side]
            if m == 3:
                two = jnp.where(lax.broadcasted_iota(jnp.int32, (32, 128), 0) < 8, two, 0.0)
            if c % 2 == 0:
                two = pltpu.roll(two, HC, 1)
            else:
                one = pltpu.roll(one, HC, 1)
            jsend[c, m] = jnp.where(low_lane, one, two)
    for k, peer in enumerate(peers):
        s_copy(peer, k).start()
        q_copy(peer, k).start()
    ghall[ch] = gh[:, pl.ds(pl.multiple_of(ch * HC, HC), HC), :]
    jrecv[ch] = jsend[ch]

    def spread(l, i, grad):
        columns = (
            jnp.where(col_id < W - 1, pltpu.roll(grad, IMG - 1, 0), 0.0),
            grad,
            jnp.where(col_id >= 1, pltpu.roll(grad, 1, 0), 0.0),
        )
        top = pl.multiple_of(i * IMG, IMG)
        blank = jnp.zeros((W, 128), BF16)
        for e in range(3):
            low = columns[e].astype(BF16)
            gs[l * 9 + e, pl.ds(top, IMG - W), :] = low[W:]
            gs[l * 9 + e, pl.ds(top + IMG - W, W), :] = blank
            gs[l * 9 + 3 + e, pl.ds(top, IMG), :] = low
            gs[l * 9 + 6 + e, pl.ds(top + W, IMG - W), :] = low[: IMG - W]
            gs[l * 9 + 6 + e, pl.ds(top, W), :] = blank

    def conv_backward(l, i):
        rows = pl.ds(pl.multiple_of(i * IMG, IMG), IMG)
        lefts = []
        for first in range(0, 9, 2):
            taps = [t for t in (first, first + 1) if t < 9]
            sides = [gs[l * 9 + t, rows, :] for t in taps]
            lefts.append(jnp.concatenate(sides, axis=1) if len(sides) > 1 else sides[0])
        for h in range(2):
            total = None
            for first in range(0, 9, 2):
                taps = [t for t in (first, first + 1) if t < 9]
                sides = [wall[slots_ref[(l * 9 + t) * 2 + h]] for t in taps]
                side = jnp.concatenate(sides, axis=1) if len(sides) > 1 else sides[0]
                term = dot(lefts[first // 2], side, NT)
                total = term if total is None else total + term
            bpart[l - 1, i, h, 0] = total[:, :128]
            bpart[l - 1, i, h, 1] = total[:, 128:]

    def bc_copy(l, i):
        return put(
            bpart.at[l - 1, i, :, 1 - core],
            bcore.at[l - 1, i],
            bc_send.at[l - 1, i],
            bc_recv.at[l - 1, i],
            at(chan=partner),
        )

    def bx_copy(l, i):
        return put(bxs.at[l - 1, i], bx.at[l - 1, i], bx_send.at[l - 1, i], bx_recv.at[l - 1, i], at(chan=across))

    def weight_grads(l):
        def half(h):
            lhs = xt[l, h]

            def pair(p):
                t = 2 * p
                rhs = jnp.concatenate([gs[l * 9 + t], gs[l * 9 + t + 1]], axis=1)
                out = dot(lhs, rhs, NN)
                dw[(l * 9 + t) * 2 + h] = out[:, :128]
                dw[(l * 9 + t + 1) * 2 + h] = out[:, 128:]

            loop(4, pair)
            dw[(l * 9 + 8) * 2 + h] = dot(lhs, gs[l * 9 + 8], NN)

        loop(2, half)

    for peer in peers:
        came(grecv.at[peer], g_recv.at[peer])

    def top_grad(i):
        rows = pl.ds(pl.multiple_of(i * IMG, IMG), IMG)
        grad = jnp.concatenate([grecv[2 * i], grecv[2 * i + 1]], axis=0).astype(F32)
        spread(LAYERS - 1, i, grad * coef[LAYERS - 1, rows, :])

    loop(2, top_grad)
    x_side = ch // 2
    for l in (2, 1):

        def partial_image(i, l=l):
            conv_backward(l, i)
            bc_copy(l, i).start()

        loop(2, partial_image)

        def chip_sum(i, l=l):
            bc_copy(l, i).wait_recv()
            bxs[l - 1, i] = bpart[l - 1, i, 1 - x_side, core] + bcore[l - 1, i, 1 - x_side]
            bx_copy(l, i).start()

        loop(2, chip_sum)
        weight_grads(l)

        def finish_image(i, l=l):
            bx_copy(l, i).wait_recv()
            grad = bpart[l - 1, i, x_side, core] + bcore[l - 1, i, x_side] + bx[l - 1, i]
            rows = pl.ds(pl.multiple_of(i * IMG, IMG), IMG)
            spread(l - 1, i, grad * coef[l - 1, rows, :])

        loop(2, finish_image)
    weight_grads(0)

    for i in range(2):
        x_arrive(LAYERS, i)
    for peer in peers:
        came(ghall.at[peer], q_recv.at[peer])
        came(jrecv.at[peer], s_recv.at[peer])
    lhs = [
        jnp.concatenate([ghall[2 * m].reshape(TASKS * HC, 128), ghall[2 * m + 1].reshape(TASKS * HC, 128)], axis=1)
        for m in range(2)
    ]
    for c in range(0, 4, 2):
        total = None
        for m in range(2):
            rows = slice(m * IMG, (m + 1) * IMG)
            rhs = jnp.concatenate([xs[LAYERS, c, rows, :], xs[LAYERS, c + 1, rows, :]], axis=1)
            term = dot(lhs[m], rhs, NN)
            total = term if total is None else total + term
        hg[c * 448 : (c + 1) * 448, :] = total[:, :128]
        hg[(c + 1) * 448 : (c + 2) * 448, :] = total[:, 128:]
    if hg.shape[0] > 1792:
        hg[1792:, :] = jnp.zeros((hg.shape[0] - 1792, 128), F32)
    small[...] = jnp.zeros_like(small)
    for m in range(4):
        small[m * 32 : (m + 1) * 32, :] = jrecv[0, m] + jrecv[1, m] + jrecv[2, m] + jrecv[3, m]
    losses[2 + me] = small[96:104, :]

    def l_copy(i):
        dev = (me + i + 1) % n
        return put(losses.at[2 + me], losses.at[2 + me], l_send.at[i], l_recv.at[me], at(dp=dev))

    def part(dest, k):
        u = inv_ref[dest * slots_per + k]
        return dw[jnp.maximum(u, 0)] * jnp.where(u >= 0, 1.0, 0.0)

    def head_part(dest):
        rows = hg[pl.ds(pl.multiple_of(dest * piece, 16), piece), :]
        return rows, small[pl.ds(pl.multiple_of(dest * SMALL, SMALL), SMALL), :]

    def write(ref, values):
        codes, powers = encode(values)
        ref[0:256, :] = codes
        ref[256:272, :] = powers

    def read(ref):
        return decode(ref[0:256, :], ref[256:272, :])

    def write_head(ref, values):
        codes, powers = encode(values[0])
        ref[0:piece, :] = codes
        ref[piece : piece + 16, :] = powers
        codes, powers = encode(values[1])
        ref[piece + 16 : piece + 32, :] = codes
        ref[piece + 32 : piece + 48, :] = powers

    def read_head(ref):
        one = decode(ref[0:piece, :], ref[piece : piece + 16, :])
        return one, decode(ref[piece + 16 : piece + 32, :], ref[piece + 32 : piece + 48, :])

    def y_copy(zz, k):
        return put(ysend.at[zz, k], yrecv.at[zz, k], y_send.at[zz, k], y_recv.at[zz, k], other)

    def z_right(zz, k):
        return put(lsend.at[zz, k], lleft.at[zz, k], z_send.at[zz, k], zl_recv.at[zz, k], right)

    def z_left(zz, k):
        return put(lsend.at[zz, k], lright.at[zz, k], z_send.at[zz, k], zr_recv.at[zz, k], left)

    def cross(zz):
        dest = zz * 2 + 1 - y

        def block(k):
            write(ysend.at[zz, k], part(dest, k))
            y_copy(zz, k).start()

        loop(first_a, block)
        write_head(ysend.at[zz, first_a], head_part(dest))
        y_copy(zz, first_a).start()

    def pass_on(zz, k):
        @pl.when(zz > z)
        def _():
            z_right(zz, k).start()

        @pl.when(zz < z)
        def _():
            z_left(zz, k).start()

    def line_conv(zz, k):
        is_a, is_own = k < first_a, k < slots_per
        dest = zz * 2 + jnp.where(is_own, y, 1 - y)
        slot = jnp.where(is_own, k, k - last_b)
        zsum[...] = part(dest, slot)

        @pl.when(is_a)
        def _():
            came(yrecv.at[zz, k], y_recv.at[zz, k])
            zsum[...] += read(yrecv.at[zz, k])

        @pl.when((zz >= z) & has_left)
        def _():
            came(lleft.at[zz, k], zl_recv.at[zz, k])
            zsum[...] += read(lleft.at[zz, k])

        @pl.when((zz <= z) & has_right)
        def _():
            came(lright.at[zz, k], zr_recv.at[zz, k])
            zsum[...] += read(lright.at[zz, k])

    def line_head(zz):
        k = cargo - 1
        dest = zz * 2 + y
        rows, few = head_part(dest)
        zsum[0:piece, :] = rows
        zsum[piece : piece + SMALL, :] = few
        came(yrecv.at[zz, first_a], y_recv.at[zz, first_a])

        def add(ref):
            one, two = read_head(ref)
            zsum[0:piece, :] += one
            zsum[piece : piece + SMALL, :] += two

        add(yrecv.at[zz, first_a])

        @pl.when((zz >= z) & has_left)
        def _():
            came(lleft.at[zz, k], zl_recv.at[zz, k])
            add(lleft.at[zz, k])

        @pl.when((zz <= z) & has_right)
        def _():
            came(lright.at[zz, k], zr_recv.at[zz, k])
            add(lright.at[zz, k])

    def head_values():
        return zsum[0:piece, :], zsum[piece : piece + SMALL, :]

    def out_step(d):
        for zz, ok in ((z - d, z - d >= 0), (z + d, z + d < nz)):

            @pl.when(ok)
            def _(zz=zz):
                cross(zz)

        for zz, ok in ((z - d, z - d >= 0), (z + d, z + d < nz)):

            @pl.when(ok)
            def _(zz=zz):
                def block(k):
                    line_conv(zz, k)
                    write(lsend.at[zz, k], zsum[...])
                    pass_on(zz, k)

                loop(cargo - 1, block)
                line_head(zz)
                write_head(lsend.at[zz, cargo - 1], head_values())
                pass_on(zz, cargo - 1)

    loop(nz - 1, lambda i: out_step(nz - 1 - i))
    loop(n - 1, lambda i: l_copy(i).start())
    cross(z)

    def b_copy(k):
        return put(bsend2.at[k], brecv2.at[k], b_send.at[k], b_recv.at[k], other)

    def give_b(k):
        line_conv(z, slots_per + k)
        write(bsend2.at[k], zsum[...])
        b_copy(k).start()

    loop(last_b, give_b)

    line_head(z)
    write_head(hag.at[me], head_values())

    def tag(j):
        return hag.at[j]

    def t_right(j):
        return put(tag(j), tag(j), t_zr.at[j], t_recv.at[j], right)

    def t_left(j):
        return put(tag(j), tag(j), t_zl.at[j], t_recv.at[j], left)

    def t_other(j):
        return put(tag(j), tag(j), t_y.at[j], t_recv.at[j], other)

    @pl.when(has_right)
    def _():
        t_right(me).start()

    @pl.when(has_left)
    def _():
        t_left(me).start()

    t_other(me).start()

    def own_slot(k):
        line_conv(z, k)
        grad_out[k] = zsum[...]

    loop(first_a, own_slot)

    def tail(d):
        @pl.when(z - d - 1 >= 0)
        def _():
            j = (z - d - 1) * 2 + y
            came(tag(j), t_recv.at[j])

            @pl.when(has_right)
            def _():
                t_right(j).start()

            t_other(j).start()

        @pl.when(z + d + 1 < nz)
        def _():
            j = (z + d + 1) * 2 + y
            came(tag(j), t_recv.at[j])

            @pl.when(has_left)
            def _():
                t_left(j).start()

            t_other(j).start()

    loop(nz - 1, tail)

    def own_last(k):
        line_conv(z, first_a + k)
        came(brecv2.at[k], b_recv.at[k])
        grad_out[first_a + k] = zsum[...] + read(brecv2.at[k])

    loop(last_b, own_last)

    loop(n - 1, lambda i: came(losses.at[2 + (me + i + 1) % n], l_recv.at[(me + i + 1) % n]))
    loss_out[...] = lax.fori_loop(0, n, lambda i, acc: acc + losses[2 + i], jnp.zeros((8, 128), F32))

    def other_row(zz):
        j = zz * 2 + 1 - y
        came(tag(j), t_recv.at[j])

    loop(nz, other_row)
    per = 448 // piece

    def unpack(j):
        one, two = read_head(hag.at[j])

        @pl.when(j < 4 * per)
        def _():
            rows = pl.ds(pl.multiple_of((j % per) * piece, 16), piece)
            head_out[rows, pl.ds(pl.multiple_of((j // per) * 128, 128), 128)] = one

        @pl.when(j < 8)
        def _():
            small_out[pl.ds(pl.multiple_of(j * SMALL, SMALL), SMALL), :] = two

    loop(n, unpack)

    def drain_w(s):
        k = s % slots_per
        zz, row = s // (2 * slots_per), (s // slots_per) % 2
        on_line = (row == y) | (k >= first_a)

        @pl.when(on_line & has_right & (zz <= z))
        def _():
            left_it(wall.at[s], w_zr.at[s])

        @pl.when(on_line & has_left & (zz >= z))
        def _():
            left_it(wall.at[s], w_zl.at[s])

        @pl.when((row == y) & ((k < first_a) | (zz == z)))
        def _():
            left_it(wall.at[s], w_y.at[s])

    loop(n * slots_per, drain_w)

    def drain_t(zz):
        j = zz * 2 + y

        @pl.when(has_right & (zz <= z))
        def _():
            left_it(tag(j), t_zr.at[j])

        @pl.when(has_left & (zz >= z))
        def _():
            left_it(tag(j), t_zl.at[j])

        left_it(tag(j), t_y.at[j])

        def y_block(k):
            y_copy(zz, k).wait_send()

        loop(first_a + 1, y_block)

        @pl.when(zz != z)
        def _():
            loop(cargo, lambda k: left_it(lsend.at[zz, k], z_send.at[zz, k]))

    loop(nz, drain_t)
    loop(last_b, lambda k: b_copy(k).wait_send())
    for l in range(LAYERS + 1):
        for i in range(2):
            x_drain(l, i)
    for k in range(3):
        loop(TASKS, lambda t, k=k: h_copy(t, ch, partner, k).wait_send())
        j_copy(ch, partner, k).wait_send()
        a_copy(ch, partner, k).wait_send()
    for k, peer in enumerate(peers):
        f_copy(peer, k).wait_send()
        g_copy(peer, k).wait_send()
        q_copy(peer, k).wait_send()
        s_copy(peer, k).wait_send()
    for l in (1, 2):
        for i in range(2):
            bc_copy(l, i).wait_send()
            bx_copy(l, i).wait_send()
    loop(n - 1, lambda i: c_copy(i).wait_send())
    loop(n - 1, lambda i: l_copy(i).wait_send())


def adamw(weight, gradient, moment_one, moment_two, step_rate, step_count):
    step_float = step_count[0].astype(F32)
    moment_one = beta_one * moment_one + (1.0 - beta_one) * gradient
    moment_two = beta_two * moment_two + (1.0 - beta_two) * gradient * gradient
    first_hat = moment_one / (1.0 - beta_one**step_float)
    second_hat = moment_two / (1.0 - beta_two**step_float)
    weight = weight - step_rate * (
        first_hat / (jnp.sqrt(second_hat) + eps_adam) + decay_rate * weight
    )
    return (weight, moment_one, moment_two)


def per_device(
    n,
    inputs,
    affine,
    image_sizes,
    labels,
    label_mask,
    unit_slots,
    conv_master,
    conv_first,
    conv_second,
    head_master,
    head_first,
    head_second,
    join_master,
    join_first,
    join_second,
    scale_master,
    scale_first,
    scale_second,
    step_count,
):
    slots_per = conv_master.shape[0]
    nz = n // 2
    last_b = slots_per // 7
    first_a = slots_per - last_b
    cargo = slots_per + last_b + 1
    piece = -(-1792 // (n * 16)) * 16
    code = jnp.where(label_mask > 0, labels, -1).reshape(4, 128, TASKS).transpose(0, 2, 1)
    code = jnp.pad(code, ((0, 0), (0, 8 - TASKS), (0, 0)), constant_values=-1)
    join_pad = jnp.concatenate(
        [
            join_master,
            jnp.zeros((TASKS, HC, 32 - K), F32),
            scale_master[:, :, None],
            jnp.zeros((TASKS, HC, 128 - 33), F32),
        ],
        axis=2,
    )
    affine_pad = jnp.pad(affine.reshape(2 * LAYERS, 128), ((0, 2), (0, 0)))
    vm, sm, dma = pltpu.VMEM, pltpu.SMEM, pltpu.SemaphoreType.DMA
    shape = jax.ShapeDtypeStruct
    scratch = [
        vm((n * slots_per, 256, 128), BF16),
        vm((LAYERS + 1, 4, PX, 128), BF16),
        vm((LAYERS, 2, 256, PX), BF16),
        vm((TASKS, 4, HC, C), BF16),
        vm((TASKS, 4, HC, 128), F32),
        vm((4, 8, 128), F32),
        vm((n, 8, 128), F32),
        vm((n + 2, 8, 128), F32),
        sm((n * slots_per,), jnp.int32),
        vm((PX, 128), F32),
        vm((LAYERS, PX, 128), F32),
        vm((3, IMG, 128), F32),
        vm((4, 128, 128), BF16),
        vm((TASKS, 256, 128), BF16),
        vm((4, TASKS, HC, 128), BF16),
        vm((128, C), F32),
        vm((4, 128, 128), BF16),
        vm((4, 128, 128), BF16),
        vm((8, 32, 256), F32),
        vm((4, 4, 32, 128), F32),
        vm((4, 4, 32, 128), F32),
        vm((27, PX, 128), BF16),
        vm((2, 2, 2, 2, IMG, 128), F32),
        vm((2, 2, 2, IMG, 128), F32),
        vm((2, 2, IMG, 128), F32),
        vm((2, 2, IMG, 128), F32),
        vm((54, 256, 128), F32),
        vm((n * piece, 128), F32),
        vm((n * SMALL, 128), F32),
        vm((nz, first_a + 1, CHUNK, 128), jnp.int16),
        vm((nz, first_a + 1, CHUNK, 128), jnp.int16),
        vm((nz, cargo, CHUNK, 128), jnp.int16),
        vm((nz, cargo, CHUNK, 128), jnp.int16),
        vm((nz, cargo, CHUNK, 128), jnp.int16),
        vm((max(last_b, 1), CHUNK, 128), jnp.int16),
        vm((max(last_b, 1), CHUNK, 128), jnp.int16),
        vm((n, CHUNK, 128), jnp.int16),
        vm((256, 128), F32),
        *[dma((n * slots_per,)) for _ in range(4)],
        *[dma((LAYERS + 1, 2, 3)) for _ in range(2)],
        *[dma((TASKS, 3)) for _ in range(2)],
        *[dma((3,)) for _ in range(4)],
        *[dma((n,)) for _ in range(4)],
        dma((3,)), dma((4,)),
        dma((3,)), dma((4,)),
        dma((3,)), dma((4,)),
        dma((3,)), dma((4,)),
        *[dma((2, 2)) for _ in range(4)],
        *[dma((nz, first_a + 1)) for _ in range(2)],
        *[dma((nz, cargo)) for _ in range(3)],
        *[dma((max(last_b, 1),)) for _ in range(2)],
        *[dma((n,)) for _ in range(4)],
    ]
    in_smem, in_vmem = pl.BlockSpec(memory_space=pltpu.SMEM), pl.BlockSpec(memory_space=pltpu.VMEM)
    slot_grads, head_total, small_total, loss_total = pl.pallas_call(
        functools.partial(kernel, n, slots_per),
        out_shape=(
            shape((slots_per, 256, 128), F32),
            shape((448, C), F32),
            shape((128, 128), F32),
            shape((8, 128), F32),
        ),
        in_specs=[in_smem] * 2 + [in_vmem] * 6,
        out_specs=(in_vmem,) * 4,
        scratch_shapes=scratch,
        compiler_params=pltpu.CompilerParams(
            collective_id=0, has_side_effects=True, vmem_limit_bytes=60 * 2**20
        ),
    )(
        unit_slots,
        image_sizes,
        inputs.reshape(PX, 128),
        affine_pad,
        code,
        conv_master,
        head_master,
        join_pad,
    )
    pairs = small_total.reshape(4, 32, 2, HC).transpose(0, 2, 1, 3).reshape(8, 32, HC)[:TASKS]
    join_total = pairs[:, :K].transpose(0, 2, 1)
    scale_total = pairs[:, 24]
    head_total = head_total.reshape(TASKS, HC, C)
    conv_out = adamw(conv_master, slot_grads, conv_first, conv_second, 0.01, step_count)
    head_out = adamw(head_master, head_total, head_first, head_second, 0.03, step_count)
    join_out = adamw(join_master, join_total, join_first, join_second, 0.4, step_count)
    scale_out = adamw(scale_master, scale_total, scale_first, scale_second, 0.8, step_count)
    loss = jnp.sum(loss_total[:TASKS, 64])
    return (loss.reshape(1),) + conv_out + head_out + join_out + scale_out


def solution(mesh):
    placed = (
        P("dp", None, None, "chan"),
        P(None, None, "chan"),
        P("dp", None),
        P("dp", None, None, None),
        P("dp", None, None, None),
        P(),
        P("dp", None, "chan"),
        P("dp", None, "chan"),
        P("dp", None, "chan"),
        P(None, "chan", None),
        P(None, "chan", None),
        P(None, "chan", None),
        P(None, "chan", None),
        P(None, "chan", None),
        P(None, "chan", None),
        P(None, "chan"),
        P(None, "chan"),
        P(None, "chan"),
        P(),
    )
    return jax.shard_map(
        functools.partial(per_device, mesh.shape["dp"]),
        mesh=mesh,
        in_specs=placed,
        out_specs=(P(),) + placed[6:18],
        check_vma=False,
    )
```

```python
import functools

import jax
import jax.numpy as jnp
from jax import lax
from jax.experimental import pallas as pl
from jax.experimental.pallas import tpu as pltpu
from jax.sharding import PartitionSpec as P

C = 512
K = 21
TASKS = 7
LAYERS = 3
H = 16
W = 16
PX = 512
IMG = 256
HC = 64
CHUNK = 272
SMALL = 16

beta_one = 0.9
beta_two = 0.999
eps_adam = 1e-08
decay_rate = 0.01
eps_norm = 1e-06

F32 = jnp.float32
BF16 = jnp.bfloat16
MESH = pl.DeviceIdType.MESH
NN = (((1,), (0,)), ((), ()))
NT = (((1,), (1,)), ((), ()))
TN = (((0,), (0,)), ((), ()))


def dot(a, b, dims, precision=None):
    return lax.dot_general(a, b, dims, precision=precision, preferred_element_type=F32)


def encode(values):
    top = jnp.max(jnp.abs(values), axis=0, keepdims=True)
    power = jnp.ceil(jnp.log2(jnp.maximum(top, 1e-30))) - 14.0
    codes = jnp.round(values * jnp.exp2(-power)).astype(jnp.int32).astype(jnp.int16)
    powers = jnp.broadcast_to(power, (16, 128)).astype(jnp.int32).astype(jnp.int16)
    return codes, powers


def decode(codes, powers):
    return codes.astype(F32) * jnp.exp2(powers.astype(F32)[0:1])


def kernel(
    n,
    slots_per,
    slots_ref,
    inv_ref,
    sizes_ref,
    inputs_ref,
    affine_ref,
    code_ref,
    conv_ref,
    head_ref,
    join_ref,
    grad_out,
    head_out,
    small_out,
    loss_out,
    wall,
    xs,
    xt,
    hall,
    jall,
    aall,
    cnt,
    losses,
    mask,
    coef,
    zacc,
    fbuf,
    gh,
    ghall,
    gfeat,
    gsend,
    grecv,
    jt,
    jsend,
    jrecv,
    gs,
    bpart,
    bcore,
    bx,
    bxs,
    dw,
    hg,
    small,
    ysend,
    yrecv,
    lsend,
    lright,
    lleft,
    bsend2,
    brecv2,
    hag,
    zsum,
    w_recv,
    w_zr,
    w_zl,
    w_y,
    x_send,
    x_recv,
    h_send,
    h_recv,
    j_send,
    j_recv,
    a_send,
    a_recv,
    c_send,
    c_recv,
    l_send,
    l_recv,
    f_send,
    f_recv,
    g_send,
    g_recv,
    q_send,
    q_recv,
    s_send,
    s_recv,
    bc_send,
    bc_recv,
    bx_send,
    bx_recv,
    y_send,
    y_recv,
    z_send,
    zr_recv,
    zl_recv,
    b_send,
    b_recv,
    t_recv,
    t_zr,
    t_zl,
    t_y,
):
    nz = n // 2
    last_b = slots_per // 7
    first_a = slots_per - last_b
    cargo = slots_per + last_b + 1
    piece = hg.shape[0] // n

    me = lax.axis_index("dp")
    ch = lax.axis_index("chan")
    z, y = me // 2, me % 2
    core = ch % 2
    partner = ch + 1 - 2 * core
    across = (ch + 2) % 4
    far = (partner + 2) % 4

    def at(dp=None, chan=None):
        return {"dp": me if dp is None else dp, "chan": ch if chan is None else chan}

    right, left, other = at(dp=me + 2), at(dp=me - 2), at(dp=z * 2 + 1 - y)
    has_right, has_left = z < nz - 1, z > 0

    def put(src, dst, send, recv, dev):
        return pltpu.make_async_remote_copy(
            src_ref=src, dst_ref=dst, send_sem=send, recv_sem=recv, device_id=dev, device_id_type=MESH
        )

    def came(ref, recv):
        put(ref, ref, recv, recv, other).wait_recv()

    def left_it(ref, send):
        put(ref, ref, send, send, other).wait_send()

    def loop(count, body):
        lax.fori_loop(0, count, lambda i, c: (body(i), c)[1], 0)

    barrier = pltpu.get_barrier_semaphore()

    def greet(i):
        pl.semaphore_signal(barrier, inc=1, device_id=at(dp=(me + i + 1) % n), device_id_type=MESH)

    loop(n - 1, greet)
    for peer in (partner, across, far):
        pl.semaphore_signal(barrier, inc=1, device_id=at(chan=peer), device_id_type=MESH)

    def cast_block(k):
        wall[me * slots_per + k] = conv_ref[k].astype(BF16)

    loop(slots_per, cast_block)
    pixel = lax.broadcasted_iota(jnp.int32, (IMG, 128), 0)
    row_id, col_id = pixel // W, pixel % W

    def mask_image(i):
        inside = (row_id < sizes_ref[i, 0]) & (col_id < sizes_ref[i, 1])
        rows = pl.ds(pl.multiple_of(i * IMG, IMG), IMG)
        mask[rows, :] = jnp.where(inside, 1.0, 0.0)
        xs[0, ch, rows, :] = (inputs_ref[rows, :].astype(F32) * mask[rows, :]).astype(BF16)

    loop(2, mask_image)

    def cast_head(t):
        hall[t, ch] = head_ref[t].astype(BF16)
        jall[t, ch] = join_ref[t]

    loop(TASKS, cast_head)
    aall[ch] = affine_ref[...]

    lane = lax.broadcasted_iota(jnp.int32, (8, 128), 1)

    def kept(q):
        spot = (q % 2) * 128 + lane
        hit = (spot // W < sizes_ref[q // 2, 0]) & (spot % W < sizes_ref[q // 2, 1])
        return jnp.where(hit & (code_ref[q] >= 0), 1.0, 0.0)

    total_kept = kept(0) + kept(1) + kept(2) + kept(3)
    cnt[me] = jnp.broadcast_to(jnp.sum(total_kept, axis=1, keepdims=True), (8, 128))

    pl.semaphore_wait(barrier, n - 1 + 3)

    def to_right(s):
        return put(wall.at[s], wall.at[s], w_zr.at[s], w_recv.at[s], right)

    def to_left(s):
        return put(wall.at[s], wall.at[s], w_zl.at[s], w_recv.at[s], left)

    def to_other(s):
        return put(wall.at[s], wall.at[s], w_y.at[s], w_recv.at[s], other)

    def both_ways(s):
        @pl.when(has_right)
        def _():
            to_right(s).start()

        @pl.when(has_left)
        def _():
            to_left(s).start()

    def x_copy(l, i, owner, peer, k):
        rows = pl.ds(pl.multiple_of(i * IMG, IMG), IMG)
        ref = xs.at[l, owner, rows, :]
        return put(ref, ref, x_send.at[l, i, k], x_recv.at[l, i, k], at(chan=peer))

    def x_start(l, i):
        x_copy(l, i, ch, across, 0).start()
        x_copy(l, i, ch, partner, 1).start()

    def x_relay(l, i):
        x_copy(l, i, across, across, 0).wait_recv()
        x_copy(l, i, across, partner, 2).start()

    def x_arrive(l, i):
        x_copy(l, i, partner, partner, 1).wait_recv()
        x_copy(l, i, far, partner, 2).wait_recv()

    def x_drain(l, i):
        for k in range(3):
            x_copy(l, i, ch, partner, k).wait_send()

    def h_copy(t, owner, peer, k):
        ref = hall.at[t, owner]
        return put(ref, ref, h_send.at[t, k], h_recv.at[t, k], at(chan=peer))

    def j_copy(owner, peer, k):
        ref = jall.at[:, owner]
        return put(ref, ref, j_send.at[k], j_recv.at[k], at(chan=peer))

    def a_copy(owner, peer, k):
        ref = aall.at[owner]
        return put(ref, ref, a_send.at[k], a_recv.at[k], at(chan=peer))

    def c_copy(i):
        dev = (me + i + 1) % n
        return put(cnt.at[me], cnt.at[me], c_send.at[i], c_recv.at[me], at(dp=dev))

    base = me * slots_per

    def own_b(k):
        to_other(base + first_a + k).start()

    loop(last_b, own_b)

    def own_a(k):
        both_ways(base + k)
        to_other(base + k).start()

    loop(first_a, own_a)
    for i in range(2):
        x_start(0, i)

    def own_head(t):
        h_copy(t, ch, across, 0).start()
        h_copy(t, ch, partner, 1).start()

    loop(TASKS, own_head)
    loop(last_b, lambda k: both_ways(base + first_a + k))
    for copy in (j_copy, a_copy):
        copy(ch, across, 0).start()
        copy(ch, partner, 1).start()
    loop(n - 1, lambda i: c_copy(i).start())

    neighbour = (z * 2 + 1 - y) * slots_per

    def pass_b(k):
        s = neighbour + first_a + k
        came(wall.at[s], w_recv.at[s])
        both_ways(s)

    loop(last_b, pass_b)
    for i in range(2):
        x_relay(0, i)

    def relay_head(t):
        h_copy(t, across, across, 0).wait_recv()
        h_copy(t, across, partner, 2).start()

    def line_in(d, c):
        def source(zz):
            row = jnp.where(c < slots_per, y, 1 - y)
            return (zz * 2 + row) * slots_per + jnp.where(c < slots_per, c, c - last_b)

        @pl.when(z - d >= 0)
        def _():
            s = source(z - d)
            came(wall.at[s], w_recv.at[s])

            @pl.when(has_right)
            def _():
                to_right(s).start()

            @pl.when(c < first_a)
            def _():
                to_other(s).start()

        @pl.when(z + d < nz)
        def _():
            s = source(z + d)
            came(wall.at[s], w_recv.at[s])

            @pl.when(has_left)
            def _():
                to_left(s).start()

            @pl.when(c < first_a)
            def _():
                to_other(s).start()

    def first_step(c):
        pl.when(c < slots_per + last_b)(lambda: line_in(1, c))
        pl.when(c < TASKS)(lambda: relay_head(c))

    loop(max(slots_per + last_b, TASKS), first_step)
    for copy in (j_copy, a_copy):
        copy(across, across, 0).wait_recv()
        copy(across, partner, 2).start()

    def transpose_layer(l):
        for c in range(4):
            xt[l, c // 2, (c % 2) * 128 : (c % 2) * 128 + 128, :] = xs[l, c].T

    for i in range(2):
        x_arrive(0, i)
    transpose_layer(0)

    loop(nz - 2, lambda d: loop(slots_per + last_b, lambda c: line_in(d + 2, c)))

    def last_in(zz):
        def block(k):
            s = (zz * 2 + 1 - y) * slots_per + k
            came(wall.at[s], w_recv.at[s])

        loop(first_a, block)

    loop(nz, last_in)

    def conv_forward(l, i):
        rows = pl.ds(pl.multiple_of(i * IMG, IMG), IMG)
        left_side = jnp.concatenate([xs[l, c, rows, :] for c in range(4)], axis=1)
        zacc[...] = jnp.zeros_like(zacc)
        for first in range(0, 9, 2):
            taps = [t for t in (first, first + 1) if t < 9]
            sides = [
                jnp.concatenate([wall[slots_ref[(l * 9 + t) * 2 + h]] for h in range(2)], axis=0)
                for t in taps
            ]
            side = jnp.concatenate(sides, axis=1) if len(sides) > 1 else sides[0]
            out = dot(left_side, side, NN)
            for k, t in enumerate(taps):
                a, e = divmod(t, 3)
                part = out[:, k * 128 : (k + 1) * 128]
                if a == 0:
                    zacc[e, W:IMG, :] += part[: IMG - W]
                elif a == 1:
                    zacc[e] += part
                else:
                    zacc[e, : IMG - W, :] += part[W:]
        linear = zacc[1]
        linear += jnp.where(col_id >= 1, pltpu.roll(zacc[0], 1, 0), 0.0)
        linear += jnp.where(col_id < W - 1, pltpu.roll(zacc[2], IMG - 1, 0), 0.0)
        inside = mask[rows, :]
        gain, shift = affine_ref[2 * l : 2 * l + 1, :], affine_ref[2 * l + 1 : 2 * l + 2, :]
        passed = jnp.where(linear > 0, inside, 0.0)
        coef[l, rows, :] = passed * gain if l < LAYERS - 1 else passed
        out = (jnp.maximum(linear, 0.0) * gain + shift) * inside
        xs[l + 1, ch, rows, :] = out.astype(BF16)

    def quarter(q):
        return pl.ds(pl.multiple_of(q * 128, 128), 128)

    for l in range(LAYERS):

        def forward_image(i, l=l):
            if l > 0:
                x_relay(l, i)
                x_arrive(l, i)
            conv_forward(l, i)
            if l < LAYERS - 1:
                x_start(l + 1, i)

        loop(2, forward_image)
        if 0 < l:
            transpose_layer(l)

    def f_copy(peer, k):
        return put(xs.at[LAYERS, ch, quarter(peer), :], fbuf.at[ch], f_send.at[k], f_recv.at[ch], at(chan=peer))

    peers = (across, far, partner)
    for k, peer in enumerate(peers):
        f_copy(peer, k).start()
    for i in range(2):
        x_start(LAYERS, i)
    fbuf[ch] = xs[LAYERS, ch, quarter(ch), :]

    loop(n - 1, lambda i: came(cnt.at[(me + i + 1) % n], c_recv.at[(me + i + 1) % n]))
    counts = lax.fori_loop(0, n, lambda i, acc: acc + cnt[i], jnp.zeros((8, 128), F32))
    counts = jnp.maximum(counts, 1.0)

    def head_in(t):
        h_copy(t, partner, partner, 1).wait_recv()
        h_copy(t, far, partner, 2).wait_recv()

    loop(TASKS, head_in)
    for copy in (j_copy, a_copy):
        copy(partner, partner, 1).wait_recv()
        copy(far, partner, 2).wait_recv()
    for peer in peers:
        came(fbuf.at[peer], f_recv.at[peer])

    weight = kept(ch) / counts
    losses[0] = weight
    losses[1] = jnp.zeros((8, 128), F32)
    features = jnp.concatenate([fbuf[c] for c in range(4)], axis=1)
    gfeat[...] = jnp.zeros_like(gfeat)
    klass = lax.broadcasted_iota(jnp.int32, (32, 128), 0)

    def head_task(t):
        low = hall[t].reshape(4 * HC, C)
        both = jall[t].reshape(4 * HC, 128)
        join = both.astype(BF16)
        scale = both[:, 32:33]
        hidden = dot(low, features, NT)
        inverse = lax.rsqrt(jnp.sum(hidden * hidden, axis=0, keepdims=True) + eps_norm)
        normed = hidden * inverse
        scaled = (scale * normed).astype(BF16)
        logits = dot(join, scaled, TN)[0:32]
        real = klass < K
        largest = jnp.max(jnp.where(real, logits, -jnp.inf), axis=0, keepdims=True)
        shifted = jnp.where(real, jnp.exp(jnp.where(real, logits - largest, 0.0)), 0.0)
        totals = jnp.sum(shifted, axis=0, keepdims=True)
        onehot = klass == code_ref[ch, pl.ds(t, 1), :]
        picked = jnp.sum(jnp.where(onehot, logits, 0.0), axis=0, keepdims=True)
        share = losses[0, pl.ds(t, 1), :]
        losses[1, pl.ds(t, 1), :] = share * (largest + jnp.log(totals) - picked)
        slope = (share * (shifted / totals - jnp.where(onehot, 1.0, 0.0))).astype(BF16)
        grad_scaled = dot(join, jnp.concatenate([slope, jnp.zeros((96, 128), BF16)], axis=0), NN)
        jt[t, 0:24, :] = dot(slope, scaled, NT)[0:24]
        jt[t, 24:32, :] = dot(jnp.ones((8, 128), F32), grad_scaled * normed, NT, lax.Precision.HIGHEST)
        grad_normed = grad_scaled * scale
        along = jnp.sum(normed * grad_normed, axis=0, keepdims=True)
        grad_hidden = ((grad_normed - normed * along) * inverse).astype(BF16)
        gh[t] = grad_hidden
        gfeat[...] += dot(grad_hidden, low, TN)

    loop(TASKS, head_task)
    loss_tile = jnp.broadcast_to(jnp.sum(losses[1], axis=1, keepdims=True), (8, 128))
    jt[TASKS, 0:8, 0:128] = loss_tile
    jt[TASKS, 0:8, 128:256] = loss_tile

    my_mask = mask[quarter(ch), :]
    for c in range(4):
        gsend[c] = (gfeat[:, c * 128 : (c + 1) * 128] * my_mask * aall[c, 4:5, :]).astype(BF16)

    def g_copy(peer, k):
        return put(gsend.at[peer], grecv.at[ch], g_send.at[k], g_recv.at[ch], at(chan=peer))

    def q_copy(peer, k):
        rows = pl.ds(pl.multiple_of(peer * HC, HC), HC)
        return put(gh.at[:, rows, :], ghall.at[ch], q_send.at[k], q_recv.at[ch], at(chan=peer))

    def s_copy(peer, k):
        return put(jsend.at[peer], jrecv.at[ch], s_send.at[k], s_recv.at[ch], at(chan=peer))

    for k, peer in enumerate(peers):
        g_copy(peer, k).start()
    for i in range(2):
        x_relay(LAYERS, i)
    grecv[ch] = gsend[ch]
    low_lane = lax.broadcasted_iota(jnp.int32, (32, 128), 1) < HC
    for c in range(4):
        side = slice((c // 2) * 128, (c // 2) * 128 + 128)
        for m in range(4):
            one, two = jt[2 * m, :, side], jt[2 * m + 1, :, side]
            if m == 3:
                two = jnp.where(lax.broadcasted_iota(jnp.int32, (32, 128), 0) < 8, two, 0.0)
            if c % 2 == 0:
                two = pltpu.roll(two, HC, 1)
            else:
                one = pltpu.roll(one, HC, 1)
            jsend[c, m] = jnp.where(low_lane, one, two)
    for k, peer in enumerate(peers):
        s_copy(peer, k).start()
        q_copy(peer, k).start()
    ghall[ch] = gh[:, pl.ds(pl.multiple_of(ch * HC, HC), HC), :]
    jrecv[ch] = jsend[ch]

    def spread(l, i, grad):
        columns = (
            jnp.where(col_id < W - 1, pltpu.roll(grad, IMG - 1, 0), 0.0),
            grad,
            jnp.where(col_id >= 1, pltpu.roll(grad, 1, 0), 0.0),
        )
        top = pl.multiple_of(i * IMG, IMG)
        blank = jnp.zeros((W, 128), BF16)
        for e in range(3):
            low = columns[e].astype(BF16)
            gs[l * 9 + e, pl.ds(top, IMG - W), :] = low[W:]
            gs[l * 9 + e, pl.ds(top + IMG - W, W), :] = blank
            gs[l * 9 + 3 + e, pl.ds(top, IMG), :] = low
            gs[l * 9 + 6 + e, pl.ds(top + W, IMG - W), :] = low[: IMG - W]
            gs[l * 9 + 6 + e, pl.ds(top, W), :] = blank

    def conv_backward(l, i):
        rows = pl.ds(pl.multiple_of(i * IMG, IMG), IMG)
        lefts = []
        for first in range(0, 9, 2):
            taps = [t for t in (first, first + 1) if t < 9]
            sides = [gs[l * 9 + t, rows, :] for t in taps]
            lefts.append(jnp.concatenate(sides, axis=1) if len(sides) > 1 else sides[0])
        for h in range(2):
            total = None
            for first in range(0, 9, 2):
                taps = [t for t in (first, first + 1) if t < 9]
                sides = [wall[slots_ref[(l * 9 + t) * 2 + h]] for t in taps]
                side = jnp.concatenate(sides, axis=1) if len(sides) > 1 else sides[0]
                term = dot(lefts[first // 2], side, NT)
                total = term if total is None else total + term
            bpart[l - 1, i, h, 0] = total[:, :128]
            bpart[l - 1, i, h, 1] = total[:, 128:]

    def bc_copy(l, i):
        return put(
            bpart.at[l - 1, i, :, 1 - core],
            bcore.at[l - 1, i],
            bc_send.at[l - 1, i],
            bc_recv.at[l - 1, i],
            at(chan=partner),
        )

    def bx_copy(l, i):
        return put(bxs.at[l - 1, i], bx.at[l - 1, i], bx_send.at[l - 1, i], bx_recv.at[l - 1, i], at(chan=across))

    def weight_grads(l):
        def half(h):
            lhs = xt[l, h]

            def pair(p):
                t = 2 * p
                rhs = jnp.concatenate([gs[l * 9 + t], gs[l * 9 + t + 1]], axis=1)
                out = dot(lhs, rhs, NN)
                dw[(l * 9 + t) * 2 + h] = out[:, :128]
                dw[(l * 9 + t + 1) * 2 + h] = out[:, 128:]

            loop(4, pair)
            dw[(l * 9 + 8) * 2 + h] = dot(lhs, gs[l * 9 + 8], NN)

        loop(2, half)

    for peer in peers:
        came(grecv.at[peer], g_recv.at[peer])

    def top_grad(i):
        rows = pl.ds(pl.multiple_of(i * IMG, IMG), IMG)
        grad = jnp.concatenate([grecv[2 * i], grecv[2 * i + 1]], axis=0).astype(F32)
        spread(LAYERS - 1, i, grad * coef[LAYERS - 1, rows, :])

    loop(2, top_grad)
    x_side = ch // 2
    for l in (2, 1):

        def partial_image(i, l=l):
            conv_backward(l, i)
            bc_copy(l, i).start()

        loop(2, partial_image)

        def chip_sum(i, l=l):
            bc_copy(l, i).wait_recv()
            bxs[l - 1, i] = bpart[l - 1, i, 1 - x_side, core] + bcore[l - 1, i, 1 - x_side]
            bx_copy(l, i).start()

        loop(2, chip_sum)
        weight_grads(l)

        def finish_image(i, l=l):
            bx_copy(l, i).wait_recv()
            grad = bpart[l - 1, i, x_side, core] + bcore[l - 1, i, x_side] + bx[l - 1, i]
            rows = pl.ds(pl.multiple_of(i * IMG, IMG), IMG)
            spread(l - 1, i, grad * coef[l - 1, rows, :])

        loop(2, finish_image)
    weight_grads(0)

    for i in range(2):
        x_arrive(LAYERS, i)
    for peer in peers:
        came(ghall.at[peer], q_recv.at[peer])
        came(jrecv.at[peer], s_recv.at[peer])
    lhs = [
        jnp.concatenate([ghall[2 * m].reshape(TASKS * HC, 128), ghall[2 * m + 1].reshape(TASKS * HC, 128)], axis=1)
        for m in range(2)
    ]
    for c in range(0, 4, 2):
        total = None
        for m in range(2):
            rows = slice(m * IMG, (m + 1) * IMG)
            rhs = jnp.concatenate([xs[LAYERS, c, rows, :], xs[LAYERS, c + 1, rows, :]], axis=1)
            term = dot(lhs[m], rhs, NN)
            total = term if total is None else total + term
        hg[c * 448 : (c + 1) * 448, :] = total[:, :128]
        hg[(c + 1) * 448 : (c + 2) * 448, :] = total[:, 128:]
    if hg.shape[0] > 1792:
        hg[1792:, :] = jnp.zeros((hg.shape[0] - 1792, 128), F32)
    small[...] = jnp.zeros_like(small)
    for m in range(4):
        small[m * 32 : (m + 1) * 32, :] = jrecv[0, m] + jrecv[1, m] + jrecv[2, m] + jrecv[3, m]
    losses[2 + me] = small[96:104, :]

    def l_copy(i):
        dev = (me + i + 1) % n
        return put(losses.at[2 + me], losses.at[2 + me], l_send.at[i], l_recv.at[me], at(dp=dev))

    def part(dest, k):
        u = inv_ref[dest * slots_per + k]
        return dw[jnp.maximum(u, 0)] * jnp.where(u >= 0, 1.0, 0.0)

    def head_part(dest):
        rows = hg[pl.ds(pl.multiple_of(dest * piece, 16), piece), :]
        return rows, small[pl.ds(pl.multiple_of(dest * SMALL, SMALL), SMALL), :]

    def write(ref, values):
        codes, powers = encode(values)
        ref[0:256, :] = codes
        ref[256:272, :] = powers

    def read(ref):
        return decode(ref[0:256, :], ref[256:272, :])

    def write_head(ref, values):
        codes, powers = encode(values[0])
        ref[0:piece, :] = codes
        ref[piece : piece + 16, :] = powers
        codes, powers = encode(values[1])
        ref[piece + 16 : piece + 32, :] = codes
        ref[piece + 32 : piece + 48, :] = powers

    def read_head(ref):
        one = decode(ref[0:piece, :], ref[piece : piece + 16, :])
        return one, decode(ref[piece + 16 : piece + 32, :], ref[piece + 32 : piece + 48, :])

    def y_copy(zz, k):
        return put(ysend.at[zz, k], yrecv.at[zz, k], y_send.at[zz, k], y_recv.at[zz, k], other)

    def z_right(zz, k):
        return put(lsend.at[zz, k], lleft.at[zz, k], z_send.at[zz, k], zl_recv.at[zz, k], right)

    def z_left(zz, k):
        return put(lsend.at[zz, k], lright.at[zz, k], z_send.at[zz, k], zr_recv.at[zz, k], left)

    def cross(zz):
        dest = zz * 2 + 1 - y

        def block(k):
            write(ysend.at[zz, k], part(dest, k))
            y_copy(zz, k).start()

        loop(first_a, block)
        write_head(ysend.at[zz, first_a], head_part(dest))
        y_copy(zz, first_a).start()

    def pass_on(zz, k):
        @pl.when(zz > z)
        def _():
            z_right(zz, k).start()

        @pl.when(zz < z)
        def _():
            z_left(zz, k).start()

    def line_conv(zz, k):
        is_a, is_own = k < first_a, k < slots_per
        dest = zz * 2 + jnp.where(is_own, y, 1 - y)
        slot = jnp.where(is_own, k, k - last_b)
        zsum[...] = part(dest, slot)

        @pl.when(is_a)
        def _():
            came(yrecv.at[zz, k], y_recv.at[zz, k])
            zsum[...] += read(yrecv.at[zz, k])

        @pl.when((zz >= z) & has_left)
        def _():
            came(lleft.at[zz, k], zl_recv.at[zz, k])
            zsum[...] += read(lleft.at[zz, k])

        @pl.when((zz <= z) & has_right)
        def _():
            came(lright.at[zz, k], zr_recv.at[zz, k])
            zsum[...] += read(lright.at[zz, k])

    def line_head(zz):
        k = cargo - 1
        dest = zz * 2 + y
        rows, few = head_part(dest)
        zsum[0:piece, :] = rows
        zsum[piece : piece + SMALL, :] = few
        came(yrecv.at[zz, first_a], y_recv.at[zz, first_a])

        def add(ref):
            one, two = read_head(ref)
            zsum[0:piece, :] += one
            zsum[piece : piece + SMALL, :] += two

        add(yrecv.at[zz, first_a])

        @pl.when((zz >= z) & has_left)
        def _():
            came(lleft.at[zz, k], zl_recv.at[zz, k])
            add(lleft.at[zz, k])

        @pl.when((zz <= z) & has_right)
        def _():
            came(lright.at[zz, k], zr_recv.at[zz, k])
            add(lright.at[zz, k])

    def head_values():
        return zsum[0:piece, :], zsum[piece : piece + SMALL, :]

    def out_step(d):
        for zz, ok in ((z - d, z - d >= 0), (z + d, z + d < nz)):

            @pl.when(ok)
            def _(zz=zz):
                cross(zz)

        for zz, ok in ((z - d, z - d >= 0), (z + d, z + d < nz)):

            @pl.when(ok)
            def _(zz=zz):
                def block(k):
                    line_conv(zz, k)
                    write(lsend.at[zz, k], zsum[...])
                    pass_on(zz, k)

                loop(cargo - 1, block)
                line_head(zz)
                write_head(lsend.at[zz, cargo - 1], head_values())
                pass_on(zz, cargo - 1)

    loop(nz - 1, lambda i: out_step(nz - 1 - i))
    loop(n - 1, lambda i: l_copy(i).start())
    cross(z)

    def b_copy(k):
        return put(bsend2.at[k], brecv2.at[k], b_send.at[k], b_recv.at[k], other)

    def give_b(k):
        line_conv(z, slots_per + k)
        write(bsend2.at[k], zsum[...])
        b_copy(k).start()

    loop(last_b, give_b)

    line_head(z)
    write_head(hag.at[me], head_values())

    def tag(j):
        return hag.at[j]

    def t_right(j):
        return put(tag(j), tag(j), t_zr.at[j], t_recv.at[j], right)

    def t_left(j):
        return put(tag(j), tag(j), t_zl.at[j], t_recv.at[j], left)

    def t_other(j):
        return put(tag(j), tag(j), t_y.at[j], t_recv.at[j], other)

    @pl.when(has_right)
    def _():
        t_right(me).start()

    @pl.when(has_left)
    def _():
        t_left(me).start()

    t_other(me).start()

    def own_slot(k):
        line_conv(z, k)
        grad_out[k] = zsum[...]

    loop(first_a, own_slot)

    def tail(d):
        @pl.when(z - d - 1 >= 0)
        def _():
            j = (z - d - 1) * 2 + y
            came(tag(j), t_recv.at[j])

            @pl.when(has_right)
            def _():
                t_right(j).start()

            t_other(j).start()

        @pl.when(z + d + 1 < nz)
        def _():
            j = (z + d + 1) * 2 + y
            came(tag(j), t_recv.at[j])

            @pl.when(has_left)
            def _():
                t_left(j).start()

            t_other(j).start()

    loop(nz - 1, tail)

    def own_last(k):
        line_conv(z, first_a + k)
        came(brecv2.at[k], b_recv.at[k])
        grad_out[first_a + k] = zsum[...] + read(brecv2.at[k])

    loop(last_b, own_last)

    loop(n - 1, lambda i: came(losses.at[2 + (me + i + 1) % n], l_recv.at[(me + i + 1) % n]))
    loss_out[...] = lax.fori_loop(0, n, lambda i, acc: acc + losses[2 + i], jnp.zeros((8, 128), F32))

    def other_row(zz):
        j = zz * 2 + 1 - y
        came(tag(j), t_recv.at[j])

    loop(nz, other_row)
    per = 448 // piece

    def unpack(j):
        one, two = read_head(hag.at[j])

        @pl.when(j < 4 * per)
        def _():
            rows = pl.ds(pl.multiple_of((j % per) * piece, 16), piece)
            head_out[rows, pl.ds(pl.multiple_of((j // per) * 128, 128), 128)] = one

        @pl.when(j < 8)
        def _():
            small_out[pl.ds(pl.multiple_of(j * SMALL, SMALL), SMALL), :] = two

    loop(n, unpack)

    def drain_w(s):
        k = s % slots_per
        zz, row = s // (2 * slots_per), (s // slots_per) % 2
        on_line = (row == y) | (k >= first_a)

        @pl.when(on_line & has_right & (zz <= z))
        def _():
            left_it(wall.at[s], w_zr.at[s])

        @pl.when(on_line & has_left & (zz >= z))
        def _():
            left_it(wall.at[s], w_zl.at[s])

        @pl.when((row == y) & ((k < first_a) | (zz == z)))
        def _():
            left_it(wall.at[s], w_y.at[s])

    loop(n * slots_per, drain_w)

    def drain_t(zz):
        j = zz * 2 + y

        @pl.when(has_right & (zz <= z))
        def _():
            left_it(tag(j), t_zr.at[j])

        @pl.when(has_left & (zz >= z))
        def _():
            left_it(tag(j), t_zl.at[j])

        left_it(tag(j), t_y.at[j])

        def y_block(k):
            y_copy(zz, k).wait_send()

        loop(first_a + 1, y_block)

        @pl.when(zz != z)
        def _():
            loop(cargo, lambda k: left_it(lsend.at[zz, k], z_send.at[zz, k]))

    loop(nz, drain_t)
    loop(last_b, lambda k: b_copy(k).wait_send())
    for l in range(LAYERS + 1):
        for i in range(2):
            x_drain(l, i)
    for k in range(3):
        loop(TASKS, lambda t, k=k: h_copy(t, ch, partner, k).wait_send())
        j_copy(ch, partner, k).wait_send()
        a_copy(ch, partner, k).wait_send()
    for k, peer in enumerate(peers):
        f_copy(peer, k).wait_send()
        g_copy(peer, k).wait_send()
        q_copy(peer, k).wait_send()
        s_copy(peer, k).wait_send()
    for l in (1, 2):
        for i in range(2):
            bc_copy(l, i).wait_send()
            bx_copy(l, i).wait_send()
    loop(n - 1, lambda i: c_copy(i).wait_send())
    loop(n - 1, lambda i: l_copy(i).wait_send())


def adamw(weight, gradient, moment_one, moment_two, step_rate, step_count):
    step_float = step_count[0].astype(F32)
    moment_one = beta_one * moment_one + (1.0 - beta_one) * gradient
    moment_two = beta_two * moment_two + (1.0 - beta_two) * gradient * gradient
    first_hat = moment_one / (1.0 - beta_one**step_float)
    second_hat = moment_two / (1.0 - beta_two**step_float)
    weight = weight - step_rate * (
        first_hat / (jnp.sqrt(second_hat) + eps_adam) + decay_rate * weight
    )
    return (weight, moment_one, moment_two)


def per_device(
    n,
    inputs,
    affine,
    image_sizes,
    labels,
    label_mask,
    unit_slots,
    conv_master,
    conv_first,
    conv_second,
    head_master,
    head_first,
    head_second,
    join_master,
    join_first,
    join_second,
    scale_master,
    scale_first,
    scale_second,
    step_count,
):
    slots_per = conv_master.shape[0]
    nz = n // 2
    last_b = slots_per // 7
    first_a = slots_per - last_b
    cargo = slots_per + last_b + 1
    piece = -(-1792 // (n * 16)) * 16
    code = jnp.where(label_mask > 0, labels, -1).reshape(4, 128, TASKS).transpose(0, 2, 1)
    code = jnp.pad(code, ((0, 0), (0, 8 - TASKS), (0, 0)), constant_values=-1)
    units = jnp.arange(unit_slots.shape[0], dtype=jnp.int32)
    holds = unit_slots[None, :] == jnp.arange(n * slots_per, dtype=jnp.int32)[:, None]
    slot_units = jnp.max(jnp.where(holds, units[None, :], -1), axis=1)
    join_pad = jnp.concatenate(
        [
            join_master,
            jnp.zeros((TASKS, HC, 32 - K), F32),
            scale_master[:, :, None],
            jnp.zeros((TASKS, HC, 128 - 33), F32),
        ],
        axis=2,
    )
    affine_pad = jnp.pad(affine.reshape(2 * LAYERS, 128), ((0, 2), (0, 0)))
    vm, dma = pltpu.VMEM, pltpu.SemaphoreType.DMA
    shape = jax.ShapeDtypeStruct
    scratch = [
        vm((n * slots_per, 256, 128), BF16),
        vm((LAYERS + 1, 4, PX, 128), BF16),
        vm((LAYERS, 2, 256, PX), BF16),
        vm((TASKS, 4, HC, C), BF16),
        vm((TASKS, 4, HC, 128), F32),
        vm((4, 8, 128), F32),
        vm((n, 8, 128), F32),
        vm((n + 2, 8, 128), F32),
        vm((PX, 128), F32),
        vm((LAYERS, PX, 128), F32),
        vm((3, IMG, 128), F32),
        vm((4, 128, 128), BF16),
        vm((TASKS, 256, 128), BF16),
        vm((4, TASKS, HC, 128), BF16),
        vm((128, C), F32),
        vm((4, 128, 128), BF16),
        vm((4, 128, 128), BF16),
        vm((8, 32, 256), F32),
        vm((4, 4, 32, 128), F32),
        vm((4, 4, 32, 128), F32),
        vm((27, PX, 128), BF16),
        vm((2, 2, 2, 2, IMG, 128), F32),
        vm((2, 2, 2, IMG, 128), F32),
        vm((2, 2, IMG, 128), F32),
        vm((2, 2, IMG, 128), F32),
        vm((54, 256, 128), F32),
        vm((n * piece, 128), F32),
        vm((n * SMALL, 128), F32),
        vm((nz, first_a + 1, CHUNK, 128), jnp.int16),
        vm((nz, first_a + 1, CHUNK, 128), jnp.int16),
        vm((nz, cargo, CHUNK, 128), jnp.int16),
        vm((nz, cargo, CHUNK, 128), jnp.int16),
        vm((nz, cargo, CHUNK, 128), jnp.int16),
        vm((max(last_b, 1), CHUNK, 128), jnp.int16),
        vm((max(last_b, 1), CHUNK, 128), jnp.int16),
        vm((n, CHUNK, 128), jnp.int16),
        vm((256, 128), F32),
        *[dma((n * slots_per,)) for _ in range(4)],
        *[dma((LAYERS + 1, 2, 3)) for _ in range(2)],
        *[dma((TASKS, 3)) for _ in range(2)],
        *[dma((3,)) for _ in range(4)],
        *[dma((n,)) for _ in range(4)],
        dma((3,)), dma((4,)),
        dma((3,)), dma((4,)),
        dma((3,)), dma((4,)),
        dma((3,)), dma((4,)),
        *[dma((2, 2)) for _ in range(4)],
        *[dma((nz, first_a + 1)) for _ in range(2)],
        *[dma((nz, cargo)) for _ in range(3)],
        *[dma((max(last_b, 1),)) for _ in range(2)],
        *[dma((n,)) for _ in range(4)],
    ]
    in_smem, in_vmem = pl.BlockSpec(memory_space=pltpu.SMEM), pl.BlockSpec(memory_space=pltpu.VMEM)
    slot_grads, head_total, small_total, loss_total = pl.pallas_call(
        functools.partial(kernel, n, slots_per),
        out_shape=(
            shape((slots_per, 256, 128), F32),
            shape((448, C), F32),
            shape((128, 128), F32),
            shape((8, 128), F32),
        ),
        in_specs=[in_smem] * 3 + [in_vmem] * 6,
        out_specs=(in_vmem,) * 4,
        scratch_shapes=scratch,
        compiler_params=pltpu.CompilerParams(
            collective_id=0, has_side_effects=True, vmem_limit_bytes=60 * 2**20
        ),
    )(
        unit_slots,
        slot_units,
        image_sizes,
        inputs.reshape(PX, 128),
        affine_pad,
        code,
        conv_master,
        head_master,
        join_pad,
    )
    pairs = small_total.reshape(4, 32, 2, HC).transpose(0, 2, 1, 3).reshape(8, 32, HC)[:TASKS]
    join_total = pairs[:, :K].transpose(0, 2, 1)
    scale_total = pairs[:, 24]
    head_total = head_total.reshape(TASKS, HC, C)
    conv_out = adamw(conv_master, slot_grads, conv_first, conv_second, 0.01, step_count)
    head_out = adamw(head_master, head_total, head_first, head_second, 0.03, step_count)
    join_out = adamw(join_master, join_total, join_first, join_second, 0.4, step_count)
    scale_out = adamw(scale_master, scale_total, scale_first, scale_second, 0.8, step_count)
    loss = jnp.sum(loss_total[:TASKS, 64])
    return (loss.reshape(1),) + conv_out + head_out + join_out + scale_out


def solution(mesh):
    placed = (
        P("dp", None, None, "chan"),
        P(None, None, "chan"),
        P("dp", None),
        P("dp", None, None, None),
        P("dp", None, None, None),
        P(),
        P("dp", None, "chan"),
        P("dp", None, "chan"),
        P("dp", None, "chan"),
        P(None, "chan", None),
        P(None, "chan", None),
        P(None, "chan", None),
        P(None, "chan", None),
        P(None, "chan", None),
        P(None, "chan", None),
        P(None, "chan"),
        P(None, "chan"),
        P(None, "chan"),
        P(),
    )
    return jax.shard_map(
        functools.partial(per_device, mesh.shape["dp"]),
        mesh=mesh,
        in_specs=placed,
        out_specs=(P(),) + placed[6:18],
        check_vma=False,
    )
```

```python
import functools

import jax
import jax.numpy as jnp
from jax import lax
from jax.experimental import pallas as pl
from jax.experimental.pallas import tpu as pltpu
from jax.sharding import PartitionSpec as P

C = 512
K = 21
TASKS = 7
LAYERS = 3
H = 16
W = 16
PX = 512
IMG = 256
HC = 64
CHUNK = 272
SMALL = 16

beta_one = 0.9
beta_two = 0.999
eps_adam = 1e-08
decay_rate = 0.01
eps_norm = 1e-06

F32 = jnp.float32
BF16 = jnp.bfloat16
MESH = pl.DeviceIdType.MESH
NN = (((1,), (0,)), ((), ()))
NT = (((1,), (1,)), ((), ()))
TN = (((0,), (0,)), ((), ()))


def dot(a, b, dims, precision=None):
    return lax.dot_general(a, b, dims, precision=precision, preferred_element_type=F32)


def encode(values):
    top = jnp.max(jnp.abs(values), axis=0, keepdims=True)
    power = jnp.ceil(jnp.log2(jnp.maximum(top, 1e-30))) - 14.0
    codes = jnp.round(values * jnp.exp2(-power)).astype(jnp.int32).astype(jnp.int16)
    powers = jnp.broadcast_to(power, (16, 128)).astype(jnp.int32).astype(jnp.int16)
    return codes, powers


def decode(codes, powers):
    return codes.astype(F32) * jnp.exp2(powers.astype(F32)[0:1])


def kernel(
    n,
    slots_per,
    slots_ref,
    inv_ref,
    sizes_ref,
    inputs_ref,
    affine_ref,
    code_ref,
    conv_ref,
    head_ref,
    join_ref,
    grad_out,
    head_out,
    small_out,
    loss_out,
    wall,
    xs,
    xt,
    hall,
    jall,
    aall,
    cnt,
    losses,
    mask,
    coef,
    zacc,
    fbuf,
    gh,
    ghall,
    gfeat,
    gsend,
    grecv,
    jt,
    jsend,
    jrecv,
    gs,
    bpart,
    bcore,
    bx,
    bxs,
    dw,
    hg,
    small,
    psend,
    precv,
    ysend,
    yrecv,
    lsend,
    lright,
    lleft,
    bsend2,
    brecv2,
    hag,
    zsum,
    w_recv,
    w_zr,
    w_zl,
    w_y,
    x_send,
    x_recv,
    h_send,
    h_recv,
    j_send,
    j_recv,
    a_send,
    a_recv,
    c_send,
    c_recv,
    l_send,
    l_recv,
    f_send,
    f_recv,
    g_send,
    g_recv,
    q_send,
    q_recv,
    p_send,
    p_recv,
    s_send,
    s_recv,
    bc_send,
    bc_recv,
    bx_send,
    bx_recv,
    y_send,
    y_recv,
    z_send,
    zr_recv,
    zl_recv,
    b_send,
    b_recv,
    t_recv,
    t_zr,
    t_zl,
    t_y,
):
    nz = n // 2
    last_b = slots_per // 7
    first_a = slots_per - last_b
    cargo = slots_per + last_b
    piece = hg.shape[0] // n

    me = lax.axis_index("dp")
    ch = lax.axis_index("chan")
    z, y = me // 2, me % 2
    core = ch % 2
    partner = ch + 1 - 2 * core
    across = (ch + 2) % 4
    far = (partner + 2) % 4

    def at(dp=None, chan=None):
        return {"dp": me if dp is None else dp, "chan": ch if chan is None else chan}

    right, left, other = at(dp=me + 2), at(dp=me - 2), at(dp=z * 2 + 1 - y)
    has_right, has_left = z < nz - 1, z > 0

    def put(src, dst, send, recv, dev):
        return pltpu.make_async_remote_copy(
            src_ref=src, dst_ref=dst, send_sem=send, recv_sem=recv, device_id=dev, device_id_type=MESH
        )

    def came(ref, recv):
        put(ref, ref, recv, recv, other).wait_recv()

    def left_it(ref, send):
        put(ref, ref, send, send, other).wait_send()

    def loop(count, body):
        lax.fori_loop(0, count, lambda i, c: (body(i), c)[1], 0)

    barrier = pltpu.get_barrier_semaphore()

    def greet(i):
        pl.semaphore_signal(barrier, inc=1, device_id=at(dp=(me + i + 1) % n), device_id_type=MESH)

    loop(n - 1, greet)
    for peer in (partner, across, far):
        pl.semaphore_signal(barrier, inc=1, device_id=at(chan=peer), device_id_type=MESH)

    def cast_block(k):
        wall[me * slots_per + k] = conv_ref[k].astype(BF16)

    loop(slots_per, cast_block)
    pixel = lax.broadcasted_iota(jnp.int32, (IMG, 128), 0)
    row_id, col_id = pixel // W, pixel % W

    def mask_image(i):
        inside = (row_id < sizes_ref[i, 0]) & (col_id < sizes_ref[i, 1])
        rows = pl.ds(pl.multiple_of(i * IMG, IMG), IMG)
        mask[rows, :] = jnp.where(inside, 1.0, 0.0)
        xs[0, ch, rows, :] = (inputs_ref[rows, :].astype(F32) * mask[rows, :]).astype(BF16)

    loop(2, mask_image)

    def cast_head(t):
        hall[t, ch] = head_ref[t].astype(BF16)
        jall[t, ch] = join_ref[t]

    loop(TASKS, cast_head)
    aall[ch] = affine_ref[...]

    lane = lax.broadcasted_iota(jnp.int32, (8, 128), 1)

    def kept(q):
        spot = (q % 2) * 128 + lane
        hit = (spot // W < sizes_ref[q // 2, 0]) & (spot % W < sizes_ref[q // 2, 1])
        return jnp.where(hit & (code_ref[q] >= 0), 1.0, 0.0)

    total_kept = kept(0) + kept(1) + kept(2) + kept(3)
    cnt[me] = jnp.broadcast_to(jnp.sum(total_kept, axis=1, keepdims=True), (8, 128))

    pl.semaphore_wait(barrier, n - 1 + 3)

    def to_right(s):
        return put(wall.at[s], wall.at[s], w_zr.at[s], w_recv.at[s], right)

    def to_left(s):
        return put(wall.at[s], wall.at[s], w_zl.at[s], w_recv.at[s], left)

    def to_other(s):
        return put(wall.at[s], wall.at[s], w_y.at[s], w_recv.at[s], other)

    def both_ways(s):
        @pl.when(has_right)
        def _():
            to_right(s).start()

        @pl.when(has_left)
        def _():
            to_left(s).start()

    def x_copy(l, i, owner, peer, k):
        rows = pl.ds(pl.multiple_of(i * IMG, IMG), IMG)
        ref = xs.at[l, owner, rows, :]
        return put(ref, ref, x_send.at[l, i, k], x_recv.at[l, i, k], at(chan=peer))

    def x_start(l, i):
        x_copy(l, i, ch, across, 0).start()
        x_copy(l, i, ch, partner, 1).start()

    def x_relay(l, i):
        x_copy(l, i, across, across, 0).wait_recv()
        x_copy(l, i, across, partner, 2).start()

    def x_arrive(l, i):
        x_copy(l, i, partner, partner, 1).wait_recv()
        x_copy(l, i, far, partner, 2).wait_recv()

    def x_drain(l, i):
        for k in range(3):
            x_copy(l, i, ch, partner, k).wait_send()

    def h_copy(t, owner, peer, k):
        ref = hall.at[t, owner]
        return put(ref, ref, h_send.at[t, k], h_recv.at[t, k], at(chan=peer))

    def j_copy(owner, peer, k):
        ref = jall.at[:, owner]
        return put(ref, ref, j_send.at[k], j_recv.at[k], at(chan=peer))

    def a_copy(owner, peer, k):
        ref = aall.at[owner]
        return put(ref, ref, a_send.at[k], a_recv.at[k], at(chan=peer))

    def c_copy(i):
        dev = (me + i + 1) % n
        return put(cnt.at[me], cnt.at[me], c_send.at[i], c_recv.at[me], at(dp=dev))

    base = me * slots_per

    def own_b(k):
        to_other(base + first_a + k).start()

    loop(last_b, own_b)

    def own_a(k):
        both_ways(base + k)
        to_other(base + k).start()

    loop(first_a, own_a)
    for i in range(2):
        x_start(0, i)

    def own_head(t):
        h_copy(t, ch, across, 0).start()
        h_copy(t, ch, partner, 1).start()

    loop(TASKS, own_head)
    loop(last_b, lambda k: both_ways(base + first_a + k))
    for copy in (j_copy, a_copy):
        copy(ch, across, 0).start()
        copy(ch, partner, 1).start()
    loop(n - 1, lambda i: c_copy(i).start())

    neighbour = (z * 2 + 1 - y) * slots_per

    def pass_b(k):
        s = neighbour + first_a + k
        came(wall.at[s], w_recv.at[s])
        both_ways(s)

    loop(last_b, pass_b)
    for i in range(2):
        x_relay(0, i)

    def relay_head(t):
        h_copy(t, across, across, 0).wait_recv()
        h_copy(t, across, partner, 2).start()

    def line_in(d, c):
        def source(zz):
            row = jnp.where(c < slots_per, y, 1 - y)
            return (zz * 2 + row) * slots_per + jnp.where(c < slots_per, c, c - last_b)

        @pl.when(z - d >= 0)
        def _():
            s = source(z - d)
            came(wall.at[s], w_recv.at[s])

            @pl.when(has_right)
            def _():
                to_right(s).start()

            @pl.when(c < first_a)
            def _():
                to_other(s).start()

        @pl.when(z + d < nz)
        def _():
            s = source(z + d)
            came(wall.at[s], w_recv.at[s])

            @pl.when(has_left)
            def _():
                to_left(s).start()

            @pl.when(c < first_a)
            def _():
                to_other(s).start()

    def first_step(c):
        pl.when(c < slots_per + last_b)(lambda: line_in(1, c))
        pl.when(c < TASKS)(lambda: relay_head(c))

    loop(max(slots_per + last_b, TASKS), first_step)
    for copy in (j_copy, a_copy):
        copy(across, across, 0).wait_recv()
        copy(across, partner, 2).start()

    def transpose_layer(l):
        for c in range(4):
            xt[l, c // 2, (c % 2) * 128 : (c % 2) * 128 + 128, :] = xs[l, c].T

    for i in range(2):
        x_arrive(0, i)
    transpose_layer(0)

    loop(nz - 2, lambda d: loop(slots_per + last_b, lambda c: line_in(d + 2, c)))

    def last_in(zz):
        def block(k):
            s = (zz * 2 + 1 - y) * slots_per + k
            came(wall.at[s], w_recv.at[s])

        loop(first_a, block)

    loop(nz, last_in)

    def conv_forward(l, i):
        rows = pl.ds(pl.multiple_of(i * IMG, IMG), IMG)
        left_side = jnp.concatenate([xs[l, c, rows, :] for c in range(4)], axis=1)
        zacc[...] = jnp.zeros_like(zacc)
        for first in range(0, 9, 2):
            taps = [t for t in (first, first + 1) if t < 9]
            sides = [
                jnp.concatenate([wall[slots_ref[(l * 9 + t) * 2 + h]] for h in range(2)], axis=0)
                for t in taps
            ]
            side = jnp.concatenate(sides, axis=1) if len(sides) > 1 else sides[0]
            out = dot(left_side, side, NN)
            for k, t in enumerate(taps):
                a, e = divmod(t, 3)
                part = out[:, k * 128 : (k + 1) * 128]
                if a == 0:
                    zacc[e, W:IMG, :] += part[: IMG - W]
                elif a == 1:
                    zacc[e] += part
                else:
                    zacc[e, : IMG - W, :] += part[W:]
        linear = zacc[1]
        linear += jnp.where(col_id >= 1, pltpu.roll(zacc[0], 1, 0), 0.0)
        linear += jnp.where(col_id < W - 1, pltpu.roll(zacc[2], IMG - 1, 0), 0.0)
        inside = mask[rows, :]
        gain, shift = affine_ref[2 * l : 2 * l + 1, :], affine_ref[2 * l + 1 : 2 * l + 2, :]
        passed = jnp.where(linear > 0, inside, 0.0)
        coef[l, rows, :] = passed * gain if l < LAYERS - 1 else passed
        out = (jnp.maximum(linear, 0.0) * gain + shift) * inside
        xs[l + 1, ch, rows, :] = out.astype(BF16)

    def quarter(q):
        return pl.ds(pl.multiple_of(q * 128, 128), 128)

    for l in range(LAYERS):

        def forward_image(i, l=l):
            if l > 0:
                x_relay(l, i)
                x_arrive(l, i)
            conv_forward(l, i)
            if l < LAYERS - 1:
                x_start(l + 1, i)

        loop(2, forward_image)
        if 0 < l:
            transpose_layer(l)

    def f_copy(peer, k):
        return put(xs.at[LAYERS, ch, quarter(peer), :], fbuf.at[ch], f_send.at[k], f_recv.at[ch], at(chan=peer))

    peers = (across, far, partner)
    for k, peer in enumerate(peers):
        f_copy(peer, k).start()
    for i in range(2):
        x_start(LAYERS, i)
    fbuf[ch] = xs[LAYERS, ch, quarter(ch), :]

    loop(n - 1, lambda i: came(cnt.at[(me + i + 1) % n], c_recv.at[(me + i + 1) % n]))
    counts = lax.fori_loop(0, n, lambda i, acc: acc + cnt[i], jnp.zeros((8, 128), F32))
    counts = jnp.maximum(counts, 1.0)

    def head_in(t):
        h_copy(t, partner, partner, 1).wait_recv()
        h_copy(t, far, partner, 2).wait_recv()

    loop(TASKS, head_in)
    for copy in (j_copy, a_copy):
        copy(partner, partner, 1).wait_recv()
        copy(far, partner, 2).wait_recv()
    for peer in peers:
        came(fbuf.at[peer], f_recv.at[peer])

    weight = kept(ch) / counts
    losses[0] = weight
    losses[1] = jnp.zeros((8, 128), F32)
    features = jnp.concatenate([fbuf[c] for c in range(4)], axis=1)
    gfeat[...] = jnp.zeros_like(gfeat)
    klass = lax.broadcasted_iota(jnp.int32, (32, 128), 0)

    def q_copy(t, peer, k):
        rows = pl.ds(pl.multiple_of(peer * HC, HC), HC)
        return put(gh.at[t, rows, :], ghall.at[ch, t], q_send.at[t, k], q_recv.at[t, ch], at(chan=peer))

    def head_task(t):
        low = hall[t].reshape(4 * HC, C)
        both = jall[t].reshape(4 * HC, 128)
        join = both.astype(BF16)
        scale = both[:, 32:33]
        hidden = dot(low, features, NT)
        inverse = lax.rsqrt(jnp.sum(hidden * hidden, axis=0, keepdims=True) + eps_norm)
        normed = hidden * inverse
        scaled = (scale * normed).astype(BF16)
        logits = dot(join, scaled, TN)[0:32]
        real = klass < K
        largest = jnp.max(jnp.where(real, logits, -jnp.inf), axis=0, keepdims=True)
        shifted = jnp.where(real, jnp.exp(jnp.where(real, logits - largest, 0.0)), 0.0)
        totals = jnp.sum(shifted, axis=0, keepdims=True)
        onehot = klass == code_ref[ch, pl.ds(t, 1), :]
        picked = jnp.sum(jnp.where(onehot, logits, 0.0), axis=0, keepdims=True)
        share = losses[0, pl.ds(t, 1), :]
        losses[1, pl.ds(t, 1), :] = share * (largest + jnp.log(totals) - picked)
        slope = (share * (shifted / totals - jnp.where(onehot, 1.0, 0.0))).astype(BF16)
        grad_scaled = dot(join, jnp.concatenate([slope, jnp.zeros((96, 128), BF16)], axis=0), NN)
        jt[t, 0:24, :] = dot(slope, scaled, NT)[0:24]
        jt[t, 24:32, :] = dot(jnp.ones((8, 128), F32), grad_scaled * normed, NT, lax.Precision.HIGHEST)
        grad_normed = grad_scaled * scale
        along = jnp.sum(normed * grad_normed, axis=0, keepdims=True)
        grad_hidden = ((grad_normed - normed * along) * inverse).astype(BF16)
        gh[t] = grad_hidden
        for k, peer in enumerate(peers):
            q_copy(t, peer, k).start()
        gfeat[...] += dot(grad_hidden, low, TN)

    loop(TASKS, head_task)
    loss_tile = jnp.broadcast_to(jnp.sum(losses[1], axis=1, keepdims=True), (8, 128))
    jt[TASKS, 0:8, 0:128] = loss_tile
    jt[TASKS, 0:8, 128:256] = loss_tile

    my_mask = mask[quarter(ch), :]
    for c in range(4):
        gsend[c] = (gfeat[:, c * 128 : (c + 1) * 128] * my_mask * aall[c, 4:5, :]).astype(BF16)

    def g_copy(peer, k):
        return put(gsend.at[peer], grecv.at[ch], g_send.at[k], g_recv.at[ch], at(chan=peer))

    def s_copy(peer, k):
        return put(jsend.at[peer], jrecv.at[ch], s_send.at[k], s_recv.at[ch], at(chan=peer))

    for k, peer in enumerate(peers):
        g_copy(peer, k).start()
    for i in range(2):
        x_relay(LAYERS, i)
    grecv[ch] = gsend[ch]
    low_lane = lax.broadcasted_iota(jnp.int32, (32, 128), 1) < HC
    for c in range(4):
        side = slice((c // 2) * 128, (c // 2) * 128 + 128)
        for m in range(4):
            one, two = jt[2 * m, :, side], jt[2 * m + 1, :, side]
            if m == 3:
                two = jnp.where(lax.broadcasted_iota(jnp.int32, (32, 128), 0) < 8, two, 0.0)
            if c % 2 == 0:
                two = pltpu.roll(two, HC, 1)
            else:
                one = pltpu.roll(one, HC, 1)
            jsend[c, m] = jnp.where(low_lane, one, two)
    for k, peer in enumerate(peers):
        s_copy(peer, k).start()
    ghall[ch] = gh[:, pl.ds(pl.multiple_of(ch * HC, HC), HC), :]
    jrecv[ch] = jsend[ch]

    def spread(l, i, grad):
        columns = (
            jnp.where(col_id < W - 1, pltpu.roll(grad, IMG - 1, 0), 0.0),
            grad,
            jnp.where(col_id >= 1, pltpu.roll(grad, 1, 0), 0.0),
        )
        top = pl.multiple_of(i * IMG, IMG)
        blank = jnp.zeros((W, 128), BF16)
        for e in range(3):
            low = columns[e].astype(BF16)
            gs[l * 9 + e, pl.ds(top, IMG - W), :] = low[W:]
            gs[l * 9 + e, pl.ds(top + IMG - W, W), :] = blank
            gs[l * 9 + 3 + e, pl.ds(top, IMG), :] = low
            gs[l * 9 + 6 + e, pl.ds(top + W, IMG - W), :] = low[: IMG - W]
            gs[l * 9 + 6 + e, pl.ds(top, W), :] = blank

    def conv_backward(l, i):
        rows = pl.ds(pl.multiple_of(i * IMG, IMG), IMG)
        lefts = []
        for first in range(0, 9, 2):
            taps = [t for t in (first, first + 1) if t < 9]
            sides = [gs[l * 9 + t, rows, :] for t in taps]
            lefts.append(jnp.concatenate(sides, axis=1) if len(sides) > 1 else sides[0])
        for h in range(2):
            total = None
            for first in range(0, 9, 2):
                taps = [t for t in (first, first + 1) if t < 9]
                sides = [wall[slots_ref[(l * 9 + t) * 2 + h]] for t in taps]
                side = jnp.concatenate(sides, axis=1) if len(sides) > 1 else sides[0]
                term = dot(lefts[first // 2], side, NT)
                total = term if total is None else total + term
            bpart[l - 1, i, h, 0] = total[:, :128]
            bpart[l - 1, i, h, 1] = total[:, 128:]

    def bc_copy(l, i):
        return put(
            bpart.at[l - 1, i, :, 1 - core],
            bcore.at[l - 1, i],
            bc_send.at[l - 1, i],
            bc_recv.at[l - 1, i],
            at(chan=partner),
        )

    def bx_copy(l, i):
        return put(bxs.at[l - 1, i], bx.at[l - 1, i], bx_send.at[l - 1, i], bx_recv.at[l - 1, i], at(chan=across))

    def weight_grads(l):
        def half(h):
            lhs = xt[l, h]

            def pair(p):
                t = 2 * p
                rhs = jnp.concatenate([gs[l * 9 + t], gs[l * 9 + t + 1]], axis=1)
                out = dot(lhs, rhs, NN)
                dw[(l * 9 + t) * 2 + h] = out[:, :128]
                dw[(l * 9 + t + 1) * 2 + h] = out[:, 128:]

            loop(4, pair)
            dw[(l * 9 + 8) * 2 + h] = dot(lhs, gs[l * 9 + 8], NN)

        loop(2, half)

    def l_copy(i):
        dev = (me + i + 1) % n
        return put(losses.at[2 + me], losses.at[2 + me], l_send.at[i], l_recv.at[me], at(dp=dev))

    def head_part(dest):
        rows = hg[pl.ds(pl.multiple_of(dest * piece, 16), piece), :]
        return rows, small[pl.ds(pl.multiple_of(dest * SMALL, SMALL), SMALL), :]

    def write(ref, values):
        codes, powers = encode(values)
        ref[0:256, :] = codes
        ref[256:272, :] = powers

    def read(ref):
        return decode(ref[0:256, :], ref[256:272, :])

    def write_head(ref, values):
        codes, powers = encode(values[0])
        ref[0:piece, :] = codes
        ref[piece : piece + 16, :] = powers
        codes, powers = encode(values[1])
        ref[piece + 16 : piece + 32, :] = codes
        ref[piece + 32 : piece + 48, :] = powers

    def read_head(ref):
        one = decode(ref[0:piece, :], ref[piece : piece + 16, :])
        return one, decode(ref[piece + 16 : piece + 32, :], ref[piece + 32 : piece + 48, :])

    def p_copy(i):
        dest = (me + i + 1) % n
        return put(psend.at[dest], precv.at[me], p_send.at[i], p_recv.at[me], at(dp=dest))

    def head_grads():
        for i in range(2):
            x_arrive(LAYERS, i)
        for peer in peers:
            loop(TASKS, lambda t, peer=peer: came(ghall.at[peer, t], q_recv.at[t, peer]))
            came(jrecv.at[peer], s_recv.at[peer])
        lhs = [
            jnp.concatenate([ghall[2 * m].reshape(TASKS * HC, 128), ghall[2 * m + 1].reshape(TASKS * HC, 128)], axis=1)
            for m in range(2)
        ]
        for c in range(0, 4, 2):
            total = None
            for m in range(2):
                rows = slice(m * IMG, (m + 1) * IMG)
                rhs = jnp.concatenate([xs[LAYERS, c, rows, :], xs[LAYERS, c + 1, rows, :]], axis=1)
                term = dot(lhs[m], rhs, NN)
                total = term if total is None else total + term
            hg[c * 448 : (c + 1) * 448, :] = total[:, :128]
            hg[(c + 1) * 448 : (c + 2) * 448, :] = total[:, 128:]
        if hg.shape[0] > 1792:
            hg[1792:, :] = jnp.zeros((hg.shape[0] - 1792, 128), F32)
        small[...] = jnp.zeros_like(small)
        for m in range(4):
            small[m * 32 : (m + 1) * 32, :] = jrecv[0, m] + jrecv[1, m] + jrecv[2, m] + jrecv[3, m]
        losses[2 + me] = small[96:104, :]


        def give(i):
            dest = (me + i + 1) % n
            write_head(psend.at[dest], head_part(dest))
            p_copy(i).start()

        loop(n - 1, give)
        loop(n - 1, lambda i: l_copy(i).start())

    for peer in peers:
        came(grecv.at[peer], g_recv.at[peer])

    def top_grad(i):
        rows = pl.ds(pl.multiple_of(i * IMG, IMG), IMG)
        grad = jnp.concatenate([grecv[2 * i], grecv[2 * i + 1]], axis=0).astype(F32)
        spread(LAYERS - 1, i, grad * coef[LAYERS - 1, rows, :])

    loop(2, top_grad)
    x_side = ch // 2
    for l in (2, 1):

        def partial_image(i, l=l):
            conv_backward(l, i)
            bc_copy(l, i).start()

        loop(2, partial_image)

        def chip_sum(i, l=l):
            bc_copy(l, i).wait_recv()
            bxs[l - 1, i] = (bpart[l - 1, i, 1 - x_side, core] + bcore[l - 1, i, 1 - x_side]).astype(BF16)
            bx_copy(l, i).start()

        loop(2, chip_sum)
        if l == LAYERS - 1:
            head_grads()
        weight_grads(l)

        def finish_image(i, l=l):
            bx_copy(l, i).wait_recv()
            grad = bpart[l - 1, i, x_side, core] + bcore[l - 1, i, x_side] + bx[l - 1, i].astype(F32)
            rows = pl.ds(pl.multiple_of(i * IMG, IMG), IMG)
            spread(l - 1, i, grad * coef[l - 1, rows, :])

        loop(2, finish_image)
    weight_grads(0)

    def part(dest, k):
        u = inv_ref[dest * slots_per + k]
        return dw[jnp.maximum(u, 0)] * jnp.where(u >= 0, 1.0, 0.0)

    def y_copy(zz, k):
        return put(ysend.at[zz, k], yrecv.at[zz, k], y_send.at[zz, k], y_recv.at[zz, k], other)

    def z_right(zz, k):
        return put(lsend.at[zz, k], lleft.at[zz, k], z_send.at[zz, k], zl_recv.at[zz, k], right)

    def z_left(zz, k):
        return put(lsend.at[zz, k], lright.at[zz, k], z_send.at[zz, k], zr_recv.at[zz, k], left)

    def both_sides(d, body):
        for zz, ok in ((z - d, z - d >= 0), (z + d, z + d < nz)):

            @pl.when(ok)
            def _(zz=zz):
                body(zz)

    def cross(zz):
        dest = zz * 2 + 1 - y

        def block(k):
            write(ysend.at[zz, k], part(dest, k))
            y_copy(zz, k).start()

        loop(first_a, block)

    def pass_on(zz, k):
        @pl.when(zz > z)
        def _():
            z_right(zz, k).start()

        @pl.when(zz < z)
        def _():
            z_left(zz, k).start()

    def line_conv(zz, k):
        is_a, is_own = k < first_a, k < slots_per
        dest = zz * 2 + jnp.where(is_own, y, 1 - y)
        slot = jnp.where(is_own, k, k - last_b)
        zsum[...] = part(dest, slot)

        @pl.when(is_a)
        def _():
            came(yrecv.at[zz, k], y_recv.at[zz, k])
            zsum[...] += read(yrecv.at[zz, k])

        @pl.when((zz >= z) & has_left)
        def _():
            came(lleft.at[zz, k], zl_recv.at[zz, k])
            zsum[...] += read(lleft.at[zz, k])

        @pl.when((zz <= z) & has_right)
        def _():
            came(lright.at[zz, k], zr_recv.at[zz, k])
            zsum[...] += read(lright.at[zz, k])

    loop(nz - 1, lambda i: both_sides(nz - 1 - i, cross))
    cross(z)

    def tag(j):
        return hag.at[j]

    def t_right(j):
        return put(tag(j), tag(j), t_zr.at[j], t_recv.at[j], right)

    def t_left(j):
        return put(tag(j), tag(j), t_zl.at[j], t_recv.at[j], left)

    def t_other(j):
        return put(tag(j), tag(j), t_y.at[j], t_recv.at[j], other)

    rows, few = head_part(me)
    zsum[0:piece, :] = rows
    zsum[piece : piece + SMALL, :] = few

    def add_piece(i):
        source = (me + i + 1) % n
        came(precv.at[source], p_recv.at[source])
        one, two = read_head(precv.at[source])
        zsum[0:piece, :] += one
        zsum[piece : piece + SMALL, :] += two

    loop(n - 1, add_piece)
    write_head(hag.at[me], (zsum[0:piece, :], zsum[piece : piece + SMALL, :]))

    @pl.when(has_right)
    def _():
        t_right(me).start()

    @pl.when(has_left)
    def _():
        t_left(me).start()

    t_other(me).start()

    def tail(d):
        @pl.when(z - d >= 0)
        def _():
            j = (z - d) * 2 + y
            came(tag(j), t_recv.at[j])

            @pl.when(has_right)
            def _():
                t_right(j).start()

            t_other(j).start()

        @pl.when(z + d < nz)
        def _():
            j = (z + d) * 2 + y
            came(tag(j), t_recv.at[j])

            @pl.when(has_left)
            def _():
                t_left(j).start()

            t_other(j).start()

    def out_step(i):
        d = nz - 1 - i

        def item(c):
            k = (c + first_a) % cargo

            def send(zz):
                line_conv(zz, k)
                write(lsend.at[zz, k], zsum[...])
                pass_on(zz, k)

            both_sides(d, send)

        loop(cargo, item)
        tail(i + 1)

    loop(nz - 1, out_step)

    def b_copy(k):
        return put(bsend2.at[k], brecv2.at[k], b_send.at[k], b_recv.at[k], other)

    def give_b(k):
        line_conv(z, slots_per + k)
        write(bsend2.at[k], zsum[...])
        b_copy(k).start()

    loop(last_b, give_b)

    def own_slot(k):
        line_conv(z, k)
        grad_out[k] = zsum[...]

    loop(first_a, own_slot)

    loop(n - 1, lambda i: came(losses.at[2 + (me + i + 1) % n], l_recv.at[(me + i + 1) % n]))
    loss_out[...] = lax.fori_loop(0, n, lambda i, acc: acc + losses[2 + i], jnp.zeros((8, 128), F32))

    def other_row(zz):
        j = zz * 2 + 1 - y
        came(tag(j), t_recv.at[j])

    loop(nz, other_row)
    per = 448 // piece

    def unpack(j):
        one, two = read_head(hag.at[j])

        @pl.when(j < 4 * per)
        def _():
            rows = pl.ds(pl.multiple_of((j % per) * piece, 16), piece)
            head_out[rows, pl.ds(pl.multiple_of((j // per) * 128, 128), 128)] = one

        @pl.when(j < 8)
        def _():
            small_out[pl.ds(pl.multiple_of(j * SMALL, SMALL), SMALL), :] = two

    loop(n, unpack)

    def own_last(k):
        line_conv(z, first_a + k)
        came(brecv2.at[k], b_recv.at[k])
        grad_out[first_a + k] = zsum[...] + read(brecv2.at[k])

    loop(last_b, own_last)

    def drain_w(s):
        k = s % slots_per
        zz, row = s // (2 * slots_per), (s // slots_per) % 2
        on_line = (row == y) | (k >= first_a)

        @pl.when(on_line & has_right & (zz <= z))
        def _():
            left_it(wall.at[s], w_zr.at[s])

        @pl.when(on_line & has_left & (zz >= z))
        def _():
            left_it(wall.at[s], w_zl.at[s])

        @pl.when((row == y) & ((k < first_a) | (zz == z)))
        def _():
            left_it(wall.at[s], w_y.at[s])

    loop(n * slots_per, drain_w)

    def drain_t(zz):
        j = zz * 2 + y

        @pl.when(has_right & (zz <= z))
        def _():
            left_it(tag(j), t_zr.at[j])

        @pl.when(has_left & (zz >= z))
        def _():
            left_it(tag(j), t_zl.at[j])

        left_it(tag(j), t_y.at[j])

        def y_block(k):
            y_copy(zz, k).wait_send()

        loop(first_a, y_block)

        @pl.when(zz != z)
        def _():
            loop(cargo, lambda k: left_it(lsend.at[zz, k], z_send.at[zz, k]))

    loop(nz, drain_t)
    loop(last_b, lambda k: b_copy(k).wait_send())
    for l in range(LAYERS + 1):
        for i in range(2):
            x_drain(l, i)
    for k in range(3):
        loop(TASKS, lambda t, k=k: h_copy(t, ch, partner, k).wait_send())
        j_copy(ch, partner, k).wait_send()
        a_copy(ch, partner, k).wait_send()
    for k, peer in enumerate(peers):
        f_copy(peer, k).wait_send()
        g_copy(peer, k).wait_send()
        loop(TASKS, lambda t, k=k, peer=peer: q_copy(t, peer, k).wait_send())
        s_copy(peer, k).wait_send()
    for l in (1, 2):
        for i in range(2):
            bc_copy(l, i).wait_send()
            bx_copy(l, i).wait_send()
    loop(n - 1, lambda i: c_copy(i).wait_send())
    loop(n - 1, lambda i: l_copy(i).wait_send())
    loop(n - 1, lambda i: p_copy(i).wait_send())


def adamw(weight, gradient, moment_one, moment_two, step_rate, step_count):
    step_float = step_count[0].astype(F32)
    moment_one = beta_one * moment_one + (1.0 - beta_one) * gradient
    moment_two = beta_two * moment_two + (1.0 - beta_two) * gradient * gradient
    first_hat = moment_one / (1.0 - beta_one**step_float)
    second_hat = moment_two / (1.0 - beta_two**step_float)
    weight = weight - step_rate * (
        first_hat / (jnp.sqrt(second_hat) + eps_adam) + decay_rate * weight
    )
    return (weight, moment_one, moment_two)


def per_device(
    n,
    inputs,
    affine,
    image_sizes,
    labels,
    label_mask,
    unit_slots,
    conv_master,
    conv_first,
    conv_second,
    head_master,
    head_first,
    head_second,
    join_master,
    join_first,
    join_second,
    scale_master,
    scale_first,
    scale_second,
    step_count,
):
    slots_per = conv_master.shape[0]
    nz = n // 2
    last_b = slots_per // 7
    first_a = slots_per - last_b
    cargo = slots_per + last_b
    piece = -(-1792 // (n * 16)) * 16
    code = jnp.where(label_mask > 0, labels, -1).reshape(4, 128, TASKS).transpose(0, 2, 1)
    code = jnp.pad(code, ((0, 0), (0, 8 - TASKS), (0, 0)), constant_values=-1)
    units = jnp.arange(unit_slots.shape[0], dtype=jnp.int32)
    holds = unit_slots[None, :] == jnp.arange(n * slots_per, dtype=jnp.int32)[:, None]
    slot_units = jnp.max(jnp.where(holds, units[None, :], -1), axis=1)
    join_pad = jnp.concatenate(
        [
            join_master,
            jnp.zeros((TASKS, HC, 32 - K), F32),
            scale_master[:, :, None],
            jnp.zeros((TASKS, HC, 128 - 33), F32),
        ],
        axis=2,
    )
    affine_pad = jnp.pad(affine.reshape(2 * LAYERS, 128), ((0, 2), (0, 0)))
    vm, dma = pltpu.VMEM, pltpu.SemaphoreType.DMA
    shape = jax.ShapeDtypeStruct
    scratch = [
        vm((n * slots_per, 256, 128), BF16),
        vm((LAYERS + 1, 4, PX, 128), BF16),
        vm((LAYERS, 2, 256, PX), BF16),
        vm((TASKS, 4, HC, C), BF16),
        vm((TASKS, 4, HC, 128), F32),
        vm((4, 8, 128), F32),
        vm((n, 8, 128), F32),
        vm((n + 2, 8, 128), F32),
        vm((PX, 128), F32),
        vm((LAYERS, PX, 128), F32),
        vm((3, IMG, 128), F32),
        vm((4, 128, 128), BF16),
        vm((TASKS, 256, 128), BF16),
        vm((4, TASKS, HC, 128), BF16),
        vm((128, C), F32),
        vm((4, 128, 128), BF16),
        vm((4, 128, 128), BF16),
        vm((8, 32, 256), F32),
        vm((4, 4, 32, 128), F32),
        vm((4, 4, 32, 128), F32),
        vm((27, PX, 128), BF16),
        vm((2, 2, 2, 2, IMG, 128), F32),
        vm((2, 2, 2, IMG, 128), F32),
        vm((2, 2, IMG, 128), BF16),
        vm((2, 2, IMG, 128), BF16),
        vm((54, 256, 128), F32),
        vm((n * piece, 128), F32),
        vm((n * SMALL, 128), F32),
        vm((n, piece + 48, 128), jnp.int16),
        vm((n, piece + 48, 128), jnp.int16),
        vm((nz, first_a, CHUNK, 128), jnp.int16),
        vm((nz, first_a, CHUNK, 128), jnp.int16),
        vm((nz, cargo, CHUNK, 128), jnp.int16),
        vm((nz, cargo, CHUNK, 128), jnp.int16),
        vm((nz, cargo, CHUNK, 128), jnp.int16),
        vm((max(last_b, 1), CHUNK, 128), jnp.int16),
        vm((max(last_b, 1), CHUNK, 128), jnp.int16),
        vm((n, piece + 48, 128), jnp.int16),
        vm((256, 128), F32),
        *[dma((n * slots_per,)) for _ in range(4)],
        *[dma((LAYERS + 1, 2, 3)) for _ in range(2)],
        *[dma((TASKS, 3)) for _ in range(2)],
        *[dma((3,)) for _ in range(4)],
        *[dma((n,)) for _ in range(4)],
        dma((3,)), dma((4,)),
        dma((3,)), dma((4,)),
        *[dma((TASKS, k)) for k in (3, 4)],
        *[dma((n,)) for _ in range(2)],
        dma((3,)), dma((4,)),
        *[dma((2, 2)) for _ in range(4)],
        *[dma((nz, first_a)) for _ in range(2)],
        *[dma((nz, cargo)) for _ in range(3)],
        *[dma((max(last_b, 1),)) for _ in range(2)],
        *[dma((n,)) for _ in range(4)],
    ]
    in_smem, in_vmem = pl.BlockSpec(memory_space=pltpu.SMEM), pl.BlockSpec(memory_space=pltpu.VMEM)
    slot_grads, head_total, small_total, loss_total = pl.pallas_call(
        functools.partial(kernel, n, slots_per),
        out_shape=(
            shape((slots_per, 256, 128), F32),
            shape((448, C), F32),
            shape((128, 128), F32),
            shape((8, 128), F32),
        ),
        in_specs=[in_smem] * 3 + [in_vmem] * 6,
        out_specs=(in_vmem,) * 4,
        scratch_shapes=scratch,
        compiler_params=pltpu.CompilerParams(
            collective_id=0, has_side_effects=True, vmem_limit_bytes=60 * 2**20
        ),
    )(
        unit_slots,
        slot_units,
        image_sizes,
        inputs.reshape(PX, 128),
        affine_pad,
        code,
        conv_master,
        head_master,
        join_pad,
    )
    pairs = small_total.reshape(4, 32, 2, HC).transpose(0, 2, 1, 3).reshape(8, 32, HC)[:TASKS]
    join_total = pairs[:, :K].transpose(0, 2, 1)
    scale_total = pairs[:, 24]
    head_total = head_total.reshape(TASKS, HC, C)
    conv_out = adamw(conv_master, slot_grads, conv_first, conv_second, 0.01, step_count)
    head_out = adamw(head_master, head_total, head_first, head_second, 0.03, step_count)
    join_out = adamw(join_master, join_total, join_first, join_second, 0.4, step_count)
    scale_out = adamw(scale_master, scale_total, scale_first, scale_second, 0.8, step_count)
    loss = jnp.sum(loss_total[:TASKS, 64])
    return (loss.reshape(1),) + conv_out + head_out + join_out + scale_out


def solution(mesh):
    placed = (
        P("dp", None, None, "chan"),
        P(None, None, "chan"),
        P("dp", None),
        P("dp", None, None, None),
        P("dp", None, None, None),
        P(),
        P("dp", None, "chan"),
        P("dp", None, "chan"),
        P("dp", None, "chan"),
        P(None, "chan", None),
        P(None, "chan", None),
        P(None, "chan", None),
        P(None, "chan", None),
        P(None, "chan", None),
        P(None, "chan", None),
        P(None, "chan"),
        P(None, "chan"),
        P(None, "chan"),
        P(),
    )
    return jax.shard_map(
        functools.partial(per_device, mesh.shape["dp"]),
        mesh=mesh,
        in_specs=placed,
        out_specs=(P(),) + placed[6:18],
        check_vma=False,
    )
```

```python
import functools

import jax
import jax.numpy as jnp
from jax import lax
from jax.experimental import pallas as pl
from jax.experimental.pallas import tpu as pltpu
from jax.sharding import PartitionSpec as P

C = 512
K = 21
TASKS = 7
LAYERS = 3
H = 16
W = 16
PX = 512
IMG = 256
HC = 64
CHUNK = 272
VMEM_MIB = 60
STEPS = 2
SMALL = 16

beta_one = 0.9
beta_two = 0.999
eps_adam = 1e-08
decay_rate = 0.01
eps_norm = 1e-06

F32 = jnp.float32
BF16 = jnp.bfloat16
MESH = pl.DeviceIdType.MESH
NN = (((1,), (0,)), ((), ()))
NT = (((1,), (1,)), ((), ()))
TN = (((0,), (0,)), ((), ()))


def dot(a, b, dims, precision=None):
    return lax.dot_general(a, b, dims, precision=precision, preferred_element_type=F32)


def encode(values):
    top = jnp.max(jnp.abs(values), axis=0, keepdims=True)
    power = jnp.ceil(jnp.log2(jnp.maximum(top, 1e-30))) - 14.0
    codes = jnp.round(values * jnp.exp2(-power)).astype(jnp.int32).astype(jnp.int16)
    powers = jnp.broadcast_to(power, (16, 128)).astype(jnp.int32).astype(jnp.int16)
    return codes, powers


def decode(codes, powers):
    return codes.astype(F32) * jnp.exp2(powers.astype(F32)[0:1])


def kernel(
    n,
    slots_per,
    slots_ref,
    sizes_ref,
    inputs_ref,
    affine_ref,
    labels_ref,
    kept_ref,
    join_ref,
    scale_ref,
    conv_ref,
    head_ref,
    grad_out,
    head_out,
    small_out,
    loss_out,
    conv_in,
    head_in_ref,
    inv_row,
    inv_ref,
    code_ref,
    flip,
    wall,
    xs,
    xt,
    hall,
    jall,
    aall,
    cnt,
    losses,
    mask,
    coef,
    zacc,
    fbuf,
    gh,
    ghall,
    gfeat,
    gsend,
    grecv,
    jt,
    jsend,
    jrecv,
    gs,
    bpart,
    bcore,
    bx,
    bxs,
    dw,
    hg,
    small,
    psend,
    precv,
    ysend,
    yrecv,
    lsend,
    lright,
    lleft,
    bsend2,
    brecv2,
    hag,
    zsum,
    in_sem,
    w_recv,
    w_zr,
    w_zl,
    w_y,
    x_send,
    x_recv,
    h_send,
    h_recv,
    j_send,
    j_recv,
    a_send,
    a_recv,
    c_send,
    c_recv,
    l_send,
    l_recv,
    f_send,
    f_recv,
    g_send,
    g_recv,
    q_send,
    q_recv,
    p_send,
    p_recv,
    s_send,
    s_recv,
    bc_send,
    bc_recv,
    bx_send,
    bx_recv,
    y_send,
    y_recv,
    z_send,
    zr_recv,
    zl_recv,
    b_send,
    b_recv,
    t_recv,
    t_zr,
    t_zl,
    t_y,
):
    nz = n // 2
    last_b = slots_per // 7
    first_a = slots_per - last_b
    last_r = 2 * slots_per // 7
    first_r = slots_per - last_r
    cargo = slots_per + last_r
    piece = hg.shape[0] // n

    me = lax.axis_index("dp")
    ch = lax.axis_index("chan")
    z, y = me // 2, me % 2
    core = ch % 2
    partner = ch + 1 - 2 * core
    across = (ch + 2) % 4
    far = (partner + 2) % 4

    def at(dp=None, chan=None):
        return {"dp": me if dp is None else dp, "chan": ch if chan is None else chan}

    right, left, other = at(dp=me + 2), at(dp=me - 2), at(dp=z * 2 + 1 - y)
    has_right, has_left = z < nz - 1, z > 0

    def put(src, dst, send, recv, dev):
        return pltpu.make_async_remote_copy(
            src_ref=src, dst_ref=dst, send_sem=send, recv_sem=recv, device_id=dev, device_id_type=MESH
        )

    def came(ref, recv):
        put(ref, ref, recv, recv, other).wait_recv()

    def left_it(ref, send):
        put(ref, ref, send, send, other).wait_send()

    def loop(count, body):
        lax.fori_loop(0, count, lambda i, c: (body(i), c)[1], 0)

    def conv_copy(k):
        return pltpu.make_async_copy(conv_ref.at[k], conv_in.at[k], in_sem.at[k])

    head_copy = pltpu.make_async_copy(head_ref, head_in_ref, in_sem.at[slots_per])
    inv_copy = pltpu.make_async_copy(inv_row, inv_ref, in_sem.at[slots_per + 1])
    loop(slots_per, lambda k: conv_copy(k).start())
    head_copy.start()
    barrier = pltpu.get_barrier_semaphore()

    def greet(i):
        pl.semaphore_signal(barrier, inc=1, device_id=at(dp=(me + i + 1) % n), device_id_type=MESH)

    loop(n - 1, greet)
    for peer in (partner, across, far):
        pl.semaphore_signal(barrier, inc=1, device_id=at(chan=peer), device_id_type=MESH)

    def cast_block(k):
        conv_copy(k).wait()
        wall[me * slots_per + k] = conv_in[k].astype(BF16)

    loop(slots_per, cast_block)
    pl.semaphore_wait(barrier, n - 1 + 3)

    def to_right(s):
        return put(wall.at[s], wall.at[s], w_zr.at[s], w_recv.at[s], right)

    def to_left(s):
        return put(wall.at[s], wall.at[s], w_zl.at[s], w_recv.at[s], left)

    def to_other(s):
        return put(wall.at[s], wall.at[s], w_y.at[s], w_recv.at[s], other)

    def both_ways(s):
        @pl.when(has_right)
        def _():
            to_right(s).start()

        @pl.when(has_left)
        def _():
            to_left(s).start()

    def x_copy(l, i, owner, peer, k):
        rows = pl.ds(pl.multiple_of(i * IMG, IMG), IMG)
        ref = xs.at[l, owner, rows, :]
        return put(ref, ref, x_send.at[l, i, k], x_recv.at[l, i, k], at(chan=peer))

    def x_start(l, i):
        x_copy(l, i, ch, across, 0).start()
        x_copy(l, i, ch, partner, 1).start()

    def x_relay(l, i):
        x_copy(l, i, across, across, 0).wait_recv()
        x_copy(l, i, across, partner, 2).start()

    def x_arrive(l, i):
        x_copy(l, i, partner, partner, 1).wait_recv()
        x_copy(l, i, far, partner, 2).wait_recv()

    def x_drain(l, i):
        for k in range(3):
            x_copy(l, i, ch, partner, k).wait_send()

    def h_copy(t, owner, peer, k):
        ref = hall.at[t, owner]
        return put(ref, ref, h_send.at[t, k], h_recv.at[t, k], at(chan=peer))

    def j_copy(owner, peer, k):
        ref = jall.at[:, owner]
        return put(ref, ref, j_send.at[k], j_recv.at[k], at(chan=peer))

    def a_copy(owner, peer, k):
        ref = aall.at[owner]
        return put(ref, ref, a_send.at[k], a_recv.at[k], at(chan=peer))

    def c_copy(i):
        dev = (me + i + 1) % n
        return put(cnt.at[me], cnt.at[me], c_send.at[i], c_recv.at[me], at(dp=dev))

    base = me * slots_per

    def own_b(k):
        to_other(base + first_a + k).start()

    loop(last_b, own_b)

    def own_a(k):
        both_ways(base + k)
        to_other(base + k).start()

    loop(first_a, own_a)
    loop(last_b, lambda k: both_ways(base + first_a + k))
    pixel = lax.broadcasted_iota(jnp.int32, (IMG, 128), 0)
    row_id, col_id = pixel // W, pixel % W

    def mask_image(i):
        inside = (row_id < sizes_ref[i, 0]) & (col_id < sizes_ref[i, 1])
        rows = pl.ds(pl.multiple_of(i * IMG, IMG), IMG)
        mask[rows, :] = jnp.where(inside, 1.0, 0.0)
        xs[0, ch, rows, :] = (inputs_ref[rows, :].astype(F32) * mask[rows, :]).astype(BF16)
        x_start(0, i)

    loop(2, mask_image)
    head_copy.wait()

    def cast_head(t):
        hall[t, ch] = head_in_ref[t].astype(BF16)
        h_copy(t, ch, across, 0).start()
        h_copy(t, ch, partner, 1).start()

    loop(TASKS, cast_head)
    flip[...] = jnp.zeros_like(flip)
    for t in range(TASKS):
        flip[0:K, 0:HC] = join_ref[t]
        flip[32:33, 0:HC] = scale_ref[t : t + 1, :]
        jall[t, ch] = flip[...].T[0:HC]
    aall[ch] = jnp.broadcast_to(affine_ref[LAYERS - 1, 0:1, :], (8, 128))

    code = jnp.where(kept_ref[...] > 0, labels_ref[...], -1).astype(F32).astype(BF16).reshape(2 * TASKS * H, W)
    lane_row = lax.broadcasted_iota(jnp.int32, (W, 128), 1) % W == lax.broadcasted_iota(jnp.int32, (W, 128), 0)
    wide = dot(code, jnp.where(lane_row, 1.0, 0.0).astype(BF16), NN).reshape(4 * TASKS, 8, 128)
    own_row = lax.broadcasted_iota(jnp.int32, (1, 8, 128), 1) == lax.broadcasted_iota(jnp.int32, (1, 8, 128), 2) // W
    rows_of = jnp.sum(jnp.where(own_row, wide, 0.0), axis=1).astype(jnp.int32)
    code_ref[...] = jnp.full(code_ref.shape, -1, jnp.int32)
    for b in range(2):
        for t in range(TASKS):
            for half in range(2):
                place = (b * TASKS + t) * 2 + half
                code_ref[2 * b + half, t : t + 1, :] = rows_of[place : place + 1, :]

    lane = lax.broadcasted_iota(jnp.int32, (8, 128), 1)

    def kept(q):
        spot = (q % 2) * 128 + lane
        hit = (spot // W < sizes_ref[q // 2, 0]) & (spot % W < sizes_ref[q // 2, 1])
        return jnp.where(hit & (code_ref[q] >= 0), 1.0, 0.0)

    total_kept = kept(0) + kept(1) + kept(2) + kept(3)
    cnt[me] = jnp.broadcast_to(jnp.sum(total_kept, axis=1, keepdims=True), (8, 128))

    found = jnp.full((8, 128), -1, jnp.int32)
    for u in range(slots_ref.shape[0]):
        found = jnp.where(lane == slots_ref[u], u, found)
    inv_row[...] = found
    inv_copy.start()

    for copy in (j_copy, a_copy):
        copy(ch, across, 0).start()
        copy(ch, partner, 1).start()
    loop(n - 1, lambda i: c_copy(i).start())

    neighbour = (z * 2 + 1 - y) * slots_per

    def pass_b(k):
        s = neighbour + first_a + k
        came(wall.at[s], w_recv.at[s])
        both_ways(s)

    loop(last_b, pass_b)
    for i in range(2):
        x_relay(0, i)

    def relay_head(t):
        h_copy(t, across, across, 0).wait_recv()
        h_copy(t, across, partner, 2).start()

    def line_in(d, c):
        def source(zz):
            row = jnp.where(c < slots_per, y, 1 - y)
            return (zz * 2 + row) * slots_per + jnp.where(c < slots_per, c, c - last_b)

        @pl.when(z - d >= 0)
        def _():
            s = source(z - d)
            came(wall.at[s], w_recv.at[s])

            @pl.when(has_right)
            def _():
                to_right(s).start()

            @pl.when(c < first_a)
            def _():
                to_other(s).start()

        @pl.when(z + d < nz)
        def _():
            s = source(z + d)
            came(wall.at[s], w_recv.at[s])

            @pl.when(has_left)
            def _():
                to_left(s).start()

            @pl.when(c < first_a)
            def _():
                to_other(s).start()

    def first_step(c):
        pl.when(c < slots_per + last_b)(lambda: line_in(1, c))
        pl.when(c < TASKS)(lambda: relay_head(c))

    loop(max(slots_per + last_b, TASKS), first_step)
    for copy in (j_copy, a_copy):
        copy(across, across, 0).wait_recv()
        copy(across, partner, 2).start()

    inv_copy.wait()

    def transpose_layer(l):
        for c in range(4):
            xt[l, c // 2, (c % 2) * 128 : (c % 2) * 128 + 128, :] = xs[l, c].T

    for i in range(2):
        x_arrive(0, i)
    transpose_layer(0)

    loop(nz - 2, lambda d: loop(slots_per + last_b, lambda c: line_in(d + 2, c)))

    def last_in(zz):
        def block(k):
            s = (zz * 2 + 1 - y) * slots_per + k
            came(wall.at[s], w_recv.at[s])

        loop(first_a, block)

    loop(nz, last_in)

    def conv_forward(l, i):
        rows = pl.ds(pl.multiple_of(i * IMG, IMG), IMG)
        left_side = jnp.concatenate([xs[l, c, rows, :] for c in range(4)], axis=1)
        zacc[...] = jnp.zeros_like(zacc)
        for first in range(0, 9, 2):
            taps = [t for t in (first, first + 1) if t < 9]
            sides = [
                jnp.concatenate([wall[slots_ref[(l * 9 + t) * 2 + h]] for h in range(2)], axis=0)
                for t in taps
            ]
            side = jnp.concatenate(sides, axis=1) if len(sides) > 1 else sides[0]
            out = dot(left_side, side, NN)
            for k, t in enumerate(taps):
                a, e = divmod(t, 3)
                part = out[:, k * 128 : (k + 1) * 128]
                if a == 0:
                    zacc[e, W:IMG, :] += part[: IMG - W]
                elif a == 1:
                    zacc[e] += part
                else:
                    zacc[e, : IMG - W, :] += part[W:]
        linear = zacc[1]
        linear += jnp.where(col_id >= 1, pltpu.roll(zacc[0], 1, 0), 0.0)
        linear += jnp.where(col_id < W - 1, pltpu.roll(zacc[2], IMG - 1, 0), 0.0)
        inside = mask[rows, :]
        gain, shift = affine_ref[l, 0:1, :], affine_ref[l, 1:2, :]
        passed = jnp.where(linear > 0, inside, 0.0)
        coef[l, rows, :] = passed * gain if l < LAYERS - 1 else passed
        out = (jnp.maximum(linear, 0.0) * gain + shift) * inside
        xs[l + 1, ch, rows, :] = out.astype(BF16)

    def quarter(q):
        return pl.ds(pl.multiple_of(q * 128, 128), 128)

    for l in range(LAYERS):

        def forward_image(i, l=l):
            if l > 0:
                x_relay(l, i)
                x_arrive(l, i)
            conv_forward(l, i)
            if l < LAYERS - 1:
                x_start(l + 1, i)

        loop(2, forward_image)
        if 0 < l:
            transpose_layer(l)

    def f_copy(peer, k):
        return put(xs.at[LAYERS, ch, quarter(peer), :], fbuf.at[ch], f_send.at[k], f_recv.at[ch], at(chan=peer))

    peers = (across, far, partner)
    for k, peer in enumerate(peers):
        f_copy(peer, k).start()
    for i in range(2):
        x_start(LAYERS, i)
    fbuf[ch] = xs[LAYERS, ch, quarter(ch), :]

    loop(n - 1, lambda i: came(cnt.at[(me + i + 1) % n], c_recv.at[(me + i + 1) % n]))
    counts = lax.fori_loop(0, n, lambda i, acc: acc + cnt[i], jnp.zeros((8, 128), F32))
    counts = jnp.maximum(counts, 1.0)

    def head_in(t):
        h_copy(t, partner, partner, 1).wait_recv()
        h_copy(t, far, partner, 2).wait_recv()

    loop(TASKS, head_in)
    for copy in (j_copy, a_copy):
        copy(partner, partner, 1).wait_recv()
        copy(far, partner, 2).wait_recv()
    for peer in peers:
        came(fbuf.at[peer], f_recv.at[peer])

    weight = kept(ch) / counts
    losses[0] = weight
    losses[1] = jnp.zeros((8, 128), F32)
    features = jnp.concatenate([fbuf[c] for c in range(4)], axis=1)
    gfeat[...] = jnp.zeros_like(gfeat)
    klass = lax.broadcasted_iota(jnp.int32, (32, 128), 0)

    def q_copy(t, peer, k):
        rows = pl.ds(pl.multiple_of(peer * HC, HC), HC)
        return put(gh.at[t, rows, :], ghall.at[ch, t], q_send.at[t, k], q_recv.at[t, ch], at(chan=peer))

    def head_task(t):
        low = hall[t].reshape(4 * HC, C)
        both = jall[t].reshape(4 * HC, 128)
        join = both.astype(BF16)
        scale = both[:, 32:33]
        hidden = dot(low, features, NT)
        inverse = lax.rsqrt(jnp.sum(hidden * hidden, axis=0, keepdims=True) + eps_norm)
        normed = hidden * inverse
        scaled = (scale * normed).astype(BF16)
        logits = dot(join, scaled, TN)[0:32]
        real = klass < K
        largest = jnp.max(jnp.where(real, logits, -jnp.inf), axis=0, keepdims=True)
        shifted = jnp.where(real, jnp.exp(jnp.where(real, logits - largest, 0.0)), 0.0)
        totals = jnp.sum(shifted, axis=0, keepdims=True)
        onehot = klass == code_ref[ch, pl.ds(t, 1), :]
        picked = jnp.sum(jnp.where(onehot, logits, 0.0), axis=0, keepdims=True)
        share = losses[0, pl.ds(t, 1), :]
        losses[1, pl.ds(t, 1), :] = share * (largest + jnp.log(totals) - picked)
        slope = (share * (shifted / totals - jnp.where(onehot, 1.0, 0.0))).astype(BF16)
        grad_scaled = dot(join, jnp.concatenate([slope, jnp.zeros((96, 128), BF16)], axis=0), NN)
        jt[t, 0:24, :] = dot(slope, scaled, NT)[0:24]
        jt[t, 24:32, :] = dot(jnp.ones((8, 128), F32), grad_scaled * normed, NT, lax.Precision.HIGHEST)
        grad_normed = grad_scaled * scale
        along = jnp.sum(normed * grad_normed, axis=0, keepdims=True)
        grad_hidden = ((grad_normed - normed * along) * inverse).astype(BF16)
        gh[t] = grad_hidden
        for k, peer in enumerate(peers):
            q_copy(t, peer, k).start()
        gfeat[...] += dot(grad_hidden, low, TN)

    for t in range(TASKS):
        head_task(t)
    loss_tile = jnp.broadcast_to(jnp.sum(losses[1], axis=1, keepdims=True), (8, 128))
    jt[TASKS, 0:8, 0:128] = loss_tile
    jt[TASKS, 0:8, 128:256] = loss_tile

    my_mask = mask[quarter(ch), :]
    for c in range(4):
        gsend[c] = (gfeat[:, c * 128 : (c + 1) * 128] * my_mask * aall[c, 0:1, :]).astype(BF16)

    def g_copy(peer, k):
        return put(gsend.at[peer], grecv.at[ch], g_send.at[k], g_recv.at[ch], at(chan=peer))

    def s_copy(peer, k):
        return put(jsend.at[peer], jrecv.at[ch], s_send.at[k], s_recv.at[ch], at(chan=peer))

    for k, peer in enumerate(peers):
        g_copy(peer, k).start()
    for i in range(2):
        x_relay(LAYERS, i)
    grecv[ch] = gsend[ch]
    low_lane = lax.broadcasted_iota(jnp.int32, (32, 128), 1) < HC
    for c in range(4):
        side = slice((c // 2) * 128, (c // 2) * 128 + 128)
        for m in range(4):
            one, two = jt[2 * m, :, side], jt[2 * m + 1, :, side]
            if m == 3:
                two = jnp.where(lax.broadcasted_iota(jnp.int32, (32, 128), 0) < 8, two, 0.0)
            if c % 2 == 0:
                two = pltpu.roll(two, HC, 1)
            else:
                one = pltpu.roll(one, HC, 1)
            jsend[c, m] = jnp.where(low_lane, one, two)
    for k, peer in enumerate(peers):
        s_copy(peer, k).start()
    ghall[ch] = gh[:, pl.ds(pl.multiple_of(ch * HC, HC), HC), :]
    jrecv[ch] = jsend[ch]

    def spread(l, i, grad):
        columns = (
            jnp.where(col_id < W - 1, pltpu.roll(grad, IMG - 1, 0), 0.0),
            grad,
            jnp.where(col_id >= 1, pltpu.roll(grad, 1, 0), 0.0),
        )
        top = pl.multiple_of(i * IMG, IMG)
        blank = jnp.zeros((W, 128), BF16)
        for e in range(3):
            low = columns[e].astype(BF16)
            gs[l * 9 + e, pl.ds(top, IMG - W), :] = low[W:]
            gs[l * 9 + e, pl.ds(top + IMG - W, W), :] = blank
            gs[l * 9 + 3 + e, pl.ds(top, IMG), :] = low
            gs[l * 9 + 6 + e, pl.ds(top + W, IMG - W), :] = low[: IMG - W]
            gs[l * 9 + 6 + e, pl.ds(top, W), :] = blank

    def conv_backward(l, i, h):
        rows = pl.ds(pl.multiple_of(i * IMG, IMG), IMG)
        total = None
        for first in range(0, 9, 2):
            taps = [t for t in (first, first + 1) if t < 9]
            grads = [gs[l * 9 + t, rows, :] for t in taps]
            sides = [wall[slots_ref[(l * 9 + t) * 2 + h]] for t in taps]
            if len(taps) > 1:
                term = dot(jnp.concatenate(grads, axis=1), jnp.concatenate(sides, axis=1), NT)
            else:
                term = dot(grads[0], sides[0], NT)
            total = term if total is None else total + term
        bpart[l - 1, i, h, 0] = total[:, :128]
        bpart[l - 1, i, h, 1] = total[:, 128:]

    def bc_copy(l, i, h):
        return put(
            bpart.at[l - 1, i, h, 1 - core],
            bcore.at[l - 1, i, h],
            bc_send.at[l - 1, i, h],
            bc_recv.at[l - 1, i, h],
            at(chan=partner),
        )

    def bx_copy(l, i):
        return put(bxs.at[l - 1, i], bx.at[l - 1, i], bx_send.at[l - 1, i], bx_recv.at[l - 1, i], at(chan=across))

    def weight_grads(l):
        lhs = xt[l].reshape(C, PX)

        def pair(p):
            t = 2 * p
            rhs = jnp.concatenate([gs[l * 9 + t], gs[l * 9 + t + 1]], axis=1)
            out = dot(lhs, rhs, NN)
            for h in range(2):
                dw[(l * 9 + t) * 2 + h] = out[h * 256 : (h + 1) * 256, :128]
                dw[(l * 9 + t + 1) * 2 + h] = out[h * 256 : (h + 1) * 256, 128:]

        loop(4, pair)
        out = dot(lhs, gs[l * 9 + 8], NN)
        for h in range(2):
            dw[(l * 9 + 8) * 2 + h] = out[h * 256 : (h + 1) * 256]

    def l_copy(i):
        dev = (me + i + 1) % n
        return put(losses.at[2 + me], losses.at[2 + me], l_send.at[i], l_recv.at[me], at(dp=dev))

    def head_part(dest):
        rows = hg[pl.ds(pl.multiple_of(dest * piece, 16), piece), :]
        return rows, small[pl.ds(pl.multiple_of(dest * SMALL, SMALL), SMALL), :]

    def write(ref, values):
        codes, powers = encode(values)
        ref[0:256, :] = codes
        ref[256:272, :] = powers

    def read(ref):
        return decode(ref[0:256, :], ref[256:272, :])

    def write_head(ref, values):
        codes, powers = encode(values[0])
        ref[0:piece, :] = codes
        ref[piece : piece + 16, :] = powers
        codes, powers = encode(values[1])
        ref[piece + 16 : piece + 32, :] = codes
        ref[piece + 32 : piece + 48, :] = powers

    def read_head(ref):
        one = decode(ref[0:piece, :], ref[piece : piece + 16, :])
        return one, decode(ref[piece + 16 : piece + 32, :], ref[piece + 32 : piece + 48, :])

    def p_copy(i):
        dest = (me + i + 1) % n
        return put(psend.at[dest], precv.at[me], p_send.at[i], p_recv.at[me], at(dp=dest))

    def head_grads():
        for i in range(2):
            x_arrive(LAYERS, i)
        for peer in peers:
            loop(TASKS, lambda t, peer=peer: came(ghall.at[peer, t], q_recv.at[t, peer]))
            came(jrecv.at[peer], s_recv.at[peer])
        lhs = [
            jnp.concatenate([ghall[2 * m].reshape(TASKS * HC, 128), ghall[2 * m + 1].reshape(TASKS * HC, 128)], axis=1)
            for m in range(2)
        ]
        for c in range(0, 4, 2):
            total = None
            for m in range(2):
                rows = slice(m * IMG, (m + 1) * IMG)
                rhs = jnp.concatenate([xs[LAYERS, c, rows, :], xs[LAYERS, c + 1, rows, :]], axis=1)
                term = dot(lhs[m], rhs, NN)
                total = term if total is None else total + term
            hg[c * 448 : (c + 1) * 448, :] = total[:, :128]
            hg[(c + 1) * 448 : (c + 2) * 448, :] = total[:, 128:]
        if hg.shape[0] > 1792:
            hg[1792:, :] = jnp.zeros((hg.shape[0] - 1792, 128), F32)
        small[...] = jnp.zeros_like(small)
        for m in range(4):
            small[m * 32 : (m + 1) * 32, :] = jrecv[0, m] + jrecv[1, m] + jrecv[2, m] + jrecv[3, m]
        losses[2 + me] = small[96:104, :]


        def give(i):
            dest = (me + i + 1) % n
            write_head(psend.at[dest], head_part(dest))
            p_copy(i).start()

        loop(n - 1, give)
        loop(n - 1, lambda i: l_copy(i).start())

    for peer in peers:
        came(grecv.at[peer], g_recv.at[peer])

    def top_grad(i):
        rows = pl.ds(pl.multiple_of(i * IMG, IMG), IMG)
        grad = jnp.concatenate([grecv[2 * i], grecv[2 * i + 1]], axis=0).astype(F32)
        spread(LAYERS - 1, i, grad * coef[LAYERS - 1, rows, :])

    loop(2, top_grad)
    x_side = ch // 2
    for l in (2, 1):

        def partial_image(i, h, l=l):
            conv_backward(l, i, h)
            bc_copy(l, i, h).start()

        def chip_sum(i, l=l):
            bc_copy(l, i, 1 - x_side).wait_recv()
            bxs[l - 1, i] = (bpart[l - 1, i, 1 - x_side, core] + bcore[l - 1, i, 1 - x_side]).astype(BF16)
            bx_copy(l, i).start()

        loop(2, lambda i: partial_image(i, 1 - x_side))
        loop(2, chip_sum)
        loop(2, lambda i: partial_image(i, x_side))
        if l == LAYERS - 1:
            head_grads()
        else:
            weight_grads(LAYERS - 1)
            weight_grads(l)

        def finish_image(i, l=l):
            bx_copy(l, i).wait_recv()
            bc_copy(l, i, x_side).wait_recv()
            grad = bpart[l - 1, i, x_side, core] + bcore[l - 1, i, x_side] + bx[l - 1, i].astype(F32)
            rows = pl.ds(pl.multiple_of(i * IMG, IMG), IMG)
            spread(l - 1, i, grad * coef[l - 1, rows, :])

        loop(2, finish_image)
    weight_grads(0)

    def part(dest, k):
        u = inv_ref[0, dest * slots_per + k]
        return dw[jnp.maximum(u, 0)] * jnp.where(u >= 0, 1.0, 0.0)

    def y_copy(zz, k):
        return put(ysend.at[zz, k], yrecv.at[zz, k], y_send.at[zz, k], y_recv.at[zz, k], other)

    def z_right(zz, k):
        return put(lsend.at[zz, k], lleft.at[zz, k], z_send.at[zz, k], zl_recv.at[zz, k], right)

    def z_left(zz, k):
        return put(lsend.at[zz, k], lright.at[zz, k], z_send.at[zz, k], zr_recv.at[zz, k], left)

    def both_sides(d, body):
        for zz, ok in ((z - d, z - d >= 0), (z + d, z + d < nz)):

            @pl.when(ok)
            def _(zz=zz):
                body(zz)

    def cross(zz):
        dest = zz * 2 + 1 - y

        def block(k):
            write(ysend.at[zz, k], part(dest, k))
            y_copy(zz, k).start()

        loop(first_r, block)

    def pass_on(zz, k):
        @pl.when(zz > z)
        def _():
            z_right(zz, k).start()

        @pl.when(zz < z)
        def _():
            z_left(zz, k).start()

    def line_conv(zz, k):
        is_a, is_own = k < first_r, k < slots_per
        dest = zz * 2 + jnp.where(is_own, y, 1 - y)
        slot = jnp.where(is_own, k, k - last_r)
        zsum[...] = part(dest, slot)

        @pl.when(is_a)
        def _():
            came(yrecv.at[zz, k], y_recv.at[zz, k])
            zsum[...] += read(yrecv.at[zz, k])

        @pl.when((zz >= z) & has_left)
        def _():
            came(lleft.at[zz, k], zl_recv.at[zz, k])
            zsum[...] += read(lleft.at[zz, k])

        @pl.when((zz <= z) & has_right)
        def _():
            came(lright.at[zz, k], zr_recv.at[zz, k])
            zsum[...] += read(lright.at[zz, k])

    loop(nz - 1, lambda i: both_sides(nz - 1 - i, cross))
    cross(z)

    def tag(j):
        return hag.at[j]

    def t_right(j):
        return put(tag(j), tag(j), t_zr.at[j], t_recv.at[j], right)

    def t_left(j):
        return put(tag(j), tag(j), t_zl.at[j], t_recv.at[j], left)

    def t_other(j):
        return put(tag(j), tag(j), t_y.at[j], t_recv.at[j], other)

    rows, few = head_part(me)
    zsum[0:piece, :] = rows
    zsum[piece : piece + SMALL, :] = few

    def add_piece(i):
        source = (me + i + 1) % n
        came(precv.at[source], p_recv.at[source])
        one, two = read_head(precv.at[source])
        zsum[0:piece, :] += one
        zsum[piece : piece + SMALL, :] += two

    loop(n - 1, add_piece)
    write_head(hag.at[me], (zsum[0:piece, :], zsum[piece : piece + SMALL, :]))

    @pl.when(has_right)
    def _():
        t_right(me).start()

    @pl.when(has_left)
    def _():
        t_left(me).start()

    t_other(me).start()

    def tail(d):
        @pl.when(z - d >= 0)
        def _():
            j = (z - d) * 2 + y
            came(tag(j), t_recv.at[j])

            @pl.when(has_right)
            def _():
                t_right(j).start()

            t_other(j).start()

        @pl.when(z + d < nz)
        def _():
            j = (z + d) * 2 + y
            came(tag(j), t_recv.at[j])

            @pl.when(has_left)
            def _():
                t_left(j).start()

            t_other(j).start()

    def out_step(i):
        d = nz - 1 - i

        def item(c):
            k = (c + first_r) % cargo

            def send(zz):
                line_conv(zz, k)
                write(lsend.at[zz, k], zsum[...])
                pass_on(zz, k)

            both_sides(d, send)

        loop(cargo, item)
        tail(i + 1)

    loop(nz - 1, out_step)

    def b_copy(k):
        return put(bsend2.at[k], brecv2.at[k], b_send.at[k], b_recv.at[k], other)

    def give_b(k):
        line_conv(z, slots_per + k)
        write(bsend2.at[k], zsum[...])
        b_copy(k).start()

    loop(last_r, give_b)

    def own_slot(k):
        line_conv(z, k)
        grad_out[k] = zsum[...]

    loop(first_r, own_slot)

    loop(n - 1, lambda i: came(losses.at[2 + (me + i + 1) % n], l_recv.at[(me + i + 1) % n]))
    loss_tile = lax.fori_loop(0, n, lambda i, acc: acc + losses[2 + i], jnp.zeros((8, 128), F32))
    loss_out[0] = jnp.sum(loss_tile[:TASKS, HC : HC + 1])

    def other_row(zz):
        j = zz * 2 + 1 - y
        came(tag(j), t_recv.at[j])

    loop(nz, other_row)
    per = 448 // piece

    def unpack(j):
        one, two = read_head(hag.at[j])

        @pl.when(j < 4 * per)
        def _():
            rows = pl.ds(pl.multiple_of((j % per) * piece, 16), piece)
            head_out[rows, pl.ds(pl.multiple_of((j // per) * 128, 128), 128)] = one

        @pl.when(j < 8)
        def _():
            small[pl.ds(pl.multiple_of(j * SMALL, SMALL), SMALL), :] = two

    loop(n, unpack)
    for m in range(4):
        pair = small[m * 32 : (m + 1) * 32, :]
        small_out[2 * m] = pair
        small_out[2 * m + 1] = pltpu.roll(pair, HC, 1)

    def own_last(k):
        line_conv(z, first_r + k)
        came(brecv2.at[k], b_recv.at[k])
        grad_out[first_r + k] = zsum[...] + read(brecv2.at[k])

    loop(last_r, own_last)

    def drain_w(s):
        k = s % slots_per
        zz, row = s // (2 * slots_per), (s // slots_per) % 2
        on_line = (row == y) | (k >= first_a)

        @pl.when(on_line & has_right & (zz <= z))
        def _():
            left_it(wall.at[s], w_zr.at[s])

        @pl.when(on_line & has_left & (zz >= z))
        def _():
            left_it(wall.at[s], w_zl.at[s])

        @pl.when((row == y) & ((k < first_a) | (zz == z)))
        def _():
            left_it(wall.at[s], w_y.at[s])

    loop(n * slots_per, drain_w)

    def drain_t(zz):
        j = zz * 2 + y

        @pl.when(has_right & (zz <= z))
        def _():
            left_it(tag(j), t_zr.at[j])

        @pl.when(has_left & (zz >= z))
        def _():
            left_it(tag(j), t_zl.at[j])

        left_it(tag(j), t_y.at[j])

        def y_block(k):
            y_copy(zz, k).wait_send()

        loop(first_r, y_block)

        @pl.when(zz != z)
        def _():
            loop(cargo, lambda k: left_it(lsend.at[zz, k], z_send.at[zz, k]))

    loop(nz, drain_t)
    loop(last_r, lambda k: b_copy(k).wait_send())
    for l in range(LAYERS + 1):
        for i in range(2):
            x_drain(l, i)
    for k in range(3):
        loop(TASKS, lambda t, k=k: h_copy(t, ch, partner, k).wait_send())
        j_copy(ch, partner, k).wait_send()
        a_copy(ch, partner, k).wait_send()
    for k, peer in enumerate(peers):
        f_copy(peer, k).wait_send()
        g_copy(peer, k).wait_send()
        loop(TASKS, lambda t, k=k, peer=peer: q_copy(t, peer, k).wait_send())
        s_copy(peer, k).wait_send()
    for l in (1, 2):
        for i in range(2):
            for h in range(2):
                bc_copy(l, i, h).wait_send()
            bx_copy(l, i).wait_send()
    loop(n - 1, lambda i: c_copy(i).wait_send())
    loop(n - 1, lambda i: l_copy(i).wait_send())
    loop(n - 1, lambda i: p_copy(i).wait_send())


def adamw(weight, gradient, moment_one, moment_two, step_rate, one_over, two_over):
    moment_one = beta_one * moment_one + (1.0 - beta_one) * gradient
    moment_two = beta_two * moment_two + (1.0 - beta_two) * gradient * gradient
    first_hat = moment_one * one_over
    second_hat = moment_two * two_over
    weight = weight - step_rate * (
        first_hat / (jnp.sqrt(second_hat) + eps_adam) + decay_rate * weight
    )
    return (weight, moment_one, moment_two)


def update(
    over_ref,
    conv_g,
    conv_w,
    conv_m,
    conv_v,
    head_g,
    head_w,
    head_m,
    head_v,
    small_g,
    join_w,
    join_m,
    join_v,
    scale_w,
    scale_m,
    scale_v,
    conv_out,
    conv_out_m,
    conv_out_v,
    head_out,
    head_out_m,
    head_out_v,
    join_out,
    join_out_m,
    join_out_v,
    scale_out,
    scale_out_m,
    scale_out_v,
):
    one_over, two_over = over_ref[0], over_ref[1]

    def put_all(outs, values):
        for out, value in zip(outs, values):
            out[...] = value

    conv = adamw(conv_w[...], conv_g[...], conv_m[...], conv_v[...], 0.01, one_over, two_over)
    put_all((conv_out, conv_out_m, conv_out_v), conv)
    head = adamw(head_w[...], head_g[...], head_m[...], head_v[...], 0.03, one_over, two_over)
    put_all((head_out, head_out_m, head_out_v), head)

    @pl.when(pl.program_id(0) == 0)
    def _():
        join_g = small_g[:TASKS, :K, :HC]
        join = adamw(join_w[...], join_g, join_m[...], join_v[...], 0.4, one_over, two_over)
        put_all((join_out, join_out_m, join_out_v), join)
        scale_g = jnp.concatenate([small_g[t, 24:25, :HC] for t in range(TASKS)], axis=0)
        scale = adamw(scale_w[...], scale_g, scale_m[...], scale_v[...], 0.8, one_over, two_over)
        put_all((scale_out, scale_out_m, scale_out_v), scale)


def per_device(
    n,
    inputs,
    affine,
    image_sizes,
    labels,
    label_mask,
    unit_slots,
    conv_master,
    conv_first,
    conv_second,
    head_master,
    head_first,
    head_second,
    join_master,
    join_first,
    join_second,
    scale_master,
    scale_first,
    scale_second,
    step_count,
):
    slots_per = conv_master.shape[0]
    nz = n // 2
    last_r = 2 * slots_per // 7
    first_r = slots_per - last_r
    cargo = slots_per + last_r
    piece = -(-1792 // (n * 16)) * 16
    vm, dma = pltpu.VMEM, pltpu.SemaphoreType.DMA
    shape = jax.ShapeDtypeStruct
    scratch = [
        vm((slots_per, 256, 128), F32),
        vm((TASKS, HC, C), F32),
        vm((8, 128), jnp.int32),
        pltpu.SMEM((8, 128), jnp.int32),
        vm((4, 8, 128), jnp.int32),
        vm((128, 128), F32),
        vm((n * slots_per, 256, 128), BF16),
        vm((LAYERS + 1, 4, PX, 128), BF16),
        vm((LAYERS, 2, 256, PX), BF16),
        vm((TASKS, 4, HC, C), BF16),
        vm((TASKS, 4, HC, 128), F32),
        vm((4, 8, 128), F32),
        vm((n, 8, 128), F32),
        vm((n + 2, 8, 128), F32),
        vm((PX, 128), F32),
        vm((LAYERS, PX, 128), F32),
        vm((3, IMG, 128), F32),
        vm((4, 128, 128), BF16),
        vm((TASKS, 256, 128), BF16),
        vm((4, TASKS, HC, 128), BF16),
        vm((128, C), F32),
        vm((4, 128, 128), BF16),
        vm((4, 128, 128), BF16),
        vm((8, 32, 256), F32),
        vm((4, 4, 32, 128), F32),
        vm((4, 4, 32, 128), F32),
        vm((27, PX, 128), BF16),
        vm((2, 2, 2, 2, IMG, 128), F32),
        vm((2, 2, 2, IMG, 128), F32),
        vm((2, 2, IMG, 128), BF16),
        vm((2, 2, IMG, 128), BF16),
        vm((54, 256, 128), F32),
        vm((n * piece, 128), F32),
        vm((n * SMALL, 128), F32),
        vm((n, piece + 48, 128), jnp.int16),
        vm((n, piece + 48, 128), jnp.int16),
        vm((nz, first_r, CHUNK, 128), jnp.int16),
        vm((nz, first_r, CHUNK, 128), jnp.int16),
        vm((nz, cargo, CHUNK, 128), jnp.int16),
        vm((nz, cargo, CHUNK, 128), jnp.int16),
        vm((nz, cargo, CHUNK, 128), jnp.int16),
        vm((max(last_r, 1), CHUNK, 128), jnp.int16),
        vm((max(last_r, 1), CHUNK, 128), jnp.int16),
        vm((n, piece + 48, 128), jnp.int16),
        vm((256, 128), F32),
        dma((slots_per + 2,)),
        *[dma((n * slots_per,)) for _ in range(4)],
        *[dma((LAYERS + 1, 2, 3)) for _ in range(2)],
        *[dma((TASKS, 3)) for _ in range(2)],
        *[dma((3,)) for _ in range(4)],
        *[dma((n,)) for _ in range(4)],
        dma((3,)), dma((4,)),
        dma((3,)), dma((4,)),
        *[dma((TASKS, k)) for k in (3, 4)],
        *[dma((n,)) for _ in range(2)],
        dma((3,)), dma((4,)),
        *[dma((2, 2, 2)) for _ in range(2)],
        *[dma((2, 2)) for _ in range(2)],
        *[dma((nz, first_r)) for _ in range(2)],
        *[dma((nz, cargo)) for _ in range(3)],
        *[dma((max(last_r, 1),)) for _ in range(2)],
        *[dma((n,)) for _ in range(4)],
    ]
    in_smem, in_vmem = pl.BlockSpec(memory_space=pltpu.SMEM), pl.BlockSpec(memory_space=pltpu.VMEM)
    in_hbm = pl.BlockSpec(memory_space=pltpu.HBM)
    slot_grads, head_total, small_total, loss = pl.pallas_call(
        functools.partial(kernel, n, slots_per),
        out_shape=(
            shape((slots_per, 256, 128), F32),
            shape((448, C), F32),
            shape((8, 32, 128), F32),
            shape((1,), F32),
        ),
        in_specs=[in_smem] * 2 + [in_vmem] * 6 + [in_hbm] * 2,
        out_specs=(in_vmem,) * 3 + (in_smem,),
        scratch_shapes=scratch,
        compiler_params=pltpu.CompilerParams(
            collective_id=0, has_side_effects=True, vmem_limit_bytes=VMEM_MIB * 2**20
        ),
    )(
        unit_slots,
        image_sizes,
        inputs.reshape(PX, 128),
        affine,
        labels.transpose(0, 3, 1, 2),
        label_mask.transpose(0, 3, 1, 2),
        join_master.transpose(0, 2, 1),
        scale_master,
        conv_master,
        head_master,
    )
    step_float = step_count.astype(F32)
    over = jnp.concatenate([1.0 / (1.0 - beta_one**step_float), 1.0 / (1.0 - beta_two**step_float)])
    conv_rows, head_rows = slots_per * 256, TASKS * HC
    steps = STEPS

    def tile(rows, columns):
        return pl.BlockSpec((rows // steps, columns), lambda i: (i, 0))

    def whole(*sizes):
        return pl.BlockSpec(sizes, lambda i: (0,) * len(sizes))

    conv_tile, head_tile = tile(conv_rows, 128), tile(head_rows, C)
    join_tile, scale_tile = whole(TASKS, K, HC), whole(TASKS, HC)
    flat_conv = [a.reshape(conv_rows, 128) for a in (slot_grads, conv_master, conv_first, conv_second)]
    flat_head = [a.reshape(head_rows, C) for a in (head_total, head_master, head_first, head_second)]
    flat_join = [a.transpose(0, 2, 1) for a in (join_master, join_first, join_second)]
    out = pl.pallas_call(
        update,
        grid=(steps,),
        out_shape=tuple(
            [shape((conv_rows, 128), F32)] * 3
            + [shape((head_rows, C), F32)] * 3
            + [shape((TASKS, K, HC), F32)] * 3
            + [shape((TASKS, HC), F32)] * 3
        ),
        in_specs=[in_smem]
        + [conv_tile] * 4
        + [head_tile] * 4
        + [whole(8, 32, 128)]
        + [join_tile] * 3
        + [scale_tile] * 3,
        out_specs=tuple([conv_tile] * 3 + [head_tile] * 3 + [join_tile] * 3 + [scale_tile] * 3),
    )(over, *flat_conv, *flat_head, small_total, *flat_join, scale_master, scale_first, scale_second)
    conv_out = tuple(a.reshape(slots_per, 256, 128) for a in out[0:3])
    head_out = tuple(a.reshape(TASKS, HC, C) for a in out[3:6])
    join_out = tuple(a.transpose(0, 2, 1) for a in out[6:9])
    return (loss,) + conv_out + head_out + join_out + tuple(out[9:12])


def solution(mesh):
    placed = (
        P("dp", None, None, "chan"),
        P(None, None, "chan"),
        P("dp", None),
        P("dp", None, None, None),
        P("dp", None, None, None),
        P(),
        P("dp", None, "chan"),
        P("dp", None, "chan"),
        P("dp", None, "chan"),
        P(None, "chan", None),
        P(None, "chan", None),
        P(None, "chan", None),
        P(None, "chan", None),
        P(None, "chan", None),
        P(None, "chan", None),
        P(None, "chan"),
        P(None, "chan"),
        P(None, "chan"),
        P(),
    )
    return jax.shard_map(
        functools.partial(per_device, mesh.shape["dp"]),
        mesh=mesh,
        in_specs=placed,
        out_specs=(P(),) + placed[6:18],
        check_vma=False,
    )
```

```python
import functools

import jax
import jax.numpy as jnp
from jax import lax
from jax.experimental import pallas as pl
from jax.experimental.pallas import tpu as pltpu
from jax.sharding import PartitionSpec as P

C = 512
K = 21
TASKS = 7
LAYERS = 3
H = 16
W = 16
PX = 512
IMG = 256
TALL = IMG + 2 * W
HC = 64
CHUNK = 272
VMEM_MIB = 60
STEPS = 2
SMALL = 16

beta_one = 0.9
beta_two = 0.999
eps_adam = 1e-08
decay_rate = 0.01
eps_norm = 1e-06

F32 = jnp.float32
BF16 = jnp.bfloat16
MESH = pl.DeviceIdType.MESH
NN = (((1,), (0,)), ((), ()))
NT = (((1,), (1,)), ((), ()))
TN = (((0,), (0,)), ((), ()))


def dot(a, b, dims, precision=None):
    return lax.dot_general(a, b, dims, precision=precision, preferred_element_type=F32)


def encode(values):
    top = jnp.max(jnp.abs(values), axis=0, keepdims=True)
    power = jnp.ceil(jnp.log2(jnp.maximum(top, 1e-30))) - 14.0
    codes = jnp.round(values * jnp.exp2(-power)).astype(jnp.int32).astype(jnp.int16)
    powers = jnp.broadcast_to(power, (16, 128)).astype(jnp.int32).astype(jnp.int16)
    return codes, powers


def decode(codes, powers):
    return codes.astype(F32) * jnp.exp2(powers.astype(F32)[0:1])


def kernel(
    n,
    slots_per,
    slots_ref,
    sizes_ref,
    inputs_ref,
    affine_ref,
    labels_ref,
    kept_ref,
    join_ref,
    scale_ref,
    conv_ref,
    head_ref,
    grad_out,
    head_out,
    small_out,
    loss_out,
    conv_in,
    head_in_ref,
    inv_row,
    inv_ref,
    code_ref,
    flip,
    wall,
    xs,
    xt,
    hall,
    jall,
    aall,
    cnt,
    losses,
    mask,
    coef,
    zacc,
    fbuf,
    gh,
    ghall,
    gfeat,
    gsend,
    grecv,
    jt,
    jsend,
    jrecv,
    gs,
    bpart,
    bcore,
    bx,
    bxs,
    dw,
    hg,
    small,
    psend,
    precv,
    ysend,
    yrecv,
    lsend,
    lright,
    lleft,
    bsend2,
    brecv2,
    hag,
    zsum,
    in_sem,
    w_recv,
    w_zr,
    w_zl,
    w_y,
    x_send,
    x_recv,
    h_send,
    h_recv,
    j_send,
    j_recv,
    a_send,
    a_recv,
    c_send,
    c_recv,
    l_send,
    l_recv,
    f_send,
    f_recv,
    g_send,
    g_recv,
    q_send,
    q_recv,
    p_send,
    p_recv,
    s_send,
    s_recv,
    bc_send,
    bc_recv,
    bx_send,
    bx_recv,
    y_send,
    y_recv,
    z_send,
    zr_recv,
    zl_recv,
    b_send,
    b_recv,
    t_recv,
    t_zr,
    t_zl,
    t_y,
):
    nz = n // 2
    last_b = slots_per // 7
    first_a = slots_per - last_b
    last_r = slots_per // 7
    first_r = slots_per - last_r
    cargo = slots_per + last_r
    piece = hg.shape[0] // n

    me = lax.axis_index("dp")
    ch = lax.axis_index("chan")
    z, y = me // 2, me % 2
    core = ch % 2
    partner = ch + 1 - 2 * core
    across = (ch + 2) % 4
    far = (partner + 2) % 4

    def at(dp=None, chan=None):
        return {"dp": me if dp is None else dp, "chan": ch if chan is None else chan}

    right, left, other = at(dp=me + 2), at(dp=me - 2), at(dp=z * 2 + 1 - y)
    has_right, has_left = z < nz - 1, z > 0

    def put(src, dst, send, recv, dev):
        return pltpu.make_async_remote_copy(
            src_ref=src, dst_ref=dst, send_sem=send, recv_sem=recv, device_id=dev, device_id_type=MESH
        )

    def came(ref, recv):
        put(ref, ref, recv, recv, other).wait_recv()

    def left_it(ref, send):
        put(ref, ref, send, send, other).wait_send()

    def loop(count, body):
        lax.fori_loop(0, count, lambda i, c: (body(i), c)[1], 0)

    def conv_copy(k):
        return pltpu.make_async_copy(conv_ref.at[k], conv_in.at[k], in_sem.at[k])

    head_copy = pltpu.make_async_copy(head_ref, head_in_ref, in_sem.at[slots_per])
    inv_copy = pltpu.make_async_copy(inv_row, inv_ref, in_sem.at[slots_per + 1])
    loop(slots_per, lambda k: conv_copy(k).start())
    head_copy.start()
    barrier = pltpu.get_barrier_semaphore()

    for peer in (partner, across, far):
        pl.semaphore_signal(barrier, inc=1, device_id=at(chan=peer), device_id_type=MESH)
    pl.semaphore_signal(barrier, inc=1, device_id=other, device_id_type=MESH)

    @pl.when(has_right)
    def _():
        pl.semaphore_signal(barrier, inc=1, device_id=right, device_id_type=MESH)

    @pl.when(has_left)
    def _():
        pl.semaphore_signal(barrier, inc=1, device_id=left, device_id_type=MESH)

    def cast_block(k):
        conv_copy(k).wait()
        wall[me * slots_per + k] = conv_in[k].astype(BF16)

    loop(slots_per, cast_block)
    pl.semaphore_wait(barrier, 4 + jnp.where(has_right, 1, 0) + jnp.where(has_left, 1, 0))

    def to_right(s):
        return put(wall.at[s], wall.at[s], w_zr.at[0], w_recv.at[s], right)

    def to_left(s):
        return put(wall.at[s], wall.at[s], w_zl.at[0], w_recv.at[s], left)

    def to_other(s):
        return put(wall.at[s], wall.at[s], w_y.at[0], w_recv.at[s], other)

    def both_ways(s):
        @pl.when(has_right)
        def _():
            to_right(s).start()

        @pl.when(has_left)
        def _():
            to_left(s).start()

    def x_copy(l, i, owner, peer, k):
        rows = pl.ds(pl.multiple_of(i * IMG, IMG), IMG)
        ref = xs.at[l, owner, rows, :]
        return put(ref, ref, x_send.at[0], x_recv.at[l, i, k], at(chan=peer))

    def x_start(l, i):
        x_copy(l, i, ch, across, 0).start()
        x_copy(l, i, ch, partner, 1).start()

    def x_relay(l, i):
        x_copy(l, i, across, across, 0).wait_recv()
        x_copy(l, i, across, partner, 2).start()

    def x_arrive(l, i):
        x_copy(l, i, partner, partner, 1).wait_recv()
        x_copy(l, i, far, partner, 2).wait_recv()

    def h_copy(t, owner, peer, k):
        ref = hall.at[t, owner]
        return put(ref, ref, h_send.at[0], h_recv.at[t, k], at(chan=peer))

    def j_copy(owner, peer, k):
        ref = jall.at[:, owner]
        return put(ref, ref, j_send.at[k], j_recv.at[k], at(chan=peer))

    def a_copy(owner, peer, k):
        ref = aall.at[owner]
        return put(ref, ref, a_send.at[k], a_recv.at[k], at(chan=peer))

    def c_copy(i):
        dev = (me + i + 1) % n
        return put(cnt.at[me], cnt.at[me], c_send.at[0], c_recv.at[me], at(dp=dev))

    base = me * slots_per

    def own_b(k):
        to_other(base + first_a + k).start()

    loop(last_b, own_b)

    def own_a(k):
        both_ways(base + k)
        to_other(base + k).start()

    loop(first_a, own_a)
    loop(last_b, lambda k: both_ways(base + first_a + k))
    pixel = lax.broadcasted_iota(jnp.int32, (IMG, 128), 0)
    row_id, col_id = pixel // W, pixel % W

    def mask_image(i):
        inside = (row_id < sizes_ref[i, 0]) & (col_id < sizes_ref[i, 1])
        rows = pl.ds(pl.multiple_of(i * IMG, IMG), IMG)
        mask[rows, :] = jnp.where(inside, 1.0, 0.0)
        xs[0, ch, rows, :] = (inputs_ref[rows, :].astype(F32) * mask[rows, :]).astype(BF16)
        x_start(0, i)

    loop(2, mask_image)
    head_copy.wait()

    def cast_head(t):
        hall[t, ch] = head_in_ref[t].astype(BF16)
        h_copy(t, ch, across, 0).start()
        h_copy(t, ch, partner, 1).start()

    loop(TASKS, cast_head)
    for i in range(2):
        gs[:, i * TALL : i * TALL + W, :] = jnp.zeros((9, W, 128), BF16)
        gs[:, (i + 1) * TALL - W : (i + 1) * TALL, :] = jnp.zeros((9, W, 128), BF16)
    flip[...] = jnp.zeros_like(flip)
    for t in range(TASKS):
        flip[0:K, 0:HC] = join_ref[t]
        flip[32:33, 0:HC] = scale_ref[t : t + 1, :]
        jall[t, ch] = flip[...].T[0:HC]
    aall[ch] = jnp.broadcast_to(affine_ref[LAYERS - 1, 0:1, :], (8, 128))

    code = jnp.where(kept_ref[...] > 0, labels_ref[...], -1).astype(F32).astype(BF16).reshape(2 * TASKS * H, W)
    lane_row = lax.broadcasted_iota(jnp.int32, (W, 128), 1) % W == lax.broadcasted_iota(jnp.int32, (W, 128), 0)
    wide = dot(code, jnp.where(lane_row, 1.0, 0.0).astype(BF16), NN).reshape(4 * TASKS, 8, 128)
    own_row = lax.broadcasted_iota(jnp.int32, (1, 8, 128), 1) == lax.broadcasted_iota(jnp.int32, (1, 8, 128), 2) // W
    rows_of = jnp.sum(jnp.where(own_row, wide, 0.0), axis=1).astype(jnp.int32)
    code_ref[...] = jnp.full(code_ref.shape, -1, jnp.int32)
    for b in range(2):
        for t in range(TASKS):
            for half in range(2):
                place = (b * TASKS + t) * 2 + half
                code_ref[2 * b + half, t : t + 1, :] = rows_of[place : place + 1, :]

    lane = lax.broadcasted_iota(jnp.int32, (8, 128), 1)

    def kept(q):
        spot = (q % 2) * 128 + lane
        hit = (spot // W < sizes_ref[q // 2, 0]) & (spot % W < sizes_ref[q // 2, 1])
        return jnp.where(hit & (code_ref[q] >= 0), 1.0, 0.0)

    total_kept = kept(0) + kept(1) + kept(2) + kept(3)
    cnt[me] = jnp.broadcast_to(jnp.sum(total_kept, axis=1, keepdims=True), (8, 128))

    found = jnp.full((8, 128), -1, jnp.int32)
    for u in range(slots_ref.shape[0]):
        found = jnp.where(lane == slots_ref[u], u, found)
    inv_row[...] = found
    inv_copy.start()

    for copy in (j_copy, a_copy):
        copy(ch, across, 0).start()
        copy(ch, partner, 1).start()

    neighbour = (z * 2 + 1 - y) * slots_per

    def pass_b(k):
        s = neighbour + first_a + k
        came(wall.at[s], w_recv.at[s])
        both_ways(s)

    loop(last_b, pass_b)
    for i in range(2):
        x_relay(0, i)

    def relay_head(t):
        h_copy(t, across, across, 0).wait_recv()
        h_copy(t, across, partner, 2).start()

    def line_in(d, c):
        def source(zz):
            row = jnp.where(c < slots_per, y, 1 - y)
            return (zz * 2 + row) * slots_per + jnp.where(c < slots_per, c, c - last_b)

        @pl.when(z - d >= 0)
        def _():
            s = source(z - d)
            came(wall.at[s], w_recv.at[s])

            @pl.when(has_right)
            def _():
                to_right(s).start()

            @pl.when(c < first_a)
            def _():
                to_other(s).start()

        @pl.when(z + d < nz)
        def _():
            s = source(z + d)
            came(wall.at[s], w_recv.at[s])

            @pl.when(has_left)
            def _():
                to_left(s).start()

            @pl.when(c < first_a)
            def _():
                to_other(s).start()

    def first_step(c):
        pl.when(c < slots_per + last_b)(lambda: line_in(1, c))
        pl.when(c < TASKS)(lambda: relay_head(c))

    loop(max(slots_per + last_b, TASKS), first_step)
    for copy in (j_copy, a_copy):
        copy(across, across, 0).wait_recv()
        copy(across, partner, 2).start()

    inv_copy.wait()

    def transpose_layer(l):
        for c in range(4):
            xt[l, c // 2, (c % 2) * 128 : (c % 2) * 128 + 128, :] = xs[l, c].T

    for i in range(2):
        x_arrive(0, i)
    transpose_layer(0)

    loop(nz - 2, lambda d: loop(slots_per + last_b, lambda c: line_in(d + 2, c)))

    def last_in(zz):
        def block(k):
            s = (zz * 2 + 1 - y) * slots_per + k
            came(wall.at[s], w_recv.at[s])

        loop(first_a, block)

    loop(nz, last_in)

    loop(n - 1, lambda i: c_copy(i).start())

    def conv_forward(l, i):
        rows = pl.ds(pl.multiple_of(i * IMG, IMG), IMG)
        left_side = jnp.concatenate([xs[l, c, rows, :] for c in range(4)], axis=1)
        zacc[...] = jnp.zeros_like(zacc)
        for first in range(0, 9, 2):
            taps = [t for t in (first, first + 1) if t < 9]
            sides = [
                jnp.concatenate([wall[slots_ref[(l * 9 + t) * 2 + h]] for h in range(2)], axis=0)
                for t in taps
            ]
            side = jnp.concatenate(sides, axis=1) if len(sides) > 1 else sides[0]
            out = dot(left_side, side, NN)
            for k, t in enumerate(taps):
                a, e = divmod(t, 3)
                part = out[:, k * 128 : (k + 1) * 128]
                if a == 0:
                    zacc[e, W:IMG, :] += part[: IMG - W]
                elif a == 1:
                    zacc[e] += part
                else:
                    zacc[e, : IMG - W, :] += part[W:]
        linear = zacc[1]
        linear += jnp.where(col_id >= 1, pltpu.roll(zacc[0], 1, 0), 0.0)
        linear += jnp.where(col_id < W - 1, pltpu.roll(zacc[2], IMG - 1, 0), 0.0)
        inside = mask[rows, :]
        gain, shift = affine_ref[l, 0:1, :], affine_ref[l, 1:2, :]
        passed = jnp.where(linear > 0, inside, 0.0)
        coef[l, rows, :] = passed * gain if l < LAYERS - 1 else passed
        out = (jnp.maximum(linear, 0.0) * gain + shift) * inside
        xs[l + 1, ch, rows, :] = out.astype(BF16)

    def quarter(q):
        return pl.ds(pl.multiple_of(q * 128, 128), 128)

    for l in range(LAYERS):

        def forward_image(i, l=l):
            if l > 0:
                x_relay(l, i)
                x_arrive(l, i)
            conv_forward(l, i)
            if l < LAYERS - 1:
                x_start(l + 1, i)

        loop(2, forward_image)
        if 0 < l:
            transpose_layer(l)

    def f_copy(peer, k):
        return put(xs.at[LAYERS, ch, quarter(peer), :], fbuf.at[ch], f_send.at[k], f_recv.at[ch], at(chan=peer))

    peers = (across, far, partner)
    for k, peer in enumerate(peers):
        f_copy(peer, k).start()
    for i in range(2):
        x_start(LAYERS, i)
    fbuf[ch] = xs[LAYERS, ch, quarter(ch), :]

    loop(n - 1, lambda i: came(cnt.at[(me + i + 1) % n], c_recv.at[(me + i + 1) % n]))
    counts = lax.fori_loop(0, n, lambda i, acc: acc + cnt[i], jnp.zeros((8, 128), F32))
    counts = jnp.maximum(counts, 1.0)

    def head_in(t):
        h_copy(t, partner, partner, 1).wait_recv()
        h_copy(t, far, partner, 2).wait_recv()

    loop(TASKS, head_in)
    for copy in (j_copy, a_copy):
        copy(partner, partner, 1).wait_recv()
        copy(far, partner, 2).wait_recv()
    for peer in peers:
        came(fbuf.at[peer], f_recv.at[peer])

    weight = kept(ch) / counts
    losses[0] = weight
    losses[1] = jnp.zeros((8, 128), F32)
    features = jnp.concatenate([fbuf[c] for c in range(4)], axis=1)
    gfeat[...] = jnp.zeros_like(gfeat)
    klass = lax.broadcasted_iota(jnp.int32, (32, 128), 0)

    def q_copy(t, peer, k):
        rows = pl.ds(pl.multiple_of(peer * HC, HC), HC)
        return put(gh.at[t, rows, :], ghall.at[ch, t], q_send.at[0], q_recv.at[t, ch], at(chan=peer))

    def head_task(t):
        low = hall[t].reshape(4 * HC, C)
        both = jall[t].reshape(4 * HC, 128)
        join = both.astype(BF16)
        scale = both[:, 32:33]
        hidden = dot(low, features, NT)
        inverse = lax.rsqrt(jnp.sum(hidden * hidden, axis=0, keepdims=True) + eps_norm)
        normed = hidden * inverse
        scaled = (scale * normed).astype(BF16)
        logits = dot(join, scaled, TN)[0:32]
        real = klass < K
        largest = jnp.max(jnp.where(real, logits, -jnp.inf), axis=0, keepdims=True)
        shifted = jnp.where(real, jnp.exp(jnp.where(real, logits - largest, 0.0)), 0.0)
        totals = jnp.sum(shifted, axis=0, keepdims=True)
        onehot = klass == code_ref[ch, pl.ds(t, 1), :]
        picked = jnp.sum(jnp.where(onehot, logits, 0.0), axis=0, keepdims=True)
        share = losses[0, pl.ds(t, 1), :]
        losses[1, pl.ds(t, 1), :] = share * (largest + jnp.log(totals) - picked)
        slope = (share * (shifted / totals - jnp.where(onehot, 1.0, 0.0))).astype(BF16)
        grad_scaled = dot(join, jnp.concatenate([slope, jnp.zeros((96, 128), BF16)], axis=0), NN)
        jt[t, 0:24, :] = dot(slope, scaled, NT)[0:24]
        jt[t, 24:32, :] = dot(jnp.ones((8, 128), F32), grad_scaled * normed, NT, lax.Precision.HIGHEST)
        grad_normed = grad_scaled * scale
        along = jnp.sum(normed * grad_normed, axis=0, keepdims=True)
        grad_hidden = ((grad_normed - normed * along) * inverse).astype(BF16)
        gh[t] = grad_hidden
        for k, peer in enumerate(peers):
            q_copy(t, peer, k).start()
        gfeat[...] += dot(grad_hidden, low, TN)

    for t in range(TASKS):
        head_task(t)
    loss_tile = jnp.broadcast_to(jnp.sum(losses[1], axis=1, keepdims=True), (8, 128))
    jt[TASKS, 0:8, 0:128] = loss_tile
    jt[TASKS, 0:8, 128:256] = loss_tile

    my_mask = mask[quarter(ch), :]
    for c in range(4):
        gsend[c] = (gfeat[:, c * 128 : (c + 1) * 128] * my_mask * aall[c, 0:1, :]).astype(BF16)

    def g_copy(peer, k):
        return put(gsend.at[peer], grecv.at[ch], g_send.at[k], g_recv.at[ch], at(chan=peer))

    def s_copy(peer, k):
        return put(jsend.at[peer], jrecv.at[ch], s_send.at[k], s_recv.at[ch], at(chan=peer))

    for k, peer in enumerate(peers):
        g_copy(peer, k).start()
    for i in range(2):
        x_relay(LAYERS, i)
    grecv[ch] = gsend[ch]
    low_lane = lax.broadcasted_iota(jnp.int32, (32, 128), 1) < HC
    for c in range(4):
        side = slice((c // 2) * 128, (c // 2) * 128 + 128)
        for m in range(4):
            one, two = jt[2 * m, :, side], jt[2 * m + 1, :, side]
            if m == 3:
                two = jnp.where(lax.broadcasted_iota(jnp.int32, (32, 128), 0) < 8, two, 0.0)
            if c % 2 == 0:
                two = pltpu.roll(two, HC, 1)
            else:
                one = pltpu.roll(one, HC, 1)
            jsend[c, m] = jnp.where(low_lane, one, two)
    for k, peer in enumerate(peers):
        s_copy(peer, k).start()
    ghall[ch] = gh[:, pl.ds(pl.multiple_of(ch * HC, HC), HC), :]
    jrecv[ch] = jsend[ch]

    def spread(l, i, grad):
        columns = (
            jnp.where(col_id < W - 1, pltpu.roll(grad, IMG - 1, 0), 0.0),
            grad,
            jnp.where(col_id >= 1, pltpu.roll(grad, 1, 0), 0.0),
        )
        top = pl.multiple_of(i * TALL + W, W)
        for e in range(3):
            gs[l * 3 + e, pl.ds(top, IMG), :] = columns[e].astype(BF16)

    def shifted(l, t, i):
        a, e = divmod(t, 3) if isinstance(t, int) else (t // 3, t % 3)
        return gs[l * 3 + e, pl.ds(pl.multiple_of(i * TALL + (2 - a) * W, W), IMG), :]

    def tap_grad(l, t):
        return jnp.concatenate([shifted(l, t, 0), shifted(l, t, 1)], axis=0)

    def conv_backward(l, i, h):
        total = None
        for first in range(0, 9, 2):
            taps = [t for t in (first, first + 1) if t < 9]
            grads = [shifted(l, t, i) for t in taps]
            sides = [wall[slots_ref[(l * 9 + t) * 2 + h]] for t in taps]
            if len(taps) > 1:
                term = dot(jnp.concatenate(grads, axis=1), jnp.concatenate(sides, axis=1), NT)
            else:
                term = dot(grads[0], sides[0], NT)
            total = term if total is None else total + term
        bpart[l - 1, i, h, 0] = total[:, :128]
        bpart[l - 1, i, h, 1] = total[:, 128:]

    def bc_copy(l, i, h):
        return put(
            bpart.at[l - 1, i, h, 1 - core],
            bcore.at[l - 1, i, h],
            bc_send.at[l - 1, i, h],
            bc_recv.at[l - 1, i, h],
            at(chan=partner),
        )

    def bx_copy(l, i):
        return put(bxs.at[l - 1, i], bx.at[l - 1, i], bx_send.at[l - 1, i], bx_recv.at[l - 1, i], at(chan=across))

    def weight_grads(l):
        lhs = xt[l].reshape(C, PX)

        def pair(p):
            t = 2 * p
            rhs = jnp.concatenate([tap_grad(l, t), tap_grad(l, t + 1)], axis=1)
            out = dot(lhs, rhs, NN)
            for h in range(2):
                dw[(l * 9 + t) * 2 + h] = out[h * 256 : (h + 1) * 256, :128]
                dw[(l * 9 + t + 1) * 2 + h] = out[h * 256 : (h + 1) * 256, 128:]

        loop(4, pair)
        out = dot(lhs, tap_grad(l, 8), NN)
        for h in range(2):
            dw[(l * 9 + 8) * 2 + h] = out[h * 256 : (h + 1) * 256]

    def l_copy(i):
        dev = (me + i + 1) % n
        return put(losses.at[2 + me], losses.at[2 + me], l_send.at[0], l_recv.at[me], at(dp=dev))

    def head_part(dest):
        rows = hg[pl.ds(pl.multiple_of(dest * piece, 16), piece), :]
        return rows, small[pl.ds(pl.multiple_of(dest * SMALL, SMALL), SMALL), :]

    def write(ref, values):
        codes, powers = encode(values)
        ref[0:256, :] = codes
        ref[256:272, :] = powers

    def read(ref):
        return decode(ref[0:256, :], ref[256:272, :])

    def write_head(ref, values):
        codes, powers = encode(values[0])
        ref[0:piece, :] = codes
        ref[piece : piece + 16, :] = powers
        codes, powers = encode(values[1])
        ref[piece + 16 : piece + 32, :] = codes
        ref[piece + 32 : piece + 48, :] = powers

    def read_head(ref):
        one = decode(ref[0:piece, :], ref[piece : piece + 16, :])
        return one, decode(ref[piece + 16 : piece + 32, :], ref[piece + 32 : piece + 48, :])

    def p_copy(i):
        dest = (me + i + 1) % n
        return put(psend.at[dest], precv.at[me], p_send.at[0], p_recv.at[me], at(dp=dest))

    def head_grads():
        for i in range(2):
            x_arrive(LAYERS, i)
        for peer in peers:
            loop(TASKS, lambda t, peer=peer: came(ghall.at[peer, t], q_recv.at[t, peer]))
            came(jrecv.at[peer], s_recv.at[peer])
        lhs = [
            jnp.concatenate([ghall[2 * m].reshape(TASKS * HC, 128), ghall[2 * m + 1].reshape(TASKS * HC, 128)], axis=1)
            for m in range(2)
        ]
        for c in range(0, 4, 2):
            total = None
            for m in range(2):
                rows = slice(m * IMG, (m + 1) * IMG)
                rhs = jnp.concatenate([xs[LAYERS, c, rows, :], xs[LAYERS, c + 1, rows, :]], axis=1)
                term = dot(lhs[m], rhs, NN)
                total = term if total is None else total + term
            hg[c * 448 : (c + 1) * 448, :] = total[:, :128]
            hg[(c + 1) * 448 : (c + 2) * 448, :] = total[:, 128:]
        if hg.shape[0] > 1792:
            hg[1792:, :] = jnp.zeros((hg.shape[0] - 1792, 128), F32)
        small[...] = jnp.zeros_like(small)
        for m in range(4):
            small[m * 32 : (m + 1) * 32, :] = jrecv[0, m] + jrecv[1, m] + jrecv[2, m] + jrecv[3, m]
        losses[2 + me] = small[96:104, :]


        def give(i):
            dest = (me + i + 1) % n
            write_head(psend.at[dest], head_part(dest))
            p_copy(i).start()

        loop(n - 1, give)
        loop(n - 1, lambda i: l_copy(i).start())

    for peer in peers:
        came(grecv.at[peer], g_recv.at[peer])

    def top_grad(i):
        rows = pl.ds(pl.multiple_of(i * IMG, IMG), IMG)
        grad = jnp.concatenate([grecv[2 * i], grecv[2 * i + 1]], axis=0).astype(F32)
        spread(LAYERS - 1, i, grad * coef[LAYERS - 1, rows, :])

    loop(2, top_grad)
    x_side = ch // 2
    for l in (2, 1):

        def partial_image(i, h, l=l):
            conv_backward(l, i, h)
            bc_copy(l, i, h).start()

        def chip_sum(i, l=l):
            bc_copy(l, i, 1 - x_side).wait_recv()
            bxs[l - 1, i] = (bpart[l - 1, i, 1 - x_side, core] + bcore[l - 1, i, 1 - x_side]).astype(BF16)
            bx_copy(l, i).start()

        loop(2, lambda i: partial_image(i, 1 - x_side))
        loop(2, chip_sum)
        loop(2, lambda i: partial_image(i, x_side))
        if l == LAYERS - 1:
            head_grads()
        else:
            weight_grads(LAYERS - 1)
            weight_grads(l)

        def finish_image(i, l=l):
            bx_copy(l, i).wait_recv()
            bc_copy(l, i, x_side).wait_recv()
            grad = bpart[l - 1, i, x_side, core] + bcore[l - 1, i, x_side] + bx[l - 1, i].astype(F32)
            rows = pl.ds(pl.multiple_of(i * IMG, IMG), IMG)
            spread(l - 1, i, grad * coef[l - 1, rows, :])

        loop(2, finish_image)
    weight_grads(0)

    def part(dest, k):
        u = inv_ref[0, dest * slots_per + k]
        return dw[jnp.maximum(u, 0)] * jnp.where(u >= 0, 1.0, 0.0)

    def y_copy(zz, k):
        return put(ysend.at[zz, k], yrecv.at[zz, k], y_send.at[0], y_recv.at[zz, k], other)

    def z_right(zz, k):
        return put(lsend.at[zz, k], lleft.at[zz, k], z_send.at[0], zl_recv.at[zz, k], right)

    def z_left(zz, k):
        return put(lsend.at[zz, k], lright.at[zz, k], z_send.at[0], zr_recv.at[zz, k], left)

    def both_sides(d, body):
        for zz, ok in ((z - d, z - d >= 0), (z + d, z + d < nz)):

            @pl.when(ok)
            def _(zz=zz):
                body(zz)

    def cross(zz):
        dest = zz * 2 + 1 - y

        def block(k):
            write(ysend.at[zz, k], part(dest, k))
            y_copy(zz, k).start()

        loop(first_r, block)

    def pass_on(zz, k):
        @pl.when(zz > z)
        def _():
            z_right(zz, k).start()

        @pl.when(zz < z)
        def _():
            z_left(zz, k).start()

    def line_conv(zz, k):
        is_a, is_own = k < first_r, k < slots_per
        dest = zz * 2 + jnp.where(is_own, y, 1 - y)
        slot = jnp.where(is_own, k, k - last_r)
        zsum[...] = part(dest, slot)

        @pl.when(is_a)
        def _():
            came(yrecv.at[zz, k], y_recv.at[zz, k])
            zsum[...] += read(yrecv.at[zz, k])

        @pl.when((zz >= z) & has_left)
        def _():
            came(lleft.at[zz, k], zl_recv.at[zz, k])
            zsum[...] += read(lleft.at[zz, k])

        @pl.when((zz <= z) & has_right)
        def _():
            came(lright.at[zz, k], zr_recv.at[zz, k])
            zsum[...] += read(lright.at[zz, k])

    def tag(j):
        return hag.at[j]

    def t_right(j):
        return put(tag(j), tag(j), t_zr.at[0], t_recv.at[j], right)

    def t_left(j):
        return put(tag(j), tag(j), t_zl.at[0], t_recv.at[j], left)

    def t_other(j):
        return put(tag(j), tag(j), t_y.at[0], t_recv.at[j], other)

    def both_tags(j):
        @pl.when(has_right)
        def _():
            t_right(j).start()

        @pl.when(has_left)
        def _():
            t_left(j).start()

    def sum_head():
        rows, few = head_part(me)
        zsum[0:piece, :] = rows
        zsum[piece : piece + SMALL, :] = few

        def add_piece(i):
            source = (me + i + 1) % n
            came(precv.at[source], p_recv.at[source])
            one, two = read_head(precv.at[source])
            zsum[0:piece, :] += one
            zsum[piece : piece + SMALL, :] += two

        loop(n - 1, add_piece)
        write_head(hag.at[me], (zsum[0:piece, :], zsum[piece : piece + SMALL, :]))
        t_other(me).start()
        both_tags(me)

    both_sides(nz - 1, cross)
    sum_head()
    loop(nz - 2, lambda i: both_sides(nz - 2 - i, cross))
    cross(z)
    neighbour_tag = z * 2 + 1 - y

    def tail(d):
        for row in range(2):

            @pl.when(z - d >= 0)
            def _(row=row):
                j = (z - d) * 2 + row
                came(tag(j), t_recv.at[j])
                pl.when(has_right)(lambda: t_right(j).start())

            @pl.when(z + d < nz)
            def _(row=row):
                j = (z + d) * 2 + row
                came(tag(j), t_recv.at[j])
                pl.when(has_left)(lambda: t_left(j).start())

    def out_step(i):
        d = nz - 1 - i

        def item(c):
            k = (c + first_r) % cargo

            def send(zz):
                line_conv(zz, k)
                write(lsend.at[zz, k], zsum[...])
                pass_on(zz, k)

            both_sides(d, send)

        loop(cargo, item)

        @pl.when(i == 0)
        def _():
            came(tag(neighbour_tag), t_recv.at[neighbour_tag])
            both_tags(neighbour_tag)

        pl.when(i > 0)(lambda: tail(i))

    loop(nz - 1, out_step)

    def b_copy(k):
        return put(bsend2.at[k], brecv2.at[k], b_send.at[k], b_recv.at[k], other)

    def give_b(k):
        line_conv(z, slots_per + k)
        write(bsend2.at[k], zsum[...])
        b_copy(k).start()

    loop(last_r, give_b)

    def own_slot(k):
        line_conv(z, k)
        grad_out[k] = zsum[...]

    tail(nz - 1)
    per = 448 // piece

    def unpack(j):
        one, two = read_head(hag.at[j])

        @pl.when(j < 4 * per)
        def _():
            rows = pl.ds(pl.multiple_of((j % per) * piece, 16), piece)
            head_out[rows, pl.ds(pl.multiple_of((j // per) * 128, 128), 128)] = one

        @pl.when(j < 8)
        def _():
            small[pl.ds(pl.multiple_of(j * SMALL, SMALL), SMALL), :] = two

    loop(n, unpack)
    for m in range(4):
        pair = small[m * 32 : (m + 1) * 32, :]
        small_out[2 * m] = pair
        small_out[2 * m + 1] = pltpu.roll(pair, HC, 1)

    loop(first_r, own_slot)

    loop(n - 1, lambda i: came(losses.at[2 + (me + i + 1) % n], l_recv.at[(me + i + 1) % n]))
    loss_tile = lax.fori_loop(0, n, lambda i, acc: acc + losses[2 + i], jnp.zeros((8, 128), F32))
    loss_out[0] = jnp.sum(loss_tile[:TASKS, HC : HC + 1])

    def own_last(k):
        line_conv(z, first_r + k)
        came(brecv2.at[k], b_recv.at[k])
        grad_out[first_r + k] = zsum[...] + read(brecv2.at[k])

    loop(last_r, own_last)

    line = slots_per + last_b

    def left_line(zz):
        @pl.when((z == zz) & has_right)
        def _():
            left_it(wall.at[pl.ds(0, (zz + 1) * line)], w_zr.at[0])
            left_it(hag.at[pl.ds(0, (zz + 1) * 2)], t_zr.at[0])

        @pl.when((z == zz) & has_left)
        def _():
            left_it(wall.at[pl.ds(0, (nz - zz) * line)], w_zl.at[0])
            left_it(hag.at[pl.ds(0, (nz - zz) * 2)], t_zl.at[0])

    for zz in range(nz):
        left_line(zz)
    left_it(wall.at[pl.ds(0, nz * first_a + last_b)], w_y.at[0])
    left_it(hag.at[0], t_y.at[0])
    left_it(ysend, y_send.at[0])
    left_it(lsend.at[pl.ds(0, nz - 1)], z_send.at[0])
    loop(last_r, lambda k: b_copy(k).wait_send())
    left_it(xs.at[pl.ds(0, LAYERS)], x_send.at[0])
    left_it(hall.at[:, pl.ds(0, 3)], h_send.at[0])
    left_it(ghall.at[pl.ds(0, 3)], q_send.at[0])
    left_it(cnt.at[pl.ds(0, n - 1)], c_send.at[0])
    left_it(losses.at[pl.ds(0, n - 1)], l_send.at[0])
    left_it(psend.at[pl.ds(0, n - 1)], p_send.at[0])
    for k in range(3):
        j_copy(ch, partner, k).wait_send()
        a_copy(ch, partner, k).wait_send()
    for k, peer in enumerate(peers):
        f_copy(peer, k).wait_send()
        g_copy(peer, k).wait_send()
        s_copy(peer, k).wait_send()
    for l in (1, 2):
        for i in range(2):
            for h in range(2):
                bc_copy(l, i, h).wait_send()
            bx_copy(l, i).wait_send()


def adamw(weight, gradient, moment_one, moment_two, step_rate, one_over, two_over):
    moment_one = beta_one * moment_one + (1.0 - beta_one) * gradient
    moment_two = beta_two * moment_two + (1.0 - beta_two) * gradient * gradient
    first_hat = moment_one * one_over
    second_hat = moment_two * two_over
    weight = weight - step_rate * (
        first_hat / (jnp.sqrt(second_hat) + eps_adam) + decay_rate * weight
    )
    return (weight, moment_one, moment_two)


def update(
    over_ref,
    conv_g,
    conv_w,
    conv_m,
    conv_v,
    head_g,
    head_w,
    head_m,
    head_v,
    small_g,
    join_w,
    join_m,
    join_v,
    scale_w,
    scale_m,
    scale_v,
    conv_out,
    conv_out_m,
    conv_out_v,
    head_out,
    head_out_m,
    head_out_v,
    join_out,
    join_out_m,
    join_out_v,
    scale_out,
    scale_out_m,
    scale_out_v,
):
    one_over, two_over = over_ref[0], over_ref[1]

    def put_all(outs, values):
        for out, value in zip(outs, values):
            out[...] = value

    conv = adamw(conv_w[...], conv_g[...], conv_m[...], conv_v[...], 0.01, one_over, two_over)
    put_all((conv_out, conv_out_m, conv_out_v), conv)
    head = adamw(head_w[...], head_g[...], head_m[...], head_v[...], 0.03, one_over, two_over)
    put_all((head_out, head_out_m, head_out_v), head)

    @pl.when(pl.program_id(0) == 0)
    def _():
        join_g = small_g[:TASKS, :K, :HC]
        join = adamw(join_w[...], join_g, join_m[...], join_v[...], 0.4, one_over, two_over)
        put_all((join_out, join_out_m, join_out_v), join)
        scale_g = jnp.concatenate([small_g[t, 24:25, :HC] for t in range(TASKS)], axis=0)
        scale = adamw(scale_w[...], scale_g, scale_m[...], scale_v[...], 0.8, one_over, two_over)
        put_all((scale_out, scale_out_m, scale_out_v), scale)


def per_device(
    n,
    inputs,
    affine,
    image_sizes,
    labels,
    label_mask,
    unit_slots,
    conv_master,
    conv_first,
    conv_second,
    head_master,
    head_first,
    head_second,
    join_master,
    join_first,
    join_second,
    scale_master,
    scale_first,
    scale_second,
    step_count,
):
    slots_per = conv_master.shape[0]
    nz = n // 2
    last_r = slots_per // 7
    first_r = slots_per - last_r
    cargo = slots_per + last_r
    piece = -(-1792 // (n * 16)) * 16
    vm, dma = pltpu.VMEM, pltpu.SemaphoreType.DMA
    shape = jax.ShapeDtypeStruct
    scratch = [
        vm((slots_per, 256, 128), F32),
        vm((TASKS, HC, C), F32),
        vm((8, 128), jnp.int32),
        pltpu.SMEM((8, 128), jnp.int32),
        vm((4, 8, 128), jnp.int32),
        vm((128, 128), F32),
        vm((n * slots_per, 256, 128), BF16),
        vm((LAYERS + 1, 4, PX, 128), BF16),
        vm((LAYERS, 2, 256, PX), BF16),
        vm((TASKS, 4, HC, C), BF16),
        vm((TASKS, 4, HC, 128), F32),
        vm((4, 8, 128), F32),
        vm((n, 8, 128), F32),
        vm((n + 2, 8, 128), F32),
        vm((PX, 128), F32),
        vm((LAYERS, PX, 128), F32),
        vm((3, IMG, 128), F32),
        vm((4, 128, 128), BF16),
        vm((TASKS, 256, 128), BF16),
        vm((4, TASKS, HC, 128), BF16),
        vm((128, C), F32),
        vm((4, 128, 128), BF16),
        vm((4, 128, 128), BF16),
        vm((8, 32, 256), F32),
        vm((4, 4, 32, 128), F32),
        vm((4, 4, 32, 128), F32),
        vm((9, 2 * TALL, 128), BF16),
        vm((2, 2, 2, 2, IMG, 128), F32),
        vm((2, 2, 2, IMG, 128), F32),
        vm((2, 2, IMG, 128), BF16),
        vm((2, 2, IMG, 128), BF16),
        vm((54, 256, 128), F32),
        vm((n * piece, 128), F32),
        vm((n * SMALL, 128), F32),
        vm((n, piece + 48, 128), jnp.int16),
        vm((n, piece + 48, 128), jnp.int16),
        vm((nz, first_r, CHUNK, 128), jnp.int16),
        vm((nz, first_r, CHUNK, 128), jnp.int16),
        vm((nz, cargo, CHUNK, 128), jnp.int16),
        vm((nz, cargo, CHUNK, 128), jnp.int16),
        vm((nz, cargo, CHUNK, 128), jnp.int16),
        vm((max(last_r, 1), CHUNK, 128), jnp.int16),
        vm((max(last_r, 1), CHUNK, 128), jnp.int16),
        vm((n, piece + 48, 128), jnp.int16),
        vm((256, 128), F32),
        dma((slots_per + 2,)),
        dma((n * slots_per,)),
        *[dma((1,)) for _ in range(3)],
        dma((1,)), dma((LAYERS + 1, 2, 3)),
        dma((1,)), dma((TASKS, 3)),
        *[dma((3,)) for _ in range(4)],
        dma((1,)), dma((n,)),
        dma((1,)), dma((n,)),
        dma((3,)), dma((4,)),
        dma((3,)), dma((4,)),
        dma((1,)), dma((TASKS, 4)),
        dma((1,)), dma((n,)),
        dma((3,)), dma((4,)),
        *[dma((2, 2, 2)) for _ in range(2)],
        *[dma((2, 2)) for _ in range(2)],
        dma((1,)), dma((nz, first_r)),
        dma((1,)), dma((nz, cargo)), dma((nz, cargo)),
        *[dma((max(last_r, 1),)) for _ in range(2)],
        dma((n,)),
        *[dma((1,)) for _ in range(3)],
    ]
    in_smem, in_vmem = pl.BlockSpec(memory_space=pltpu.SMEM), pl.BlockSpec(memory_space=pltpu.VMEM)
    in_hbm = pl.BlockSpec(memory_space=pltpu.HBM)
    slot_grads, head_total, small_total, loss = pl.pallas_call(
        functools.partial(kernel, n, slots_per),
        out_shape=(
            shape((slots_per, 256, 128), F32),
            shape((448, C), F32),
            shape((8, 32, 128), F32),
            shape((1,), F32),
        ),
        in_specs=[in_smem] * 2 + [in_vmem] * 6 + [in_hbm] * 2,
        out_specs=(in_vmem,) * 3 + (in_smem,),
        scratch_shapes=scratch,
        compiler_params=pltpu.CompilerParams(
            collective_id=0, has_side_effects=True, vmem_limit_bytes=VMEM_MIB * 2**20
        ),
    )(
        unit_slots,
        image_sizes,
        inputs.reshape(PX, 128),
        affine,
        labels.transpose(0, 3, 1, 2),
        label_mask.transpose(0, 3, 1, 2),
        join_master.transpose(0, 2, 1),
        scale_master,
        conv_master,
        head_master,
    )
    step_float = step_count.astype(F32)
    over = jnp.concatenate([1.0 / (1.0 - beta_one**step_float), 1.0 / (1.0 - beta_two**step_float)])
    conv_rows, head_rows = slots_per * 256, TASKS * HC
    steps = STEPS

    def tile(rows, columns):
        return pl.BlockSpec((rows // steps, columns), lambda i: (i, 0))

    def whole(*sizes):
        return pl.BlockSpec(sizes, lambda i: (0,) * len(sizes))

    conv_tile, head_tile = tile(conv_rows, 128), tile(head_rows, C)
    join_tile, scale_tile = whole(TASKS, K, HC), whole(TASKS, HC)
    flat_conv = [a.reshape(conv_rows, 128) for a in (slot_grads, conv_master, conv_first, conv_second)]
    flat_head = [a.reshape(head_rows, C) for a in (head_total, head_master, head_first, head_second)]
    flat_join = [a.transpose(0, 2, 1) for a in (join_master, join_first, join_second)]
    out = pl.pallas_call(
        update,
        grid=(steps,),
        out_shape=tuple(
            [shape((conv_rows, 128), F32)] * 3
            + [shape((head_rows, C), F32)] * 3
            + [shape((TASKS, K, HC), F32)] * 3
            + [shape((TASKS, HC), F32)] * 3
        ),
        in_specs=[in_smem]
        + [conv_tile] * 4
        + [head_tile] * 4
        + [whole(8, 32, 128)]
        + [join_tile] * 3
        + [scale_tile] * 3,
        out_specs=tuple([conv_tile] * 3 + [head_tile] * 3 + [join_tile] * 3 + [scale_tile] * 3),
    )(over, *flat_conv, *flat_head, small_total, *flat_join, scale_master, scale_first, scale_second)
    conv_out = tuple(a.reshape(slots_per, 256, 128) for a in out[0:3])
    head_out = tuple(a.reshape(TASKS, HC, C) for a in out[3:6])
    join_out = tuple(a.transpose(0, 2, 1) for a in out[6:9])
    return (loss,) + conv_out + head_out + join_out + tuple(out[9:12])


def solution(mesh):
    placed = (
        P("dp", None, None, "chan"),
        P(None, None, "chan"),
        P("dp", None),
        P("dp", None, None, None),
        P("dp", None, None, None),
        P(),
        P("dp", None, "chan"),
        P("dp", None, "chan"),
        P("dp", None, "chan"),
        P(None, "chan", None),
        P(None, "chan", None),
        P(None, "chan", None),
        P(None, "chan", None),
        P(None, "chan", None),
        P(None, "chan", None),
        P(None, "chan"),
        P(None, "chan"),
        P(None, "chan"),
        P(),
    )
    return jax.shard_map(
        functools.partial(per_device, mesh.shape["dp"]),
        mesh=mesh,
        in_specs=placed,
        out_specs=(P(),) + placed[6:18],
        check_vma=False,
    )
```

```python
import functools
import math

import jax
import jax.numpy as jnp
from jax import lax
from jax.experimental import pallas as pl
from jax.experimental.pallas import tpu as pltpu
from jax.sharding import PartitionSpec as P

C = 512
K = 21
TASKS = 7
LAYERS = 3
H = 16
W = 16
PX = 512
IMG = 256
TALL = IMG + 2 * W
HC = 64
CHUNK = 272
VMEM_MIB = 60
STEPS = 2
SMALL = 16

beta_one = 0.9
beta_two = 0.999
eps_adam = 1e-08
decay_rate = 0.01
eps_norm = 1e-06

F32 = jnp.float32
BF16 = jnp.bfloat16
MESH = pl.DeviceIdType.MESH
NN = (((1,), (0,)), ((), ()))
NT = (((1,), (1,)), ((), ()))
TN = (((0,), (0,)), ((), ()))


def dot(a, b, dims, precision=None):
    return lax.dot_general(a, b, dims, precision=precision, preferred_element_type=F32)


def encode(values):
    top = jnp.max(jnp.abs(values), axis=0, keepdims=True)
    power = jnp.ceil(jnp.log2(jnp.maximum(top, 1e-30))) - 14.0
    codes = jnp.round(values * jnp.exp2(-power)).astype(jnp.int32).astype(jnp.int16)
    powers = jnp.broadcast_to(power, (16, 128)).astype(jnp.int32).astype(jnp.int16)
    return codes, powers


def decode(codes, powers):
    return codes.astype(F32) * jnp.exp2(powers.astype(F32)[0:1])


def kernel(
    n,
    slots_per,
    slots_ref,
    sizes_ref,
    inputs_ref,
    affine_ref,
    labels_ref,
    kept_ref,
    join_ref,
    scale_ref,
    conv_ref,
    head_ref,
    grad_out,
    head_out,
    small_out,
    loss_out,
    conv_in,
    head_in_ref,
    inv_row,
    inv_ref,
    code_ref,
    flip,
    wall,
    xs,
    xt,
    hall,
    jall,
    aall,
    cnt,
    losses,
    mask,
    coef,
    zacc,
    fbuf,
    gh,
    ghall,
    gfeat,
    gsend,
    grecv,
    jt,
    jsend,
    jrecv,
    gs,
    bpart,
    bcore,
    bx,
    bxs,
    dw,
    hg,
    small,
    psend,
    precv,
    ysend,
    yrecv,
    lsend,
    lright,
    lleft,
    bsend2,
    brecv2,
    hag,
    zsum,
    in_sem,
    w_recv,
    w_zr,
    w_zl,
    w_y,
    x_send,
    x_recv,
    h_send,
    h_recv,
    j_send,
    j_recv,
    a_send,
    a_recv,
    c_send,
    c_recv,
    l_send,
    l_recv,
    f_send,
    f_recv,
    g_send,
    g_recv,
    q_send,
    q_recv,
    p_send,
    p_recv,
    s_send,
    s_recv,
    bc_send,
    bc_recv,
    bx_send,
    bx_recv,
    y_send,
    y_recv,
    z_send,
    zr_recv,
    b_send,
    b_recv,
    t_recv,
    t_zr,
    t_zl,
    t_y,
):
    nz = n // 2
    last_b = slots_per // 7
    first_a = slots_per - last_b
    last_r = slots_per // 7
    first_r = slots_per - last_r
    cargo = slots_per + last_r
    piece = hg.shape[0] // n

    me = lax.axis_index("dp")
    ch = lax.axis_index("chan")
    z, y = me // 2, me % 2
    core = ch % 2
    partner = ch + 1 - 2 * core
    across = (ch + 2) % 4
    far = (partner + 2) % 4

    def at(dp=None, chan=None):
        return {"dp": me if dp is None else dp, "chan": ch if chan is None else chan}

    right, left, other = at(dp=me + 2), at(dp=me - 2), at(dp=z * 2 + 1 - y)
    has_right, has_left = z < nz - 1, z > 0

    def put(src, dst, send, recv, dev):
        return pltpu.make_async_remote_copy(
            src_ref=src, dst_ref=dst, send_sem=send, recv_sem=recv, device_id=dev, device_id_type=MESH
        )

    def came(ref, recv):
        put(ref, ref, recv, recv, other).wait_recv()

    def left_it(ref, send):
        put(ref, ref, send, send, other).wait_send()

    def loop(count, body):
        lax.fori_loop(0, count, lambda i, c: (body(i), c)[1], 0)

    def conv_copy(k):
        return pltpu.make_async_copy(conv_ref.at[k], conv_in.at[k], in_sem.at[k])

    head_copy = pltpu.make_async_copy(head_ref, head_in_ref, in_sem.at[slots_per])
    inv_copy = pltpu.make_async_copy(inv_row, inv_ref, in_sem.at[slots_per + 1])
    loop(slots_per, lambda k: conv_copy(k).start())
    head_copy.start()
    barrier = pltpu.get_barrier_semaphore()

    for peer in (partner, across, far):
        pl.semaphore_signal(barrier, inc=1, device_id=at(chan=peer), device_id_type=MESH)
    pl.semaphore_signal(barrier, inc=1, device_id=other, device_id_type=MESH)

    @pl.when(has_right)
    def _():
        pl.semaphore_signal(barrier, inc=1, device_id=right, device_id_type=MESH)

    @pl.when(has_left)
    def _():
        pl.semaphore_signal(barrier, inc=1, device_id=left, device_id_type=MESH)

    def cast_block(k):
        conv_copy(k).wait()
        wall[me * slots_per + k] = conv_in[k].astype(BF16)

    loop(slots_per, cast_block)
    pl.semaphore_wait(barrier, 4 + jnp.where(has_right, 1, 0) + jnp.where(has_left, 1, 0))

    def to_right(s):
        return put(wall.at[s], wall.at[s], w_zr.at[0], w_recv.at[s], right)

    def to_left(s):
        return put(wall.at[s], wall.at[s], w_zl.at[0], w_recv.at[s], left)

    def to_other(s):
        return put(wall.at[s], wall.at[s], w_y.at[0], w_recv.at[s], other)

    def both_ways(s):
        @pl.when(has_right)
        def _():
            to_right(s).start()

        @pl.when(has_left)
        def _():
            to_left(s).start()

    def x_copy(l, i, owner, peer, k):
        rows = pl.ds(pl.multiple_of(i * IMG, IMG), IMG)
        ref = xs.at[l, owner, rows, :]
        return put(ref, ref, x_send.at[0], x_recv.at[l, i, k], at(chan=peer))

    def x_start(l, i):
        x_copy(l, i, ch, across, 0).start()
        x_copy(l, i, ch, partner, 1).start()

    def x_relay(l, i):
        x_copy(l, i, across, across, 0).wait_recv()
        x_copy(l, i, across, partner, 2).start()

    def x_arrive(l, i):
        x_copy(l, i, partner, partner, 1).wait_recv()
        x_copy(l, i, far, partner, 2).wait_recv()

    def h_copy(t, owner, peer, k):
        ref = hall.at[t, owner]
        return put(ref, ref, h_send.at[0], h_recv.at[k], at(chan=peer))

    def j_copy(owner, peer, k):
        ref = jall.at[:, owner]
        return put(ref, ref, j_send.at[k], j_recv.at[k], at(chan=peer))

    def a_copy(owner, peer, k):
        ref = aall.at[owner]
        return put(ref, ref, a_send.at[k], a_recv.at[k], at(chan=peer))

    def c_copy(i):
        dev = (me + i + 1) % n
        return put(cnt.at[me], cnt.at[me], c_send.at[0], c_recv.at[0], at(dp=dev))

    base = me * slots_per

    def own_b(k):
        to_other(base + first_a + k).start()

    loop(last_b, own_b)

    def own_a(k):
        both_ways(base + k)
        to_other(base + k).start()

    loop(first_a, own_a)
    loop(last_b, lambda k: both_ways(base + first_a + k))
    pixel = lax.broadcasted_iota(jnp.int32, (IMG, 128), 0)
    row_id, col_id = pixel // W, pixel % W

    def mask_image(i):
        inside = (row_id < sizes_ref[i, 0]) & (col_id < sizes_ref[i, 1])
        rows = pl.ds(pl.multiple_of(i * IMG, IMG), IMG)
        mask[rows, :] = jnp.where(inside, 1.0, 0.0)
        xs[0, ch, rows, :] = (inputs_ref[rows, :].astype(F32) * mask[rows, :]).astype(BF16)
        x_start(0, i)

    loop(2, mask_image)
    head_copy.wait()

    def cast_head(t):
        hall[t, ch] = head_in_ref[t].astype(BF16)
        h_copy(t, ch, across, 0).start()
        h_copy(t, ch, partner, 1).start()

    loop(TASKS, cast_head)
    for i in range(2):
        gs[:, i * TALL : i * TALL + W, :] = jnp.zeros((9, W, 128), BF16)
        gs[:, (i + 1) * TALL - W : (i + 1) * TALL, :] = jnp.zeros((9, W, 128), BF16)
    flip[...] = jnp.zeros_like(flip)
    for t in range(TASKS):
        flip[0:K, 0:HC] = join_ref[t]
        flip[32:33, 0:HC] = scale_ref[t : t + 1, :]
        jall[t, ch] = flip[...].T[0:HC]
    aall[ch] = jnp.broadcast_to(affine_ref[LAYERS - 1, 0:1, :], (8, 128))

    code = jnp.where(kept_ref[...] > 0, labels_ref[...], -1).astype(F32).astype(BF16).reshape(2 * TASKS * H, W)
    lane_row = lax.broadcasted_iota(jnp.int32, (W, 128), 1) % W == lax.broadcasted_iota(jnp.int32, (W, 128), 0)
    wide = dot(code, jnp.where(lane_row, 1.0, 0.0).astype(BF16), NN).reshape(4 * TASKS, 8, 128)
    own_row = lax.broadcasted_iota(jnp.int32, (1, 8, 128), 1) == lax.broadcasted_iota(jnp.int32, (1, 8, 128), 2) // W
    rows_of = jnp.sum(jnp.where(own_row, wide, 0.0), axis=1).astype(jnp.int32)
    code_ref[...] = jnp.full(code_ref.shape, -1, jnp.int32)
    for b in range(2):
        for t in range(TASKS):
            for half in range(2):
                place = (b * TASKS + t) * 2 + half
                code_ref[2 * b + half, t : t + 1, :] = rows_of[place : place + 1, :]

    lane = lax.broadcasted_iota(jnp.int32, (8, 128), 1)

    def kept(q):
        spot = (q % 2) * 128 + lane
        hit = (spot // W < sizes_ref[q // 2, 0]) & (spot % W < sizes_ref[q // 2, 1])
        return jnp.where(hit & (code_ref[q] >= 0), 1.0, 0.0)

    total_kept = kept(0) + kept(1) + kept(2) + kept(3)
    cnt[me] = jnp.broadcast_to(jnp.sum(total_kept, axis=1, keepdims=True), (8, 128))

    found = jnp.full((8, 128), -1, jnp.int32)
    for u in range(slots_ref.shape[0]):
        found = jnp.where(lane == slots_ref[u], u, found)
    inv_row[...] = found
    inv_copy.start()

    for copy in (j_copy, a_copy):
        copy(ch, across, 0).start()
        copy(ch, partner, 1).start()

    neighbour = (z * 2 + 1 - y) * slots_per

    def pass_b(k):
        s = neighbour + first_a + k
        came(wall.at[s], w_recv.at[s])
        both_ways(s)

    loop(last_b, pass_b)
    for i in range(2):
        x_relay(0, i)

    def relay_head(t):
        h_copy(t, across, partner, 2).start()

    def line_in(d, c):
        def source(zz):
            row = jnp.where(c < slots_per, y, 1 - y)
            return (zz * 2 + row) * slots_per + jnp.where(c < slots_per, c, c - last_b)

        @pl.when(z - d >= 0)
        def _():
            s = source(z - d)
            came(wall.at[s], w_recv.at[s])

            @pl.when(has_right)
            def _():
                to_right(s).start()

            @pl.when(c < first_a)
            def _():
                to_other(s).start()

        @pl.when(z + d < nz)
        def _():
            s = source(z + d)
            came(wall.at[s], w_recv.at[s])

            @pl.when(has_left)
            def _():
                to_left(s).start()

            @pl.when(c < first_a)
            def _():
                to_other(s).start()

    def first_step(c):
        line_in(1, c)

    loop(slots_per + last_b, first_step)
    came(hall.at[:, 0], h_recv.at[0])
    loop(TASKS, relay_head)
    for copy in (j_copy, a_copy):
        copy(across, across, 0).wait_recv()
        copy(across, partner, 2).start()

    inv_copy.wait()

    def transpose_layer(l):
        for c in range(4):
            xt[l, c // 2, (c % 2) * 128 : (c % 2) * 128 + 128, :] = xs[l, c].T

    for i in range(2):
        x_arrive(0, i)
    transpose_layer(0)

    loop(nz - 2, lambda d: loop(slots_per + last_b, lambda c: line_in(d + 2, c)))

    def last_in(zz):
        def block(k):
            s = (zz * 2 + 1 - y) * slots_per + k
            came(wall.at[s], w_recv.at[s])

        loop(first_a, block)

    loop(nz, last_in)

    loop(n - 1, lambda i: c_copy(i).start())

    def conv_forward(l, i):
        rows = pl.ds(pl.multiple_of(i * IMG, IMG), IMG)
        left_side = jnp.concatenate([xs[l, c, rows, :] for c in range(4)], axis=1)
        zacc[...] = jnp.zeros_like(zacc)
        for first in range(0, 9, 2):
            taps = [t for t in (first, first + 1) if t < 9]
            sides = [
                jnp.concatenate([wall[slots_ref[(l * 9 + t) * 2 + h]] for h in range(2)], axis=0)
                for t in taps
            ]
            side = jnp.concatenate(sides, axis=1) if len(sides) > 1 else sides[0]
            out = dot(left_side, side, NN)
            for k, t in enumerate(taps):
                a, e = divmod(t, 3)
                part = out[:, k * 128 : (k + 1) * 128]
                if a == 0:
                    zacc[e, W:IMG, :] += part[: IMG - W]
                elif a == 1:
                    zacc[e] += part
                else:
                    zacc[e, : IMG - W, :] += part[W:]
        linear = zacc[1]
        linear += jnp.where(col_id >= 1, pltpu.roll(zacc[0], 1, 0), 0.0)
        linear += jnp.where(col_id < W - 1, pltpu.roll(zacc[2], IMG - 1, 0), 0.0)
        inside = mask[rows, :]
        gain, shift = affine_ref[l, 0:1, :], affine_ref[l, 1:2, :]
        passed = jnp.where(linear > 0, inside, 0.0)
        coef[l, rows, :] = passed * gain if l < LAYERS - 1 else passed
        out = (jnp.maximum(linear, 0.0) * gain + shift) * inside
        xs[l + 1, ch, rows, :] = out.astype(BF16)

    def quarter(q):
        return pl.ds(pl.multiple_of(q * 128, 128), 128)

    for l in range(LAYERS):

        def forward_image(i, l=l):
            if l > 0:
                x_relay(l, i)
                x_arrive(l, i)
            conv_forward(l, i)
            if l < LAYERS - 1:
                x_start(l + 1, i)

        loop(2, forward_image)
        if 0 < l:
            transpose_layer(l)

    def f_copy(peer, k):
        return put(xs.at[LAYERS, ch, quarter(peer), :], fbuf.at[ch], f_send.at[k], f_recv.at[ch], at(chan=peer))

    peers = (across, far, partner)
    for k, peer in enumerate(peers):
        f_copy(peer, k).start()
    for i in range(2):
        x_start(LAYERS, i)
    fbuf[ch] = xs[LAYERS, ch, quarter(ch), :]

    came(cnt.at[pl.ds(0, n - 1)], c_recv.at[0])
    counts = lax.fori_loop(0, n, lambda i, acc: acc + cnt[i], jnp.zeros((8, 128), F32))
    counts = jnp.maximum(counts, 1.0)

    came(hall.at[:, 0], h_recv.at[1])
    came(hall.at[:, 0], h_recv.at[2])
    for copy in (j_copy, a_copy):
        copy(partner, partner, 1).wait_recv()
        copy(far, partner, 2).wait_recv()
    for peer in peers:
        came(fbuf.at[peer], f_recv.at[peer])

    weight = kept(ch) / counts
    losses[0] = weight
    losses[1] = jnp.zeros((8, 128), F32)
    features = jnp.concatenate([fbuf[c] for c in range(4)], axis=1)
    gfeat[...] = jnp.zeros_like(gfeat)
    klass = lax.broadcasted_iota(jnp.int32, (32, 128), 0)

    def q_copy(t, peer, k):
        rows = pl.ds(pl.multiple_of(peer * HC, HC), HC)
        return put(gh.at[t, rows, :], ghall.at[ch, t], q_send.at[0], q_recv.at[0], at(chan=peer))

    def head_task(t):
        low = hall[t].reshape(4 * HC, C)
        both = jall[t].reshape(4 * HC, 128)
        join = both.astype(BF16)
        scale = both[:, 32:33]
        hidden = dot(low, features, NT)
        inverse = lax.rsqrt(jnp.sum(hidden * hidden, axis=0, keepdims=True) + eps_norm)
        normed = hidden * inverse
        scaled = (scale * normed).astype(BF16)
        logits = dot(join, scaled, TN)[0:32]
        real = klass < K
        largest = jnp.max(jnp.where(real, logits, -jnp.inf), axis=0, keepdims=True)
        shifted = jnp.where(real, jnp.exp(jnp.where(real, logits - largest, 0.0)), 0.0)
        totals = jnp.sum(shifted, axis=0, keepdims=True)
        onehot = klass == code_ref[ch, pl.ds(t, 1), :]
        picked = jnp.sum(jnp.where(onehot, logits, 0.0), axis=0, keepdims=True)
        share = losses[0, pl.ds(t, 1), :]
        losses[1, pl.ds(t, 1), :] = share * (largest + jnp.log(totals) - picked)
        slope = (share * (shifted / totals - jnp.where(onehot, 1.0, 0.0))).astype(BF16)
        grad_scaled = dot(join, jnp.concatenate([slope, jnp.zeros((96, 128), BF16)], axis=0), NN)
        jt[t, 0:24, :] = dot(slope, scaled, NT)[0:24]
        jt[t, 24:32, :] = dot(jnp.ones((8, 128), F32), grad_scaled * normed, NT, lax.Precision.HIGHEST)
        grad_normed = grad_scaled * scale
        along = jnp.sum(normed * grad_normed, axis=0, keepdims=True)
        grad_hidden = ((grad_normed - normed * along) * inverse).astype(BF16)
        gh[t] = grad_hidden
        for k, peer in enumerate(peers):
            q_copy(t, peer, k).start()
        gfeat[...] += dot(grad_hidden, low, TN)

    for t in range(TASKS):
        head_task(t)
    loss_tile = jnp.broadcast_to(jnp.sum(losses[1], axis=1, keepdims=True), (8, 128))
    jt[TASKS, 0:8, 0:128] = loss_tile
    jt[TASKS, 0:8, 128:256] = loss_tile

    my_mask = mask[quarter(ch), :]
    for c in range(4):
        gsend[c] = (gfeat[:, c * 128 : (c + 1) * 128] * my_mask * aall[c, 0:1, :]).astype(BF16)

    def g_copy(peer, k):
        return put(gsend.at[peer], grecv.at[ch], g_send.at[k], g_recv.at[ch], at(chan=peer))

    def s_copy(peer, k):
        return put(jsend.at[peer], jrecv.at[ch], s_send.at[k], s_recv.at[ch], at(chan=peer))

    for k, peer in enumerate(peers):
        g_copy(peer, k).start()
    for i in range(2):
        x_relay(LAYERS, i)
    grecv[ch] = gsend[ch]
    low_lane = lax.broadcasted_iota(jnp.int32, (32, 128), 1) < HC
    for c in range(4):
        side = slice((c // 2) * 128, (c // 2) * 128 + 128)
        for m in range(4):
            one, two = jt[2 * m, :, side], jt[2 * m + 1, :, side]
            if m == 3:
                two = jnp.where(lax.broadcasted_iota(jnp.int32, (32, 128), 0) < 8, two, 0.0)
            if c % 2 == 0:
                two = pltpu.roll(two, HC, 1)
            else:
                one = pltpu.roll(one, HC, 1)
            jsend[c, m] = jnp.where(low_lane, one, two)
    for k, peer in enumerate(peers):
        s_copy(peer, k).start()
    ghall[ch] = gh[:, pl.ds(pl.multiple_of(ch * HC, HC), HC), :]
    jrecv[ch] = jsend[ch]

    def spread(l, i, grad):
        columns = (
            jnp.where(col_id < W - 1, pltpu.roll(grad, IMG - 1, 0), 0.0),
            grad,
            jnp.where(col_id >= 1, pltpu.roll(grad, 1, 0), 0.0),
        )
        top = pl.multiple_of(i * TALL + W, W)
        for e in range(3):
            gs[l * 3 + e, pl.ds(top, IMG), :] = columns[e].astype(BF16)

    def shifted(l, t, i):
        a, e = divmod(t, 3) if isinstance(t, int) else (t // 3, t % 3)
        return gs[l * 3 + e, pl.ds(pl.multiple_of(i * TALL + (2 - a) * W, W), IMG), :]

    def tap_grad(l, t):
        return jnp.concatenate([shifted(l, t, 0), shifted(l, t, 1)], axis=0)

    def conv_backward(l, i, h):
        total = None
        for first in range(0, 9, 2):
            taps = [t for t in (first, first + 1) if t < 9]
            grads = [shifted(l, t, i) for t in taps]
            sides = [wall[slots_ref[(l * 9 + t) * 2 + h]] for t in taps]
            if len(taps) > 1:
                term = dot(jnp.concatenate(grads, axis=1), jnp.concatenate(sides, axis=1), NT)
            else:
                term = dot(grads[0], sides[0], NT)
            total = term if total is None else total + term
        bpart[l - 1, i, h, 0] = total[:, :128]
        bpart[l - 1, i, h, 1] = total[:, 128:]

    def bc_copy(l, i, h):
        return put(
            bpart.at[l - 1, i, h, 1 - core],
            bcore.at[l - 1, i, h],
            bc_send.at[0],
            bc_recv.at[l - 1, i, h],
            at(chan=partner),
        )

    def bx_copy(l, i):
        return put(bxs.at[l - 1, i], bx.at[l - 1, i], bx_send.at[0], bx_recv.at[l - 1, i], at(chan=across))

    def weight_grads(l):
        lhs = xt[l].reshape(C, PX)

        def pair(p):
            t = 2 * p
            rhs = jnp.concatenate([tap_grad(l, t), tap_grad(l, t + 1)], axis=1)
            out = dot(lhs, rhs, NN)
            for h in range(2):
                dw[(l * 9 + t) * 2 + h] = out[h * 256 : (h + 1) * 256, :128]
                dw[(l * 9 + t + 1) * 2 + h] = out[h * 256 : (h + 1) * 256, 128:]

        loop(4, pair)
        out = dot(lhs, tap_grad(l, 8), NN)
        for h in range(2):
            dw[(l * 9 + 8) * 2 + h] = out[h * 256 : (h + 1) * 256]

    def l_copy(i):
        dev = (me + i + 1) % n
        return put(losses.at[2 + me], losses.at[2 + me], l_send.at[0], l_recv.at[0], at(dp=dev))

    def head_part(dest):
        rows = hg[pl.ds(pl.multiple_of(dest * piece, 16), piece), :]
        return rows, small[pl.ds(pl.multiple_of(dest * SMALL, SMALL), SMALL), :]

    def write(ref, values):
        codes, powers = encode(values)
        ref[0:256, :] = codes
        ref[256:272, :] = powers

    def read(ref):
        return decode(ref[0:256, :], ref[256:272, :])

    def write_head(ref, values):
        codes, powers = encode(values[0])
        ref[0:piece, :] = codes
        ref[piece : piece + 16, :] = powers
        codes, powers = encode(values[1])
        ref[piece + 16 : piece + 32, :] = codes
        ref[piece + 32 : piece + 48, :] = powers

    def read_head(ref):
        one = decode(ref[0:piece, :], ref[piece : piece + 16, :])
        return one, decode(ref[piece + 16 : piece + 32, :], ref[piece + 32 : piece + 48, :])

    def p_copy(i):
        dest = (me + i + 1) % n
        return put(psend.at[dest], precv.at[me], p_send.at[0], p_recv.at[0], at(dp=dest))

    def head_grads():
        for i in range(2):
            x_arrive(LAYERS, i)
        for peer in peers:
            came(jrecv.at[peer], s_recv.at[peer])
        came(ghall.at[pl.ds(0, 3)], q_recv.at[0])
        lhs = [
            jnp.concatenate([ghall[2 * m].reshape(TASKS * HC, 128), ghall[2 * m + 1].reshape(TASKS * HC, 128)], axis=1)
            for m in range(2)
        ]
        for c in range(0, 4, 2):
            total = None
            for m in range(2):
                rows = slice(m * IMG, (m + 1) * IMG)
                rhs = jnp.concatenate([xs[LAYERS, c, rows, :], xs[LAYERS, c + 1, rows, :]], axis=1)
                term = dot(lhs[m], rhs, NN)
                total = term if total is None else total + term
            hg[c * 448 : (c + 1) * 448, :] = total[:, :128]
            hg[(c + 1) * 448 : (c + 2) * 448, :] = total[:, 128:]
        if hg.shape[0] > 1792:
            hg[1792:, :] = jnp.zeros((hg.shape[0] - 1792, 128), F32)
        small[...] = jnp.zeros_like(small)
        for m in range(4):
            small[m * 32 : (m + 1) * 32, :] = jrecv[0, m] + jrecv[1, m] + jrecv[2, m] + jrecv[3, m]
        losses[2 + me] = small[96:104, :]


        def give(i):
            dest = (me + i + 1) % n
            write_head(psend.at[dest], head_part(dest))
            p_copy(i).start()

        loop(n - 1, give)
        loop(n - 1, lambda i: l_copy(i).start())

    for peer in peers:
        came(grecv.at[peer], g_recv.at[peer])

    def top_grad(i):
        rows = pl.ds(pl.multiple_of(i * IMG, IMG), IMG)
        grad = jnp.concatenate([grecv[2 * i], grecv[2 * i + 1]], axis=0).astype(F32)
        spread(LAYERS - 1, i, grad * coef[LAYERS - 1, rows, :])

    loop(2, top_grad)
    x_side = ch // 2
    for l in (2, 1):

        def partial_image(i, h, l=l):
            conv_backward(l, i, h)
            bc_copy(l, i, h).start()

        def chip_sum(i, l=l):
            bc_copy(l, i, 1 - x_side).wait_recv()
            bxs[l - 1, i] = (bpart[l - 1, i, 1 - x_side, core] + bcore[l - 1, i, 1 - x_side]).astype(BF16)
            bx_copy(l, i).start()

        loop(2, lambda i: partial_image(i, 1 - x_side))
        loop(2, chip_sum)
        loop(2, lambda i: partial_image(i, x_side))
        if l == LAYERS - 1:
            head_grads()
        else:
            weight_grads(LAYERS - 1)
            weight_grads(l)

        def finish_image(i, l=l):
            bx_copy(l, i).wait_recv()
            bc_copy(l, i, x_side).wait_recv()
            grad = bpart[l - 1, i, x_side, core] + bcore[l - 1, i, x_side] + bx[l - 1, i].astype(F32)
            rows = pl.ds(pl.multiple_of(i * IMG, IMG), IMG)
            spread(l - 1, i, grad * coef[l - 1, rows, :])

        loop(2, finish_image)
    weight_grads(0)

    def part(dest, k):
        u = inv_ref[0, dest * slots_per + k]
        return dw[jnp.maximum(u, 0)] * jnp.where(u >= 0, 1.0, 0.0)

    def y_copy(zz, k):
        return put(ysend.at[zz, k], yrecv.at[zz, k], y_send.at[0], y_recv.at[zz, k], other)

    def z_right(zz, k):
        return put(lsend.at[zz, k], lleft.at[zz, k], z_send.at[0], zr_recv.at[zz + 1, k], right)

    def z_left(zz, k):
        return put(lsend.at[zz, k], lright.at[zz, k], z_send.at[0], zr_recv.at[zz, k], left)

    def both_sides(d, body):
        for zz, ok in ((z - d, z - d >= 0), (z + d, z + d < nz)):

            @pl.when(ok)
            def _(zz=zz):
                body(zz)

    def cross(zz):
        dest = zz * 2 + 1 - y

        def block(k):
            write(ysend.at[zz, k], part(dest, k))
            y_copy(zz, k).start()

        loop(first_r, block)

    def pass_on(zz, k):
        @pl.when(zz > z)
        def _():
            z_right(zz, k).start()

        @pl.when(zz < z)
        def _():
            z_left(zz, k).start()

    def line_conv(zz, k):
        is_a, is_own = k < first_r, k < slots_per
        dest = zz * 2 + jnp.where(is_own, y, 1 - y)
        slot = jnp.where(is_own, k, k - last_r)
        zsum[...] = part(dest, slot)

        @pl.when(is_a)
        def _():
            came(yrecv.at[zz, k], y_recv.at[zz, k])
            zsum[...] += read(yrecv.at[zz, k])

        @pl.when((zz >= z) & has_left)
        def _():
            came(lleft.at[zz, k], zr_recv.at[zz + 1, k])
            zsum[...] += read(lleft.at[zz, k])

        @pl.when((zz <= z) & has_right)
        def _():
            came(lright.at[zz, k], zr_recv.at[zz, k])
            zsum[...] += read(lright.at[zz, k])

    def tag(j):
        return hag.at[j]

    def t_right(j):
        return put(tag(j), tag(j), t_zr.at[0], t_recv.at[j], right)

    def t_left(j):
        return put(tag(j), tag(j), t_zl.at[0], t_recv.at[j], left)

    def t_other(j):
        return put(tag(j), tag(j), t_y.at[0], t_recv.at[j], other)

    def both_tags(j):
        @pl.when(has_right)
        def _():
            t_right(j).start()

        @pl.when(has_left)
        def _():
            t_left(j).start()

    def sum_head():
        rows, few = head_part(me)
        zsum[0:piece, :] = rows
        zsum[piece : piece + SMALL, :] = few

        came(precv.at[pl.ds(0, n - 1)], p_recv.at[0])

        def add_piece(i):
            source = (me + i + 1) % n
            one, two = read_head(precv.at[source])
            zsum[0:piece, :] += one
            zsum[piece : piece + SMALL, :] += two

        loop(n - 1, add_piece)
        write_head(hag.at[me], (zsum[0:piece, :], zsum[piece : piece + SMALL, :]))
        t_other(me).start()
        both_tags(me)

    both_sides(nz - 1, cross)
    sum_head()
    loop(nz - 2, lambda i: both_sides(nz - 2 - i, cross))
    cross(z)
    neighbour_tag = z * 2 + 1 - y

    def tail(d):
        for row in range(2):

            @pl.when(z - d >= 0)
            def _(row=row):
                j = (z - d) * 2 + row
                came(tag(j), t_recv.at[j])
                pl.when(has_right)(lambda: t_right(j).start())

            @pl.when(z + d < nz)
            def _(row=row):
                j = (z + d) * 2 + row
                came(tag(j), t_recv.at[j])
                pl.when(has_left)(lambda: t_left(j).start())

    def out_step(i):
        d = nz - 1 - i

        def item(c):
            k = (c + first_r) % cargo

            def send(zz):
                line_conv(zz, k)
                write(lsend.at[zz, k], zsum[...])
                pass_on(zz, k)

            both_sides(d, send)

        loop(cargo, item)

        @pl.when(i == 0)
        def _():
            came(tag(neighbour_tag), t_recv.at[neighbour_tag])
            both_tags(neighbour_tag)

        pl.when(i > 0)(lambda: tail(i))

    loop(nz - 1, out_step)

    def b_copy(k):
        return put(bsend2.at[k], brecv2.at[k], b_send.at[k], b_recv.at[k], other)

    def give_b(k):
        line_conv(z, slots_per + k)
        write(bsend2.at[k], zsum[...])
        b_copy(k).start()

    loop(last_r, give_b)

    def own_slot(k):
        line_conv(z, k)
        grad_out[k] = zsum[...]

    tail(nz - 1)
    per = 448 // piece

    def unpack(j):
        one, two = read_head(hag.at[j])

        @pl.when(j < 4 * per)
        def _():
            rows = pl.ds(pl.multiple_of((j % per) * piece, 16), piece)
            head_out[rows, pl.ds(pl.multiple_of((j // per) * 128, 128), 128)] = one

        @pl.when(j < 8)
        def _():
            small[pl.ds(pl.multiple_of(j * SMALL, SMALL), SMALL), :] = two

    loop(n, unpack)
    for m in range(4):
        pair = small[m * 32 : (m + 1) * 32, :]
        small_out[2 * m] = pair
        small_out[2 * m + 1] = pltpu.roll(pair, HC, 1)

    loop(first_r, own_slot)

    came(losses.at[pl.ds(0, n - 1)], l_recv.at[0])
    loss_tile = lax.fori_loop(0, n, lambda i, acc: acc + losses[2 + i], jnp.zeros((8, 128), F32))
    loss_out[0] = jnp.sum(loss_tile[:TASKS, HC : HC + 1])

    def own_last(k):
        line_conv(z, first_r + k)
        came(brecv2.at[k], b_recv.at[k])
        grad_out[first_r + k] = zsum[...] + read(brecv2.at[k])

    loop(last_r, own_last)

    line = slots_per + last_b

    def left_line(zz):
        @pl.when((z == zz) & has_right)
        def _():
            left_it(wall.at[pl.ds(0, (zz + 1) * line)], w_zr.at[0])
            left_it(hag.at[pl.ds(0, (zz + 1) * 2)], t_zr.at[0])

        @pl.when((z == zz) & has_left)
        def _():
            left_it(wall.at[pl.ds(0, (nz - zz) * line)], w_zl.at[0])
            left_it(hag.at[pl.ds(0, (nz - zz) * 2)], t_zl.at[0])

    for zz in range(nz):
        left_line(zz)
    left_it(wall.at[pl.ds(0, nz * first_a + last_b)], w_y.at[0])
    left_it(hag.at[0], t_y.at[0])
    left_it(ysend, y_send.at[0])
    left_it(lsend.at[pl.ds(0, nz - 1)], z_send.at[0])
    loop(last_r, lambda k: b_copy(k).wait_send())
    left_it(xs.at[pl.ds(0, LAYERS)], x_send.at[0])
    left_it(hall.at[:, pl.ds(0, 3)], h_send.at[0])
    left_it(ghall.at[pl.ds(0, 3)], q_send.at[0])
    left_it(cnt.at[pl.ds(0, n - 1)], c_send.at[0])
    left_it(losses.at[pl.ds(0, n - 1)], l_send.at[0])
    left_it(psend.at[pl.ds(0, n - 1)], p_send.at[0])
    for k in range(3):
        j_copy(ch, partner, k).wait_send()
        a_copy(ch, partner, k).wait_send()
    for k, peer in enumerate(peers):
        f_copy(peer, k).wait_send()
        g_copy(peer, k).wait_send()
        s_copy(peer, k).wait_send()
    left_it(bcore, bc_send.at[0])
    left_it(bxs, bx_send.at[0])


def adamw(weight, gradient, moment_one, moment_two, step_rate, one_over, two_over):
    moment_one = beta_one * moment_one + (1.0 - beta_one) * gradient
    moment_two = beta_two * moment_two + (1.0 - beta_two) * gradient * gradient
    first_hat = moment_one * one_over
    second_hat = moment_two * two_over
    weight = weight - step_rate * (
        first_hat / (jnp.sqrt(second_hat) + eps_adam) + decay_rate * weight
    )
    return (weight, moment_one, moment_two)


def update(
    step_ref,
    conv_g,
    conv_w,
    conv_m,
    conv_v,
    head_g,
    head_w,
    head_m,
    head_v,
    small_g,
    join_w,
    join_m,
    join_v,
    scale_w,
    scale_m,
    scale_v,
    conv_out,
    conv_out_m,
    conv_out_v,
    head_out,
    head_out_m,
    head_out_v,
    join_out,
    join_out_m,
    join_out_v,
    scale_out,
    scale_out_m,
    scale_out_v,
):
    steps = jnp.full((8, 128), step_ref[0].astype(F32))
    one_over = (1.0 / (1.0 - jnp.exp(steps * math.log(beta_one))))[0:1, 0:1]
    two_over = (1.0 / (1.0 - jnp.exp(steps * math.log(beta_two))))[0:1, 0:1]

    def put_all(outs, values):
        for out, value in zip(outs, values):
            out[...] = value

    conv = adamw(conv_w[...], conv_g[...], conv_m[...], conv_v[...], 0.01, one_over, two_over)
    put_all((conv_out, conv_out_m, conv_out_v), conv)
    head = adamw(head_w[...], head_g[...], head_m[...], head_v[...], 0.03, one_over, two_over)
    put_all((head_out, head_out_m, head_out_v), head)

    @pl.when(pl.program_id(0) == 0)
    def _():
        join_g = small_g[:TASKS, :K, :HC]
        join = adamw(join_w[...], join_g, join_m[...], join_v[...], 0.4, one_over[None], two_over[None])
        put_all((join_out, join_out_m, join_out_v), join)
        scale_g = jnp.concatenate([small_g[t, 24:25, :HC] for t in range(TASKS)], axis=0)
        scale = adamw(scale_w[...], scale_g, scale_m[...], scale_v[...], 0.8, one_over, two_over)
        put_all((scale_out, scale_out_m, scale_out_v), scale)


def per_device(
    n,
    inputs,
    affine,
    image_sizes,
    labels,
    label_mask,
    unit_slots,
    conv_master,
    conv_first,
    conv_second,
    head_master,
    head_first,
    head_second,
    join_master,
    join_first,
    join_second,
    scale_master,
    scale_first,
    scale_second,
    step_count,
):
    slots_per = conv_master.shape[0]
    nz = n // 2
    last_r = slots_per // 7
    first_r = slots_per - last_r
    cargo = slots_per + last_r
    piece = -(-1792 // (n * 16)) * 16
    vm, dma = pltpu.VMEM, pltpu.SemaphoreType.DMA
    shape = jax.ShapeDtypeStruct
    scratch = [
        vm((slots_per, 256, 128), F32),
        vm((TASKS, HC, C), F32),
        vm((8, 128), jnp.int32),
        pltpu.SMEM((8, 128), jnp.int32),
        vm((4, 8, 128), jnp.int32),
        vm((128, 128), F32),
        vm((n * slots_per, 256, 128), BF16),
        vm((LAYERS + 1, 4, PX, 128), BF16),
        vm((LAYERS, 2, 256, PX), BF16),
        vm((TASKS, 4, HC, C), BF16),
        vm((TASKS, 4, HC, 128), F32),
        vm((4, 8, 128), F32),
        vm((n, 8, 128), F32),
        vm((n + 2, 8, 128), F32),
        vm((PX, 128), F32),
        vm((LAYERS, PX, 128), F32),
        vm((3, IMG, 128), F32),
        vm((4, 128, 128), BF16),
        vm((TASKS, 256, 128), BF16),
        vm((4, TASKS, HC, 128), BF16),
        vm((128, C), F32),
        vm((4, 128, 128), BF16),
        vm((4, 128, 128), BF16),
        vm((8, 32, 256), F32),
        vm((4, 4, 32, 128), F32),
        vm((4, 4, 32, 128), F32),
        vm((9, 2 * TALL, 128), BF16),
        vm((2, 2, 2, 2, IMG, 128), F32),
        vm((2, 2, 2, IMG, 128), F32),
        vm((2, 2, IMG, 128), BF16),
        vm((2, 2, IMG, 128), BF16),
        vm((54, 256, 128), F32),
        vm((n * piece, 128), F32),
        vm((n * SMALL, 128), F32),
        vm((n, piece + 48, 128), jnp.int16),
        vm((n, piece + 48, 128), jnp.int16),
        vm((nz, first_r, CHUNK, 128), jnp.int16),
        vm((nz, first_r, CHUNK, 128), jnp.int16),
        vm((nz, cargo, CHUNK, 128), jnp.int16),
        vm((nz, cargo, CHUNK, 128), jnp.int16),
        vm((nz, cargo, CHUNK, 128), jnp.int16),
        vm((max(last_r, 1), CHUNK, 128), jnp.int16),
        vm((max(last_r, 1), CHUNK, 128), jnp.int16),
        vm((n, piece + 48, 128), jnp.int16),
        vm((256, 128), F32),
        dma((slots_per + 2,)),
        dma((n * slots_per,)),
        *[dma((1,)) for _ in range(3)],
        dma((1,)), dma((LAYERS + 1, 2, 3)),
        dma((1,)), dma((3,)),
        *[dma((3,)) for _ in range(4)],
        *[dma((1,)) for _ in range(4)],
        dma((3,)), dma((4,)),
        dma((3,)), dma((4,)),
        *[dma((1,)) for _ in range(2)],
        *[dma((1,)) for _ in range(2)],
        dma((3,)), dma((4,)),
        dma((1,)), dma((2, 2, 2)),
        dma((1,)), dma((2, 2)),
        dma((1,)), dma((nz, first_r)),
        dma((1,)), dma((nz + 1, cargo)),
        *[dma((max(last_r, 1),)) for _ in range(2)],
        dma((n,)),
        *[dma((1,)) for _ in range(3)],
    ]
    in_smem, in_vmem = pl.BlockSpec(memory_space=pltpu.SMEM), pl.BlockSpec(memory_space=pltpu.VMEM)
    in_hbm = pl.BlockSpec(memory_space=pltpu.HBM)
    slot_grads, head_total, small_total, loss = pl.pallas_call(
        functools.partial(kernel, n, slots_per),
        out_shape=(
            shape((slots_per, 256, 128), F32),
            shape((448, C), F32),
            shape((8, 32, 128), F32),
            shape((1,), F32),
        ),
        in_specs=[in_smem] * 2 + [in_vmem] * 6 + [in_hbm] * 2,
        out_specs=(in_vmem,) * 3 + (in_smem,),
        scratch_shapes=scratch,
        compiler_params=pltpu.CompilerParams(
            collective_id=0, has_side_effects=True, vmem_limit_bytes=VMEM_MIB * 2**20
        ),
    )(
        unit_slots,
        image_sizes,
        inputs.reshape(PX, 128),
        affine,
        labels.transpose(0, 3, 1, 2),
        label_mask.transpose(0, 3, 1, 2),
        join_master.transpose(0, 2, 1),
        scale_master,
        conv_master,
        head_master,
    )
    conv_rows, head_rows = slots_per * 256, TASKS * HC
    steps = STEPS

    def tile(rows, columns):
        return pl.BlockSpec((rows // steps, columns), lambda i: (i, 0))

    def whole(*sizes):
        return pl.BlockSpec(sizes, lambda i: (0,) * len(sizes))

    conv_tile, head_tile = tile(conv_rows, 128), tile(head_rows, C)
    join_tile, scale_tile = whole(TASKS, K, HC), whole(TASKS, HC)
    flat_conv = [a.reshape(conv_rows, 128) for a in (slot_grads, conv_master, conv_first, conv_second)]
    flat_head = [a.reshape(head_rows, C) for a in (head_total, head_master, head_first, head_second)]
    flat_join = [a.transpose(0, 2, 1) for a in (join_master, join_first, join_second)]
    out = pl.pallas_call(
        update,
        grid=(steps,),
        out_shape=tuple(
            [shape((conv_rows, 128), F32)] * 3
            + [shape((head_rows, C), F32)] * 3
            + [shape((TASKS, K, HC), F32)] * 3
            + [shape((TASKS, HC), F32)] * 3
        ),
        in_specs=[in_smem]
        + [conv_tile] * 4
        + [head_tile] * 4
        + [whole(8, 32, 128)]
        + [join_tile] * 3
        + [scale_tile] * 3,
        out_specs=tuple([conv_tile] * 3 + [head_tile] * 3 + [join_tile] * 3 + [scale_tile] * 3),
    )(step_count, *flat_conv, *flat_head, small_total, *flat_join, scale_master, scale_first, scale_second)
    conv_out = tuple(a.reshape(slots_per, 256, 128) for a in out[0:3])
    head_out = tuple(a.reshape(TASKS, HC, C) for a in out[3:6])
    join_out = tuple(a.transpose(0, 2, 1) for a in out[6:9])
    return (loss,) + conv_out + head_out + join_out + tuple(out[9:12])


def solution(mesh):
    placed = (
        P("dp", None, None, "chan"),
        P(None, None, "chan"),
        P("dp", None),
        P("dp", None, None, None),
        P("dp", None, None, None),
        P(),
        P("dp", None, "chan"),
        P("dp", None, "chan"),
        P("dp", None, "chan"),
        P(None, "chan", None),
        P(None, "chan", None),
        P(None, "chan", None),
        P(None, "chan", None),
        P(None, "chan", None),
        P(None, "chan", None),
        P(None, "chan"),
        P(None, "chan"),
        P(None, "chan"),
        P(),
    )
    return jax.shard_map(
        functools.partial(per_device, mesh.shape["dp"]),
        mesh=mesh,
        in_specs=placed,
        out_specs=(P(),) + placed[6:18],
        check_vma=False,
    )
```

```python
import functools
import math

import jax
import jax.numpy as jnp
from jax import lax
from jax.experimental import pallas as pl
from jax.experimental.pallas import tpu as pltpu
from jax.sharding import PartitionSpec as P

C = 512
K = 21
TASKS = 7
LAYERS = 3
H = 16
W = 16
PX = 512
IMG = 256
TALL = IMG + 2 * W
HC = 64
CHUNK = 272
VMEM_MIB = 60
STEPS = 2
SMALL = 16

beta_one = 0.9
beta_two = 0.999
eps_adam = 1e-08
decay_rate = 0.01
eps_norm = 1e-06

F32 = jnp.float32
BF16 = jnp.bfloat16
MESH = pl.DeviceIdType.MESH
NN = (((1,), (0,)), ((), ()))
NT = (((1,), (1,)), ((), ()))
TN = (((0,), (0,)), ((), ()))


def dot(a, b, dims, precision=None):
    return lax.dot_general(a, b, dims, precision=precision, preferred_element_type=F32)


def encode(values):
    top = jnp.max(jnp.abs(values), axis=0, keepdims=True)
    power = jnp.ceil(jnp.log2(jnp.maximum(top, 1e-30))) - 14.0
    codes = jnp.round(values * jnp.exp2(-power)).astype(jnp.int32).astype(jnp.int16)
    powers = jnp.broadcast_to(power, (16, 128)).astype(jnp.int32).astype(jnp.int16)
    return codes, powers


def decode(codes, powers):
    return codes.astype(F32) * jnp.exp2(powers.astype(F32)[0:1])


def kernel(
    n,
    slots_per,
    slots_hbm,
    sizes_hbm,
    inputs_hbm,
    affine_hbm,
    labels_hbm,
    kept_hbm,
    join_hbm,
    scale_hbm,
    conv_ref,
    head_ref,
    grad_out,
    head_out,
    small_out,
    loss_out,
    slots_ref,
    sizes_ref,
    inputs_ref,
    affine_ref,
    labels_ref,
    kept_ref,
    join_ref,
    scale_ref,
    conv_in,
    head_in_ref,
    inv_row,
    inv_ref,
    code_ref,
    flip,
    wall,
    xs,
    xt,
    hall,
    jall,
    aall,
    cnt,
    losses,
    mask,
    coef,
    zacc,
    fbuf,
    gh,
    ghall,
    gfeat,
    gsend,
    grecv,
    jt,
    jsend,
    jrecv,
    gs,
    bpart,
    bcore,
    bx,
    bxs,
    dw,
    hg,
    small,
    psend,
    precv,
    ysend,
    yrecv,
    lsend,
    lright,
    lleft,
    bsend2,
    brecv2,
    hag,
    zsum,
    in_sem,
    w_recv,
    w_zr,
    w_zl,
    w_y,
    x_send,
    x_recv,
    h_send,
    h_recv,
    j_send,
    j_recv,
    a_send,
    a_recv,
    c_send,
    c_recv,
    l_send,
    l_recv,
    f_send,
    f_recv,
    g_send,
    g_recv,
    q_send,
    q_recv,
    p_send,
    p_recv,
    s_send,
    s_recv,
    bc_send,
    bc_recv,
    bx_send,
    bx_recv,
    y_send,
    y_recv,
    z_send,
    zr_recv,
    b_send,
    b_recv,
    t_recv,
    t_zr,
    t_zl,
    t_y,
):
    nz = n // 2
    last_b = slots_per // 7
    first_a = slots_per - last_b
    last_r = slots_per // 7
    first_r = slots_per - last_r
    cargo = slots_per + last_r
    piece = hg.shape[0] // n

    me = lax.axis_index("dp")
    ch = lax.axis_index("chan")
    z, y = me // 2, me % 2
    core = ch % 2
    partner = ch + 1 - 2 * core
    across = (ch + 2) % 4
    far = (partner + 2) % 4

    def at(dp=None, chan=None):
        return {"dp": me if dp is None else dp, "chan": ch if chan is None else chan}

    right, left, other = at(dp=me + 2), at(dp=me - 2), at(dp=z * 2 + 1 - y)
    has_right, has_left = z < nz - 1, z > 0

    def put(src, dst, send, recv, dev):
        return pltpu.make_async_remote_copy(
            src_ref=src, dst_ref=dst, send_sem=send, recv_sem=recv, device_id=dev, device_id_type=MESH
        )

    def came(ref, recv):
        put(ref, ref, recv, recv, other).wait_recv()

    def left_it(ref, send):
        put(ref, ref, send, send, other).wait_send()

    def loop(count, body):
        lax.fori_loop(0, count, lambda i, c: (body(i), c)[1], 0)

    def conv_copy(k):
        return pltpu.make_async_copy(conv_ref.at[k], conv_in.at[k], in_sem.at[k])

    head_copy = pltpu.make_async_copy(head_ref, head_in_ref, in_sem.at[slots_per])
    inv_copy = pltpu.make_async_copy(inv_row, inv_ref, in_sem.at[slots_per + 1])
    loop(slots_per, lambda k: conv_copy(k).start())
    fetched = (
        (sizes_hbm, sizes_ref),
        (inputs_hbm, inputs_ref),
        (slots_hbm, slots_ref),
        (affine_hbm, affine_ref),
        (labels_hbm, labels_ref),
        (kept_hbm, kept_ref),
        (join_hbm, join_ref),
        (scale_hbm, scale_ref),
    )
    fetches = [
        pltpu.make_async_copy(src, dst, in_sem.at[slots_per + 2 + i]) for i, (src, dst) in enumerate(fetched)
    ]
    for fetch in fetches:
        fetch.start()
    head_copy.start()
    barrier = pltpu.get_barrier_semaphore()

    for peer in (partner, across, far):
        pl.semaphore_signal(barrier, inc=1, device_id=at(chan=peer), device_id_type=MESH)
    pl.semaphore_signal(barrier, inc=1, device_id=other, device_id_type=MESH)

    @pl.when(has_right)
    def _():
        pl.semaphore_signal(barrier, inc=1, device_id=right, device_id_type=MESH)

    @pl.when(has_left)
    def _():
        pl.semaphore_signal(barrier, inc=1, device_id=left, device_id_type=MESH)

    def cast_block(k):
        conv_copy(k).wait()
        wall[me * slots_per + k] = conv_in[k].astype(BF16)

    loop(slots_per, cast_block)
    pl.semaphore_wait(barrier, 4 + jnp.where(has_right, 1, 0) + jnp.where(has_left, 1, 0))

    def to_right(s):
        return put(wall.at[s], wall.at[s], w_zr.at[0], w_recv.at[s], right)

    def to_left(s):
        return put(wall.at[s], wall.at[s], w_zl.at[0], w_recv.at[s], left)

    def to_other(s):
        return put(wall.at[s], wall.at[s], w_y.at[0], w_recv.at[s], other)

    def both_ways(s):
        @pl.when(has_right)
        def _():
            to_right(s).start()

        @pl.when(has_left)
        def _():
            to_left(s).start()

    def x_copy(l, i, owner, peer, k):
        rows = pl.ds(pl.multiple_of(i * IMG, IMG), IMG)
        ref = xs.at[l, owner, rows, :]
        return put(ref, ref, x_send.at[0], x_recv.at[l, i, k], at(chan=peer))

    def x_start(l, i):
        x_copy(l, i, ch, across, 0).start()
        x_copy(l, i, ch, partner, 1).start()

    def x_relay(l, i):
        x_copy(l, i, across, across, 0).wait_recv()
        x_copy(l, i, across, partner, 2).start()

    def x_arrive(l, i):
        x_copy(l, i, partner, partner, 1).wait_recv()
        x_copy(l, i, far, partner, 2).wait_recv()

    def h_copy(t, owner, peer, k):
        ref = hall.at[t, owner]
        return put(ref, ref, h_send.at[0], h_recv.at[k], at(chan=peer))

    def j_copy(owner, peer, k):
        ref = jall.at[:, owner]
        return put(ref, ref, j_send.at[k], j_recv.at[k], at(chan=peer))

    def a_copy(owner, peer, k):
        ref = aall.at[owner]
        return put(ref, ref, a_send.at[k], a_recv.at[k], at(chan=peer))

    def c_copy(i):
        dev = (me + i + 1) % n
        return put(cnt.at[me], cnt.at[me], c_send.at[0], c_recv.at[0], at(dp=dev))

    base = me * slots_per

    def own_b(k):
        to_other(base + first_a + k).start()

    loop(last_b, own_b)

    def own_a(k):
        both_ways(base + k)
        to_other(base + k).start()

    loop(first_a, own_a)
    loop(last_b, lambda k: both_ways(base + first_a + k))
    for fetch in fetches:
        fetch.wait()
    pixel = lax.broadcasted_iota(jnp.int32, (IMG, 128), 0)
    row_id, col_id = pixel // W, pixel % W

    def mask_image(i):
        inside = (row_id < sizes_ref[i, 0]) & (col_id < sizes_ref[i, 1])
        rows = pl.ds(pl.multiple_of(i * IMG, IMG), IMG)
        mask[rows, :] = jnp.where(inside, 1.0, 0.0)
        xs[0, ch, rows, :] = (inputs_ref[rows, :].astype(F32) * mask[rows, :]).astype(BF16)
        x_start(0, i)

    loop(2, mask_image)
    head_copy.wait()

    def cast_head(t):
        hall[t, ch] = head_in_ref[t].astype(BF16)
        h_copy(t, ch, across, 0).start()
        h_copy(t, ch, partner, 1).start()

    loop(TASKS, cast_head)
    for i in range(2):
        gs[:, i * TALL : i * TALL + W, :] = jnp.zeros((9, W, 128), BF16)
        gs[:, (i + 1) * TALL - W : (i + 1) * TALL, :] = jnp.zeros((9, W, 128), BF16)
    flip[...] = jnp.zeros_like(flip)
    for t in range(TASKS):
        flip[0:K, 0:HC] = join_ref[t]
        flip[32:33, 0:HC] = scale_ref[t : t + 1, :]
        jall[t, ch] = flip[...].T[0:HC]
    aall[ch] = jnp.broadcast_to(affine_ref[LAYERS - 1, 0:1, :], (8, 128))

    code = jnp.where(kept_ref[...] > 0, labels_ref[...], -1).astype(F32).astype(BF16).reshape(2 * TASKS * H, W)
    lane_row = lax.broadcasted_iota(jnp.int32, (W, 128), 1) % W == lax.broadcasted_iota(jnp.int32, (W, 128), 0)
    wide = dot(code, jnp.where(lane_row, 1.0, 0.0).astype(BF16), NN).reshape(4 * TASKS, 8, 128)
    own_row = lax.broadcasted_iota(jnp.int32, (1, 8, 128), 1) == lax.broadcasted_iota(jnp.int32, (1, 8, 128), 2) // W
    rows_of = jnp.sum(jnp.where(own_row, wide, 0.0), axis=1).astype(jnp.int32)
    code_ref[...] = jnp.full(code_ref.shape, -1, jnp.int32)
    for b in range(2):
        for t in range(TASKS):
            for half in range(2):
                place = (b * TASKS + t) * 2 + half
                code_ref[2 * b + half, t : t + 1, :] = rows_of[place : place + 1, :]

    lane = lax.broadcasted_iota(jnp.int32, (8, 128), 1)

    def kept(q):
        spot = (q % 2) * 128 + lane
        hit = (spot // W < sizes_ref[q // 2, 0]) & (spot % W < sizes_ref[q // 2, 1])
        return jnp.where(hit & (code_ref[q] >= 0), 1.0, 0.0)

    total_kept = kept(0) + kept(1) + kept(2) + kept(3)
    cnt[me] = jnp.broadcast_to(jnp.sum(total_kept, axis=1, keepdims=True), (8, 128))

    found = jnp.full((8, 128), -1, jnp.int32)
    for u in range(slots_ref.shape[0]):
        found = jnp.where(lane == slots_ref[u], u, found)
    inv_row[...] = found
    inv_copy.start()

    for copy in (j_copy, a_copy):
        copy(ch, across, 0).start()
        copy(ch, partner, 1).start()

    neighbour = (z * 2 + 1 - y) * slots_per

    def pass_b(k):
        s = neighbour + first_a + k
        came(wall.at[s], w_recv.at[s])
        both_ways(s)

    loop(last_b, pass_b)
    for i in range(2):
        x_relay(0, i)

    def relay_head(t):
        h_copy(t, across, partner, 2).start()

    def line_in(d, c):
        def source(zz):
            row = jnp.where(c < slots_per, y, 1 - y)
            return (zz * 2 + row) * slots_per + jnp.where(c < slots_per, c, c - last_b)

        @pl.when(z - d >= 0)
        def _():
            s = source(z - d)
            came(wall.at[s], w_recv.at[s])

            @pl.when(has_right)
            def _():
                to_right(s).start()

            @pl.when(c < first_a)
            def _():
                to_other(s).start()

        @pl.when(z + d < nz)
        def _():
            s = source(z + d)
            came(wall.at[s], w_recv.at[s])

            @pl.when(has_left)
            def _():
                to_left(s).start()

            @pl.when(c < first_a)
            def _():
                to_other(s).start()

    def first_step(c):
        line_in(1, c)

    loop(slots_per + last_b, first_step)
    came(hall.at[:, 0], h_recv.at[0])
    loop(TASKS, relay_head)
    for copy in (j_copy, a_copy):
        copy(across, across, 0).wait_recv()
        copy(across, partner, 2).start()

    inv_copy.wait()

    def transpose_layer(l):
        for c in range(4):
            xt[l, c // 2, (c % 2) * 128 : (c % 2) * 128 + 128, :] = xs[l, c].T

    for i in range(2):
        x_arrive(0, i)
    transpose_layer(0)

    loop(nz - 2, lambda d: loop(slots_per + last_b, lambda c: line_in(d + 2, c)))

    def last_in(zz):
        def block(k):
            s = (zz * 2 + 1 - y) * slots_per + k
            came(wall.at[s], w_recv.at[s])

        loop(first_a, block)

    loop(nz, last_in)

    loop(n - 1, lambda i: c_copy(i).start())

    def conv_forward(l, i):
        rows = pl.ds(pl.multiple_of(i * IMG, IMG), IMG)
        left_side = jnp.concatenate([xs[l, c, rows, :] for c in range(4)], axis=1)
        zacc[...] = jnp.zeros_like(zacc)
        for first in range(0, 9, 2):
            taps = [t for t in (first, first + 1) if t < 9]
            sides = [
                jnp.concatenate([wall[slots_ref[(l * 9 + t) * 2 + h]] for h in range(2)], axis=0)
                for t in taps
            ]
            side = jnp.concatenate(sides, axis=1) if len(sides) > 1 else sides[0]
            out = dot(left_side, side, NN)
            for k, t in enumerate(taps):
                a, e = divmod(t, 3)
                part = out[:, k * 128 : (k + 1) * 128]
                if a == 0:
                    zacc[e, W:IMG, :] += part[: IMG - W]
                elif a == 1:
                    zacc[e] += part
                else:
                    zacc[e, : IMG - W, :] += part[W:]
        linear = zacc[1]
        linear += jnp.where(col_id >= 1, pltpu.roll(zacc[0], 1, 0), 0.0)
        linear += jnp.where(col_id < W - 1, pltpu.roll(zacc[2], IMG - 1, 0), 0.0)
        inside = mask[rows, :]
        gain, shift = affine_ref[l, 0:1, :], affine_ref[l, 1:2, :]
        passed = jnp.where(linear > 0, inside, 0.0)
        coef[l, rows, :] = passed * gain if l < LAYERS - 1 else passed
        out = (jnp.maximum(linear, 0.0) * gain + shift) * inside
        xs[l + 1, ch, rows, :] = out.astype(BF16)

    def quarter(q):
        return pl.ds(pl.multiple_of(q * 128, 128), 128)

    for l in range(LAYERS):

        def forward_image(i, l=l):
            if l > 0:
                x_relay(l, i)
                x_arrive(l, i)
            conv_forward(l, i)
            if l < LAYERS - 1:
                x_start(l + 1, i)

        loop(2, forward_image)
        if 0 < l:
            transpose_layer(l)

    def f_copy(peer, k):
        return put(xs.at[LAYERS, ch, quarter(peer), :], fbuf.at[ch], f_send.at[k], f_recv.at[ch], at(chan=peer))

    peers = (across, far, partner)
    for k, peer in enumerate(peers):
        f_copy(peer, k).start()
    for i in range(2):
        x_start(LAYERS, i)
    fbuf[ch] = xs[LAYERS, ch, quarter(ch), :]

    came(cnt.at[pl.ds(0, n - 1)], c_recv.at[0])
    counts = lax.fori_loop(0, n, lambda i, acc: acc + cnt[i], jnp.zeros((8, 128), F32))
    counts = jnp.maximum(counts, 1.0)

    came(hall.at[:, 0], h_recv.at[1])
    came(hall.at[:, 0], h_recv.at[2])
    for copy in (j_copy, a_copy):
        copy(partner, partner, 1).wait_recv()
        copy(far, partner, 2).wait_recv()
    for peer in peers:
        came(fbuf.at[peer], f_recv.at[peer])

    weight = kept(ch) / counts
    losses[0] = weight
    losses[1] = jnp.zeros((8, 128), F32)
    features = jnp.concatenate([fbuf[c] for c in range(4)], axis=1)
    gfeat[...] = jnp.zeros_like(gfeat)
    klass = lax.broadcasted_iota(jnp.int32, (32, 128), 0)

    def q_copy(t, peer, k):
        rows = pl.ds(pl.multiple_of(peer * HC, HC), HC)
        return put(gh.at[t, rows, :], ghall.at[ch, t], q_send.at[0], q_recv.at[0], at(chan=peer))

    def head_task(t):
        low = hall[t].reshape(4 * HC, C)
        both = jall[t].reshape(4 * HC, 128)
        join = both.astype(BF16)
        scale = both[:, 32:33]
        hidden = dot(low, features, NT)
        inverse = lax.rsqrt(jnp.sum(hidden * hidden, axis=0, keepdims=True) + eps_norm)
        normed = hidden * inverse
        scaled = (scale * normed).astype(BF16)
        logits = dot(join, scaled, TN)[0:32]
        real = klass < K
        largest = jnp.max(jnp.where(real, logits, -jnp.inf), axis=0, keepdims=True)
        shifted = jnp.where(real, jnp.exp(jnp.where(real, logits - largest, 0.0)), 0.0)
        totals = jnp.sum(shifted, axis=0, keepdims=True)
        onehot = klass == code_ref[ch, pl.ds(t, 1), :]
        picked = jnp.sum(jnp.where(onehot, logits, 0.0), axis=0, keepdims=True)
        share = losses[0, pl.ds(t, 1), :]
        losses[1, pl.ds(t, 1), :] = share * (largest + jnp.log(totals) - picked)
        slope = (share * (shifted / totals - jnp.where(onehot, 1.0, 0.0))).astype(BF16)
        grad_scaled = dot(join, jnp.concatenate([slope, jnp.zeros((96, 128), BF16)], axis=0), NN)
        jt[t, 0:24, :] = dot(slope, scaled, NT)[0:24]
        jt[t, 24:32, :] = dot(jnp.ones((8, 128), F32), grad_scaled * normed, NT, lax.Precision.HIGHEST)
        grad_normed = grad_scaled * scale
        along = jnp.sum(normed * grad_normed, axis=0, keepdims=True)
        grad_hidden = ((grad_normed - normed * along) * inverse).astype(BF16)
        gh[t] = grad_hidden
        for k, peer in enumerate(peers):
            q_copy(t, peer, k).start()
        gfeat[...] += dot(grad_hidden, low, TN)

    for t in range(TASKS):
        head_task(t)
    loss_tile = jnp.broadcast_to(jnp.sum(losses[1], axis=1, keepdims=True), (8, 128))
    jt[TASKS, 0:8, 0:128] = loss_tile
    jt[TASKS, 0:8, 128:256] = loss_tile

    my_mask = mask[quarter(ch), :]
    for c in range(4):
        gsend[c] = (gfeat[:, c * 128 : (c + 1) * 128] * my_mask * aall[c, 0:1, :]).astype(BF16)

    def g_copy(peer, k):
        return put(gsend.at[peer], grecv.at[ch], g_send.at[k], g_recv.at[ch], at(chan=peer))

    def s_copy(peer, k):
        return put(jsend.at[peer], jrecv.at[ch], s_send.at[k], s_recv.at[ch], at(chan=peer))

    for k, peer in enumerate(peers):
        g_copy(peer, k).start()
    for i in range(2):
        x_relay(LAYERS, i)
    grecv[ch] = gsend[ch]
    low_lane = lax.broadcasted_iota(jnp.int32, (32, 128), 1) < HC
    for c in range(4):
        side = slice((c // 2) * 128, (c // 2) * 128 + 128)
        for m in range(4):
            one, two = jt[2 * m, :, side], jt[2 * m + 1, :, side]
            if m == 3:
                two = jnp.where(lax.broadcasted_iota(jnp.int32, (32, 128), 0) < 8, two, 0.0)
            if c % 2 == 0:
                two = pltpu.roll(two, HC, 1)
            else:
                one = pltpu.roll(one, HC, 1)
            jsend[c, m] = jnp.where(low_lane, one, two)
    for k, peer in enumerate(peers):
        s_copy(peer, k).start()
    ghall[ch] = gh[:, pl.ds(pl.multiple_of(ch * HC, HC), HC), :]
    jrecv[ch] = jsend[ch]

    def spread(l, i, grad):
        columns = (
            jnp.where(col_id < W - 1, pltpu.roll(grad, IMG - 1, 0), 0.0),
            grad,
            jnp.where(col_id >= 1, pltpu.roll(grad, 1, 0), 0.0),
        )
        top = pl.multiple_of(i * TALL + W, W)
        for e in range(3):
            gs[l * 3 + e, pl.ds(top, IMG), :] = columns[e].astype(BF16)

    def shifted(l, t, i):
        a, e = divmod(t, 3) if isinstance(t, int) else (t // 3, t % 3)
        return gs[l * 3 + e, pl.ds(pl.multiple_of(i * TALL + (2 - a) * W, W), IMG), :]

    def tap_grad(l, t):
        return jnp.concatenate([shifted(l, t, 0), shifted(l, t, 1)], axis=0)

    def conv_backward(l, i, h):
        total = None
        for first in range(0, 9, 2):
            taps = [t for t in (first, first + 1) if t < 9]
            grads = [shifted(l, t, i) for t in taps]
            sides = [wall[slots_ref[(l * 9 + t) * 2 + h]] for t in taps]
            if len(taps) > 1:
                term = dot(jnp.concatenate(grads, axis=1), jnp.concatenate(sides, axis=1), NT)
            else:
                term = dot(grads[0], sides[0], NT)
            total = term if total is None else total + term
        bpart[l - 1, i, h, 0] = total[:, :128]
        bpart[l - 1, i, h, 1] = total[:, 128:]

    def bc_copy(l, i, h):
        return put(
            bpart.at[l - 1, i, h, 1 - core],
            bcore.at[l - 1, i, h],
            bc_send.at[0],
            bc_recv.at[l - 1, i, h],
            at(chan=partner),
        )

    def bx_copy(l, i):
        return put(bxs.at[l - 1, i], bx.at[l - 1, i], bx_send.at[0], bx_recv.at[l - 1, i], at(chan=across))

    def weight_grads(l):
        lhs = xt[l].reshape(C, PX)

        def pair(p):
            t = 2 * p
            rhs = jnp.concatenate([tap_grad(l, t), tap_grad(l, t + 1)], axis=1)
            out = dot(lhs, rhs, NN)
            for h in range(2):
                dw[(l * 9 + t) * 2 + h] = out[h * 256 : (h + 1) * 256, :128]
                dw[(l * 9 + t + 1) * 2 + h] = out[h * 256 : (h + 1) * 256, 128:]

        loop(4, pair)
        out = dot(lhs, tap_grad(l, 8), NN)
        for h in range(2):
            dw[(l * 9 + 8) * 2 + h] = out[h * 256 : (h + 1) * 256]

    def l_copy(i):
        dev = (me + i + 1) % n
        return put(losses.at[2 + me], losses.at[2 + me], l_send.at[0], l_recv.at[0], at(dp=dev))

    def head_part(dest):
        rows = hg[pl.ds(pl.multiple_of(dest * piece, 16), piece), :]
        return rows, small[pl.ds(pl.multiple_of(dest * SMALL, SMALL), SMALL), :]

    def write(ref, values):
        codes, powers = encode(values)
        ref[0:256, :] = codes
        ref[256:272, :] = powers

    def read(ref):
        return decode(ref[0:256, :], ref[256:272, :])

    def write_head(ref, values):
        codes, powers = encode(values[0])
        ref[0:piece, :] = codes
        ref[piece : piece + 16, :] = powers
        codes, powers = encode(values[1])
        ref[piece + 16 : piece + 32, :] = codes
        ref[piece + 32 : piece + 48, :] = powers

    def read_head(ref):
        one = decode(ref[0:piece, :], ref[piece : piece + 16, :])
        return one, decode(ref[piece + 16 : piece + 32, :], ref[piece + 32 : piece + 48, :])

    def p_copy(i):
        dest = (me + i + 1) % n
        return put(psend.at[dest], precv.at[me], p_send.at[0], p_recv.at[0], at(dp=dest))

    def head_grads():
        for i in range(2):
            x_arrive(LAYERS, i)
        for peer in peers:
            came(jrecv.at[peer], s_recv.at[peer])
        came(ghall.at[pl.ds(0, 3)], q_recv.at[0])
        lhs = [
            jnp.concatenate([ghall[2 * m].reshape(TASKS * HC, 128), ghall[2 * m + 1].reshape(TASKS * HC, 128)], axis=1)
            for m in range(2)
        ]
        for c in range(0, 4, 2):
            total = None
            for m in range(2):
                rows = slice(m * IMG, (m + 1) * IMG)
                rhs = jnp.concatenate([xs[LAYERS, c, rows, :], xs[LAYERS, c + 1, rows, :]], axis=1)
                term = dot(lhs[m], rhs, NN)
                total = term if total is None else total + term
            hg[c * 448 : (c + 1) * 448, :] = total[:, :128]
            hg[(c + 1) * 448 : (c + 2) * 448, :] = total[:, 128:]
        if hg.shape[0] > 1792:
            hg[1792:, :] = jnp.zeros((hg.shape[0] - 1792, 128), F32)
        small[...] = jnp.zeros_like(small)
        for m in range(4):
            small[m * 32 : (m + 1) * 32, :] = jrecv[0, m] + jrecv[1, m] + jrecv[2, m] + jrecv[3, m]
        losses[2 + me] = small[96:104, :]


        def give(i):
            dest = (me + i + 1) % n
            write_head(psend.at[dest], head_part(dest))
            p_copy(i).start()

        loop(n - 1, give)
        loop(n - 1, lambda i: l_copy(i).start())

    for peer in peers:
        came(grecv.at[peer], g_recv.at[peer])

    def top_grad(i):
        rows = pl.ds(pl.multiple_of(i * IMG, IMG), IMG)
        grad = jnp.concatenate([grecv[2 * i], grecv[2 * i + 1]], axis=0).astype(F32)
        spread(LAYERS - 1, i, grad * coef[LAYERS - 1, rows, :])

    loop(2, top_grad)
    x_side = ch // 2
    for l in (2, 1):

        def partial_image(i, h, l=l):
            conv_backward(l, i, h)
            bc_copy(l, i, h).start()

        def chip_sum(i, l=l):
            bc_copy(l, i, 1 - x_side).wait_recv()
            bxs[l - 1, i] = (bpart[l - 1, i, 1 - x_side, core] + bcore[l - 1, i, 1 - x_side]).astype(BF16)
            bx_copy(l, i).start()

        loop(2, lambda i: partial_image(i, 1 - x_side))
        loop(2, chip_sum)
        loop(2, lambda i: partial_image(i, x_side))
        if l == LAYERS - 1:
            head_grads()
        else:
            weight_grads(LAYERS - 1)
            weight_grads(l)

        def finish_image(i, l=l):
            bx_copy(l, i).wait_recv()
            bc_copy(l, i, x_side).wait_recv()
            grad = bpart[l - 1, i, x_side, core] + bcore[l - 1, i, x_side] + bx[l - 1, i].astype(F32)
            rows = pl.ds(pl.multiple_of(i * IMG, IMG), IMG)
            spread(l - 1, i, grad * coef[l - 1, rows, :])

        loop(2, finish_image)
    weight_grads(0)

    def part(dest, k):
        u = inv_ref[0, dest * slots_per + k]
        return dw[jnp.maximum(u, 0)] * jnp.where(u >= 0, 1.0, 0.0)

    def y_copy(zz, k):
        return put(ysend.at[zz, k], yrecv.at[zz, k], y_send.at[0], y_recv.at[zz, k], other)

    def z_right(zz, k):
        return put(lsend.at[zz, k], lleft.at[zz, k], z_send.at[0], zr_recv.at[zz + 1, k], right)

    def z_left(zz, k):
        return put(lsend.at[zz, k], lright.at[zz, k], z_send.at[0], zr_recv.at[zz, k], left)

    def both_sides(d, body):
        for zz, ok in ((z - d, z - d >= 0), (z + d, z + d < nz)):

            @pl.when(ok)
            def _(zz=zz):
                body(zz)

    def cross(zz):
        dest = zz * 2 + 1 - y

        def block(k):
            write(ysend.at[zz, k], part(dest, k))
            y_copy(zz, k).start()

        loop(first_r, block)

    def pass_on(zz, k):
        @pl.when(zz > z)
        def _():
            z_right(zz, k).start()

        @pl.when(zz < z)
        def _():
            z_left(zz, k).start()

    def line_conv(zz, k):
        is_a, is_own = k < first_r, k < slots_per
        dest = zz * 2 + jnp.where(is_own, y, 1 - y)
        slot = jnp.where(is_own, k, k - last_r)
        zsum[...] = part(dest, slot)

        @pl.when(is_a)
        def _():
            came(yrecv.at[zz, k], y_recv.at[zz, k])
            zsum[...] += read(yrecv.at[zz, k])

        @pl.when((zz >= z) & has_left)
        def _():
            came(lleft.at[zz, k], zr_recv.at[zz + 1, k])
            zsum[...] += read(lleft.at[zz, k])

        @pl.when((zz <= z) & has_right)
        def _():
            came(lright.at[zz, k], zr_recv.at[zz, k])
            zsum[...] += read(lright.at[zz, k])

    def tag(j):
        return hag.at[j]

    def t_right(j):
        return put(tag(j), tag(j), t_zr.at[0], t_recv.at[j], right)

    def t_left(j):
        return put(tag(j), tag(j), t_zl.at[0], t_recv.at[j], left)

    def t_other(j):
        return put(tag(j), tag(j), t_y.at[0], t_recv.at[j], other)

    def both_tags(j):
        @pl.when(has_right)
        def _():
            t_right(j).start()

        @pl.when(has_left)
        def _():
            t_left(j).start()

    def sum_head():
        rows, few = head_part(me)
        zsum[0:piece, :] = rows
        zsum[piece : piece + SMALL, :] = few

        came(precv.at[pl.ds(0, n - 1)], p_recv.at[0])

        def add_piece(i):
            source = (me + i + 1) % n
            one, two = read_head(precv.at[source])
            zsum[0:piece, :] += one
            zsum[piece : piece + SMALL, :] += two

        loop(n - 1, add_piece)
        write_head(hag.at[me], (zsum[0:piece, :], zsum[piece : piece + SMALL, :]))
        t_other(me).start()
        both_tags(me)

    both_sides(nz - 1, cross)
    sum_head()
    loop(nz - 2, lambda i: both_sides(nz - 2 - i, cross))
    cross(z)
    neighbour_tag = z * 2 + 1 - y

    def tail(d):
        for row in range(2):

            @pl.when(z - d >= 0)
            def _(row=row):
                j = (z - d) * 2 + row
                came(tag(j), t_recv.at[j])
                pl.when(has_right)(lambda: t_right(j).start())

            @pl.when(z + d < nz)
            def _(row=row):
                j = (z + d) * 2 + row
                came(tag(j), t_recv.at[j])
                pl.when(has_left)(lambda: t_left(j).start())

    def out_step(i):
        d = nz - 1 - i

        def item(c):
            k = (c + first_r) % cargo

            def send(zz):
                line_conv(zz, k)
                write(lsend.at[zz, k], zsum[...])
                pass_on(zz, k)

            both_sides(d, send)

        loop(cargo, item)

        @pl.when(i == 0)
        def _():
            came(tag(neighbour_tag), t_recv.at[neighbour_tag])
            both_tags(neighbour_tag)

        pl.when(i > 0)(lambda: tail(i))

    loop(nz - 1, out_step)

    def b_copy(k):
        return put(bsend2.at[k], brecv2.at[k], b_send.at[k], b_recv.at[k], other)

    def give_b(k):
        line_conv(z, slots_per + k)
        write(bsend2.at[k], zsum[...])
        b_copy(k).start()

    loop(last_r, give_b)

    def own_slot(k):
        line_conv(z, k)
        grad_out[k] = zsum[...]

    tail(nz - 1)
    per = 448 // piece

    def unpack(j):
        one, two = read_head(hag.at[j])

        @pl.when(j < 4 * per)
        def _():
            rows = pl.ds(pl.multiple_of((j % per) * piece, 16), piece)
            head_out[rows, pl.ds(pl.multiple_of((j // per) * 128, 128), 128)] = one

        @pl.when(j < 8)
        def _():
            small[pl.ds(pl.multiple_of(j * SMALL, SMALL), SMALL), :] = two

    loop(n, unpack)
    for m in range(4):
        pair = small[m * 32 : (m + 1) * 32, :]
        small_out[2 * m] = pair
        small_out[2 * m + 1] = pltpu.roll(pair, HC, 1)

    loop(first_r, own_slot)

    came(losses.at[pl.ds(0, n - 1)], l_recv.at[0])
    loss_tile = lax.fori_loop(0, n, lambda i, acc: acc + losses[2 + i], jnp.zeros((8, 128), F32))
    loss_out[0] = jnp.sum(loss_tile[:TASKS, HC : HC + 1])

    def own_last(k):
        line_conv(z, first_r + k)
        came(brecv2.at[k], b_recv.at[k])
        grad_out[first_r + k] = zsum[...] + read(brecv2.at[k])

    loop(last_r, own_last)

    line = slots_per + last_b

    def left_line(zz):
        @pl.when((z == zz) & has_right)
        def _():
            left_it(wall.at[pl.ds(0, (zz + 1) * line)], w_zr.at[0])
            left_it(hag.at[pl.ds(0, (zz + 1) * 2)], t_zr.at[0])

        @pl.when((z == zz) & has_left)
        def _():
            left_it(wall.at[pl.ds(0, (nz - zz) * line)], w_zl.at[0])
            left_it(hag.at[pl.ds(0, (nz - zz) * 2)], t_zl.at[0])

    for zz in range(nz):
        left_line(zz)
    left_it(wall.at[pl.ds(0, nz * first_a + last_b)], w_y.at[0])
    left_it(hag.at[0], t_y.at[0])
    left_it(ysend, y_send.at[0])
    left_it(lsend.at[pl.ds(0, nz - 1)], z_send.at[0])
    loop(last_r, lambda k: b_copy(k).wait_send())
    left_it(xs.at[pl.ds(0, LAYERS)], x_send.at[0])
    left_it(hall.at[:, pl.ds(0, 3)], h_send.at[0])
    left_it(ghall.at[pl.ds(0, 3)], q_send.at[0])
    left_it(cnt.at[pl.ds(0, n - 1)], c_send.at[0])
    left_it(losses.at[pl.ds(0, n - 1)], l_send.at[0])
    left_it(psend.at[pl.ds(0, n - 1)], p_send.at[0])
    for k in range(3):
        j_copy(ch, partner, k).wait_send()
        a_copy(ch, partner, k).wait_send()
    for k, peer in enumerate(peers):
        f_copy(peer, k).wait_send()
        g_copy(peer, k).wait_send()
        s_copy(peer, k).wait_send()
    left_it(bcore, bc_send.at[0])
    left_it(bxs, bx_send.at[0])


def adamw(weight, gradient, moment_one, moment_two, step_rate, one_over, two_over):
    moment_one = beta_one * moment_one + (1.0 - beta_one) * gradient
    moment_two = beta_two * moment_two + (1.0 - beta_two) * gradient * gradient
    first_hat = moment_one * one_over
    second_hat = moment_two * two_over
    weight = weight - step_rate * (
        first_hat / (jnp.sqrt(second_hat) + eps_adam) + decay_rate * weight
    )
    return (weight, moment_one, moment_two)


def update(
    step_ref,
    conv_g,
    conv_w,
    conv_m,
    conv_v,
    head_g,
    head_w,
    head_m,
    head_v,
    small_g,
    join_w,
    join_m,
    join_v,
    scale_w,
    scale_m,
    scale_v,
    conv_out,
    conv_out_m,
    conv_out_v,
    head_out,
    head_out_m,
    head_out_v,
    join_out,
    join_out_m,
    join_out_v,
    scale_out,
    scale_out_m,
    scale_out_v,
):
    steps = jnp.full((8, 128), step_ref[0].astype(F32))
    one_over = (1.0 / (1.0 - jnp.exp(steps * math.log(beta_one))))[0:1, 0:1]
    two_over = (1.0 / (1.0 - jnp.exp(steps * math.log(beta_two))))[0:1, 0:1]

    def put_all(outs, values):
        for out, value in zip(outs, values):
            out[...] = value

    conv = adamw(conv_w[...], conv_g[...], conv_m[...], conv_v[...], 0.01, one_over, two_over)
    put_all((conv_out, conv_out_m, conv_out_v), conv)
    head = adamw(head_w[...], head_g[...], head_m[...], head_v[...], 0.03, one_over, two_over)
    put_all((head_out, head_out_m, head_out_v), head)

    @pl.when(pl.program_id(0) == 0)
    def _():
        join_g = small_g[:TASKS, :K, :HC]
        join = adamw(join_w[...], join_g, join_m[...], join_v[...], 0.4, one_over[None], two_over[None])
        put_all((join_out, join_out_m, join_out_v), join)
        scale_g = jnp.concatenate([small_g[t, 24:25, :HC] for t in range(TASKS)], axis=0)
        scale = adamw(scale_w[...], scale_g, scale_m[...], scale_v[...], 0.8, one_over, two_over)
        put_all((scale_out, scale_out_m, scale_out_v), scale)


def per_device(
    n,
    inputs,
    affine,
    image_sizes,
    labels,
    label_mask,
    unit_slots,
    conv_master,
    conv_first,
    conv_second,
    head_master,
    head_first,
    head_second,
    join_master,
    join_first,
    join_second,
    scale_master,
    scale_first,
    scale_second,
    step_count,
):
    slots_per = conv_master.shape[0]
    nz = n // 2
    last_r = slots_per // 7
    first_r = slots_per - last_r
    cargo = slots_per + last_r
    piece = -(-1792 // (n * 16)) * 16
    vm, dma = pltpu.VMEM, pltpu.SemaphoreType.DMA
    shape = jax.ShapeDtypeStruct
    scratch = [
        pltpu.SMEM(unit_slots.shape, jnp.int32),
        pltpu.SMEM(image_sizes.shape, jnp.int32),
        vm((PX, 128), BF16),
        vm(affine.shape, F32),
        *[vm((2, TASKS, H, W), jnp.int32) for _ in range(2)],
        vm((TASKS, K, HC), F32),
        vm((TASKS, HC), F32),
        vm((slots_per, 256, 128), F32),
        vm((TASKS, HC, C), F32),
        vm((8, 128), jnp.int32),
        pltpu.SMEM((8, 128), jnp.int32),
        vm((4, 8, 128), jnp.int32),
        vm((128, 128), F32),
        vm((n * slots_per, 256, 128), BF16),
        vm((LAYERS + 1, 4, PX, 128), BF16),
        vm((LAYERS, 2, 256, PX), BF16),
        vm((TASKS, 4, HC, C), BF16),
        vm((TASKS, 4, HC, 128), F32),
        vm((4, 8, 128), F32),
        vm((n, 8, 128), F32),
        vm((n + 2, 8, 128), F32),
        vm((PX, 128), F32),
        vm((LAYERS, PX, 128), F32),
        vm((3, IMG, 128), F32),
        vm((4, 128, 128), BF16),
        vm((TASKS, 256, 128), BF16),
        vm((4, TASKS, HC, 128), BF16),
        vm((128, C), F32),
        vm((4, 128, 128), BF16),
        vm((4, 128, 128), BF16),
        vm((8, 32, 256), F32),
        vm((4, 4, 32, 128), F32),
        vm((4, 4, 32, 128), F32),
        vm((9, 2 * TALL, 128), BF16),
        vm((2, 2, 2, 2, IMG, 128), F32),
        vm((2, 2, 2, IMG, 128), F32),
        vm((2, 2, IMG, 128), BF16),
        vm((2, 2, IMG, 128), BF16),
        vm((54, 256, 128), F32),
        vm((n * piece, 128), F32),
        vm((n * SMALL, 128), F32),
        vm((n, piece + 48, 128), jnp.int16),
        vm((n, piece + 48, 128), jnp.int16),
        vm((nz, first_r, CHUNK, 128), jnp.int16),
        vm((nz, first_r, CHUNK, 128), jnp.int16),
        vm((nz, cargo, CHUNK, 128), jnp.int16),
        vm((nz, cargo, CHUNK, 128), jnp.int16),
        vm((nz, cargo, CHUNK, 128), jnp.int16),
        vm((max(last_r, 1), CHUNK, 128), jnp.int16),
        vm((max(last_r, 1), CHUNK, 128), jnp.int16),
        vm((n, piece + 48, 128), jnp.int16),
        vm((256, 128), F32),
        dma((slots_per + 10,)),
        dma((n * slots_per,)),
        *[dma((1,)) for _ in range(3)],
        dma((1,)), dma((LAYERS + 1, 2, 3)),
        dma((1,)), dma((3,)),
        *[dma((3,)) for _ in range(4)],
        *[dma((1,)) for _ in range(4)],
        dma((3,)), dma((4,)),
        dma((3,)), dma((4,)),
        *[dma((1,)) for _ in range(2)],
        *[dma((1,)) for _ in range(2)],
        dma((3,)), dma((4,)),
        dma((1,)), dma((2, 2, 2)),
        dma((1,)), dma((2, 2)),
        dma((1,)), dma((nz, first_r)),
        dma((1,)), dma((nz + 1, cargo)),
        *[dma((max(last_r, 1),)) for _ in range(2)],
        dma((n,)),
        *[dma((1,)) for _ in range(3)],
    ]
    in_smem, in_vmem = pl.BlockSpec(memory_space=pltpu.SMEM), pl.BlockSpec(memory_space=pltpu.VMEM)
    in_hbm = pl.BlockSpec(memory_space=pltpu.HBM)
    slot_grads, head_total, small_total, loss = pl.pallas_call(
        functools.partial(kernel, n, slots_per),
        out_shape=(
            shape((slots_per, 256, 128), F32),
            shape((448, C), F32),
            shape((8, 32, 128), F32),
            shape((1,), F32),
        ),
        in_specs=[in_hbm] * 10,
        out_specs=(in_vmem,) * 3 + (in_smem,),
        scratch_shapes=scratch,
        compiler_params=pltpu.CompilerParams(
            collective_id=0, has_side_effects=True, vmem_limit_bytes=VMEM_MIB * 2**20
        ),
    )(
        unit_slots,
        image_sizes,
        inputs.reshape(PX, 128),
        affine,
        labels.transpose(0, 3, 1, 2),
        label_mask.transpose(0, 3, 1, 2),
        join_master.transpose(0, 2, 1),
        scale_master,
        conv_master,
        head_master,
    )
    conv_rows, head_rows = slots_per * 256, TASKS * HC
    steps = STEPS

    def tile(rows, columns):
        return pl.BlockSpec((rows // steps, columns), lambda i: (i, 0))

    def whole(*sizes):
        return pl.BlockSpec(sizes, lambda i: (0,) * len(sizes))

    conv_tile, head_tile = tile(conv_rows, 128), tile(head_rows, C)
    join_tile, scale_tile = whole(TASKS, K, HC), whole(TASKS, HC)
    flat_conv = [a.reshape(conv_rows, 128) for a in (slot_grads, conv_master, conv_first, conv_second)]
    flat_head = [a.reshape(head_rows, C) for a in (head_total, head_master, head_first, head_second)]
    flat_join = [a.transpose(0, 2, 1) for a in (join_master, join_first, join_second)]
    out = pl.pallas_call(
        update,
        grid=(steps,),
        out_shape=tuple(
            [shape((conv_rows, 128), F32)] * 3
            + [shape((head_rows, C), F32)] * 3
            + [shape((TASKS, K, HC), F32)] * 3
            + [shape((TASKS, HC), F32)] * 3
        ),
        in_specs=[in_smem]
        + [conv_tile] * 4
        + [head_tile] * 4
        + [whole(8, 32, 128)]
        + [join_tile] * 3
        + [scale_tile] * 3,
        out_specs=tuple([conv_tile] * 3 + [head_tile] * 3 + [join_tile] * 3 + [scale_tile] * 3),
    )(step_count, *flat_conv, *flat_head, small_total, *flat_join, scale_master, scale_first, scale_second)
    conv_out = tuple(a.reshape(slots_per, 256, 128) for a in out[0:3])
    head_out = tuple(a.reshape(TASKS, HC, C) for a in out[3:6])
    join_out = tuple(a.transpose(0, 2, 1) for a in out[6:9])
    return (loss,) + conv_out + head_out + join_out + tuple(out[9:12])


def solution(mesh):
    placed = (
        P("dp", None, None, "chan"),
        P(None, None, "chan"),
        P("dp", None),
        P("dp", None, None, None),
        P("dp", None, None, None),
        P(),
        P("dp", None, "chan"),
        P("dp", None, "chan"),
        P("dp", None, "chan"),
        P(None, "chan", None),
        P(None, "chan", None),
        P(None, "chan", None),
        P(None, "chan", None),
        P(None, "chan", None),
        P(None, "chan", None),
        P(None, "chan"),
        P(None, "chan"),
        P(None, "chan"),
        P(),
    )
    return jax.shard_map(
        functools.partial(per_device, mesh.shape["dp"]),
        mesh=mesh,
        in_specs=placed,
        out_specs=(P(),) + placed[6:18],
        check_vma=False,
    )
```
